32 devices in a mesh: dp: 16 (over z, x, core), blk: 2 (over y).
Axes of the slice: x: 2, y: 2, z: 4, core: 2. Of those that a mesh axis runs over, the one named last changes fastest.
Arguments:
- tokens: bfloat16 [32, 512, 768], P('dp', 'blk'), may hold values from -6 to 6
- lengths: int32 [32], P('dp'), may hold values from 64 to 512, as said below
- query_weight: bfloat16 [768, 768], replicated, may hold values from -0.3125 to 0.3125
- query_bias: bfloat16 [768], replicated, may hold values from -3 to 3
- key_weight: bfloat16 [768, 768], replicated, may hold values from -0.3125 to 0.3125
- value_weight: bfloat16 [768, 768], replicated, may hold values from -0.21875 to 0.21875
- value_bias: bfloat16 [768], replicated, may hold values from -3 to 3
- out_weight: bfloat16 [768, 768], replicated, may hold values from -1.25 to 1.25
- out_bias: bfloat16 [768], replicated, may hold values from -3 to 3
- norm_gain: float32 [768], replicated, may hold values from 0.5 to 1.5
- norm_shift: float32 [768], replicated, may hold values from -3 to 3
- inner_weight: bfloat16 [768, 3072], replicated, may hold values from -0.21875 to 0.21875
- inner_bias: bfloat16 [3072], replicated, may hold values from -3 to 3
- outer_weight: bfloat16 [3072, 768], replicated, may hold values from -0.109375 to 0.109375
- outer_bias: bfloat16 [768], replicated, may hold values from -3 to 3
- final_gain: float32 [768], replicated, may hold values from 0.5 to 1.5
- final_shift: float32 [768], replicated, may hold values from -3 to 3
- cotangent: bfloat16 [32, 512, 768], P('dp', 'blk'), may hold values from -6 to 6
Outputs:
- layer_out: bfloat16 [32, 512, 768], P('dp', 'blk')
- input_grad: float32 [32, 512, 768], P('dp', 'blk')
- query_weight_grad: float32 [768, 768], P('dp')
- query_bias_grad: float32 [768], P('dp')
- key_weight_grad: float32 [768, 768], P('dp')
- value_weight_grad: float32 [768, 768], P('dp')
- value_bias_grad: float32 [768], P('dp')
- out_weight_grad: float32 [768, 768], P('dp')
- out_bias_grad: float32 [768], P('dp')
- norm_gain_grad: float32 [768], P('dp')
- norm_shift_grad: float32 [768], P('dp')
- inner_weight_grad: float32 [768, 3072], P('dp')
- inner_bias_grad: float32 [3072], P('dp')
- outer_weight_grad: float32 [3072, 768], P('dp')
- outer_bias_grad: float32 [768], P('dp')
- final_gain_grad: float32 [768], P('dp')
- final_shift_grad: float32 [768], P('dp')
The draws below stay inside these ranges and needn't reach their ends.
Inputs may be any that keep to these rules, and one draw needn't show every extreme that they name: `lengths`: some sequence has all 512 positions valid and some has only 64.
All inputs are finite; a program needn't handle non-finite values.
Results may differ from the reference program's by a relative error of at most 0.017.
Values may be sent and summed in bfloat16 or wider, within the bound.
A program may use at most 128 MiB of HBM per device.

```python
import math
import jax
import jax.numpy as jnp
from jax import lax

D = 768
HEADS = 12
HEAD_DIM = 64
FF = 3072
SEQ_LEN = 512
NSEQ = 32


def draw_lengths(key, part):
    key_full, key_short = jax.random.split(key)
    full_flag = jax.random.randint(key_full, (NSEQ,), 0, 2)
    short_len = jax.random.randint(key_short, (NSEQ,), SEQ_LEN // 8, SEQ_LEN + 1)
    counts = jnp.where(full_flag == 0, SEQ_LEN, short_len).astype(jnp.int32)
    return counts.at[0].set(SEQ_LEN).at[NSEQ - 1].set(SEQ_LEN // 8)


def spiked(entries, stream_key, source, target, blocks, factor):
    owner, partner = [(jnp.arange(entries.shape[dim]) // (entries.shape[dim] // blocks)).reshape([-1 if axis == dim else 1 for axis in range(entries.ndim)]) for dim in (source, target)]
    chosen = jax.random.permutation(stream_key, blocks)[partner]
    strong = (owner == chosen) | (owner == (partner + blocks // 2) % blocks)
    return jnp.where(strong, factor * entries, entries)


def levels(stream_key, dims, shards, smallest, top_value):
    gain, own = 1.0, jax.random.fold_in(stream_key, 6)
    for position, blocks in shards:
        draws = jnp.exp(jax.random.uniform(jax.random.fold_in(own, position), (blocks,), jnp.float32, smallest / len(shards), top_value / len(shards)))
        gain = gain * jnp.repeat(draws, dims[position] // blocks).reshape([-1 if axis == position else 1 for axis in range(len(dims))])
    return gain


def noise(key, extent, scale, most, cuts=(), kind=jnp.bfloat16):
    values = jax.random.normal(key, extent, jnp.float32) * scale
    if len(cuts) > 0:
        values = levels(key, extent, cuts, -0.22, 0.18) * values
    return jnp.clip(values, min=-most, max=most).astype(kind)


def noise_with(key, dims, deviation, reach, pieces, heavy, kind=jnp.bfloat16):
    values = deviation * jax.random.normal(key, dims, jnp.float32)
    if pieces:
        values = values * levels(key, dims, pieces, -0.22, 0.18)
    return jnp.clip(spiked(values, jax.random.fold_in(key, 3), *heavy), -reach, reach).astype(kind)


def setup_inputs(seed: int = 0) -> dict:
    keys = jax.random.split(jax.random.key(seed), 19)
    tokens = noise(keys[0], (NSEQ, SEQ_LEN, D), 1.0, 6.0, ((0, 16), (1, 2)))
    lengths = draw_lengths(jax.random.fold_in(keys[18], 71), 0)
    query_weight = noise(keys[2], (D, D), (D // 2) ** -0.5, 0.3125)
    query_bias = noise(keys[3], (D,), 0.5, 3.0)
    key_weight = noise(keys[4], (D, D), (D // 2) ** -0.5, 0.3125)
    value_weight = noise(keys[5], (D, D), D ** -0.5, 0.21875)
    value_bias = noise(keys[6], (D,), 0.5, 3.0)
    out_weight = noise(keys[7], (D, D), (D // 32) ** -0.5, 1.25)
    out_bias = noise(keys[8], (D,), 0.5, 3.0)
    norm_gain = jnp.clip(1.0 + 0.1 * jax.random.normal(keys[9], (D,), jnp.float32), 0.5, 1.5)
    norm_shift = noise(keys[10], (D,), 0.5, 3.0, (), jnp.float32)
    inner_weight = noise(keys[11], (D, FF), D ** -0.5, 0.21875)
    inner_bias = noise(keys[12], (FF,), 0.5, 3.0)
    outer_weight = noise(keys[13], (FF, D), FF ** -0.5, 0.109375)
    outer_bias = noise(keys[14], (D,), 0.5, 3.0)
    final_gain = jnp.clip(1.0 + 0.1 * jax.random.normal(keys[15], (D,), jnp.float32), 0.5, 1.5)
    final_shift = noise(keys[16], (D,), 0.5, 3.0, (), jnp.float32)
    cotangent = noise_with(keys[17], (NSEQ, SEQ_LEN, D), 1.0, 6.0, ((0, 16), (1, 2)), (0, 2, 16, 2.0))
    return {"tokens": tokens, "lengths": lengths, "query_weight": query_weight, "query_bias": query_bias, "key_weight": key_weight, "value_weight": value_weight, "value_bias": value_bias, "out_weight": out_weight, "out_bias": out_bias, "norm_gain": norm_gain, "norm_shift": norm_shift, "inner_weight": inner_weight, "inner_bias": inner_bias, "outer_weight": outer_weight, "outer_bias": outer_bias, "final_gain": final_gain, "final_shift": final_shift, "cotangent": cotangent}


@jax.custom_vjp
def low(v):
    return lax.optimization_barrier(v.astype(jnp.bfloat16)).astype(jnp.float32)

@jax.custom_vjp
def low_back(v):
    return v

def low_keep(v):
    return (low(v), None)

def low_pass(kept, grad):
    return (grad,)

def back_keep(v):
    return (v, None)

def back_low(kept, grad):
    return (low(grad),)
low.defvjp(low_keep, low_pass)
low_back.defvjp(back_keep, back_low)
EPS = 1e-12
HIGH = lax.Precision.HIGHEST

def matmul(left_mat, right_mat):
    return jnp.einsum('nld,de->nle', left_mat, right_mat, precision=HIGH)

def layer_norm(hidden, gain_vec, shift_vec):
    row_mean = lax.optimization_barrier(jnp.mean(hidden, axis=-1, keepdims=True))
    centred = hidden - row_mean
    reciprocal = lax.rsqrt(lax.optimization_barrier(jnp.mean(centred * centred, axis=-1, keepdims=True)) + EPS)
    return centred * reciprocal * gain_vec + shift_vec

def attend(block):
    query_blk, key_blk, value_blk, mask_blk = block
    factor = HEAD_DIM ** (-0.5)
    scores = jnp.einsum('gqhd,gkhd->ghqk', query_blk, key_blk, precision=HIGH) * factor
    scores = low_back(scores)
    scores = jnp.where(mask_blk[:, None, None, :], scores, jnp.float32(-1e+30))
    probs = low(jax.nn.softmax(scores, axis=-1))
    return jnp.einsum('ghqk,gkhd->gqhd', probs, value_blk, precision=HIGH)

def forward(params, inputs, key_mask):
    query_weight, query_bias, key_weight, value_weight, value_bias, out_weight, out_bias, norm_gain, norm_shift, inner_weight, inner_bias, outer_weight, outer_bias, final_gain, final_shift = params
    nseq_all = inputs.shape[0]
    group = math.gcd(nseq_all, 8)
    query_all = low(low_back(matmul(inputs, query_weight) + query_bias))
    key_all = low(low_back(matmul(inputs, key_weight)))
    value_all = low(low_back(matmul(inputs, value_weight) + value_bias))
    shape_grp = (nseq_all // group, group, SEQ_LEN, HEADS, HEAD_DIM)
    blocks = (query_all.reshape(shape_grp), key_all.reshape(shape_grp), value_all.reshape(shape_grp), key_mask.reshape(nseq_all // group, group, SEQ_LEN))
    context = lax.map(jax.checkpoint(attend), blocks).reshape(nseq_all, SEQ_LEN, D)
    context = low(low_back(context))
    branch = low_back(matmul(context, out_weight) + out_bias)
    normed_one = layer_norm(inputs + branch, norm_gain, norm_shift)
    inner_pre = low_back(matmul(low(normed_one), inner_weight) + inner_bias)
    active = low(jax.nn.gelu(inner_pre, approximate=False))
    ffn_out = low_back(matmul(active, outer_weight) + outer_bias)
    return layer_norm(normed_one + ffn_out, final_gain, final_shift)

def reference(tokens, lengths, query_weight, query_bias, key_weight, value_weight, value_bias, out_weight, out_bias, norm_gain, norm_shift, inner_weight, inner_bias, outer_weight, outer_bias, final_gain, final_shift, cotangent):
    params = tuple((w.astype(jnp.float32) for w in (query_weight, query_bias, key_weight, value_weight, value_bias, out_weight, out_bias, norm_gain, norm_shift, inner_weight, inner_bias, outer_weight, outer_bias, final_gain, final_shift)))
    inputs = tokens.astype(jnp.float32)
    key_mask = jnp.arange(SEQ_LEN, dtype=jnp.int32)[None, :] < lengths[:, None]
    result, puller = jax.vjp(lambda prm, inp: forward(prm, inp, key_mask), params, inputs)
    param_grads, input_grad = puller(cotangent.astype(jnp.float32))
    return (result.astype(jnp.bfloat16), input_grad, param_grads[0], param_grads[1], param_grads[2], param_grads[3], param_grads[4], param_grads[5], param_grads[6], param_grads[7], param_grads[8], param_grads[9], param_grads[10], param_grads[11], param_grads[12], param_grads[13], param_grads[14])
```

```python
import functools

import jax
import jax.numpy as jnp
from jax import lax
from jax.experimental import pallas as pl
from jax.experimental.pallas import tpu as pltpu
from jax.sharding import PartitionSpec as P

HEADS = 12
HEAD_DIM = 64
EPS = 1e-12
HALF_ROOT = 0.7071067811865476
INV_ROOT_TAU = 0.3989422804014327
MESH = pl.DeviceIdType.MESH
BF16 = jnp.bfloat16
F32 = jnp.float32

ORDER_A = ("c", "x", "y", "zl", "zh")
ORDER_B = ("c", "y", "x", "zl", "zh")
ORDER_C = ("c", "zl", "x", "y", "zh")
BIT_OF = {"c": 1, "x": 2, "zl": 4, "zh": 8}
SPAN = 16
OFFSETS = (0, 16, 24, 28, 30, 31)
VMEM_LIMIT = 66_000_000


def contract_rows(left_mat, right_mat):
    return lax.dot_general(
        left_mat, right_mat, (((0,), (0,)), ((), ())), preferred_element_type=F32
    )


def times_trans(left_mat, right_mat):
    return lax.dot_general(
        left_mat, right_mat, (((1,), (1,)), ((), ())), preferred_element_type=F32
    )


def mat(left_mat, right_mat):
    return jnp.dot(left_mat, right_mat, preferred_element_type=F32)


def norm_rows(hidden, gain_vec, shift_vec):
    row_mean = jnp.mean(hidden, axis=-1, keepdims=True)
    centred = hidden - row_mean
    reciprocal = lax.rsqrt(jnp.mean(centred * centred, axis=-1, keepdims=True) + EPS)
    normed = centred * reciprocal
    return (normed * gain_vec + shift_vec, normed, reciprocal)


def norm_back(grad_in, normed, reciprocal, gain_vec):
    scaled = grad_in * gain_vec
    return reciprocal * (
        scaled
        - jnp.mean(scaled, axis=-1, keepdims=True)
        - normed * jnp.mean(scaled * normed, axis=-1, keepdims=True)
    )


def gelu_slope(pre_act):
    return (
        0.5 * (1.0 + lax.erf(pre_act * HALF_ROOT))
        + pre_act * jnp.exp(-0.5 * pre_act * pre_act) * INV_ROOT_TAU
    )


def block_index(owner, half, order):
    place = 0
    for dim in order:
        bit = half if dim == "y" else (owner // BIT_OF[dim]) % 2
        place = place * 2 + bit
    return place


def slab_plan(width, ff):
    rows, ff_rows = width // SPAN, ff // SPAN
    orders = (ORDER_A, ORDER_B, ORDER_C)
    plan = []
    for order in orders:
        plan.append((ff_rows, width // 6, order))
    for order in orders:
        plan.append((rows, ff // 6, order))
    for order in (ORDER_C,) + orders:
        plan.append((rows, width // 2, order))
    plan.append((16, 128, ORDER_A))
    return tuple(plan)


def reduce_kernel(plan, low, *refs):
    count = len(plan)
    (x_ref, dq_ref, dk_ref, dv_ref, ctx_ref, dattn_ref, n1_ref, dpre_ref, act_ref, db_ref, vec_ref, ib_ref) = refs[:12]
    res = refs[12 : 12 + count]
    bufs = refs[12 + count : 12 + 2 * count]
    recvs = refs[12 + 2 * count : 12 + 3 * count]
    turned, tmp, send_sem, recv_sem = refs[12 + 3 * count :]

    dp = lax.axis_index("dp")
    y = lax.axis_index("blk")
    top = dp // low
    bits = {dim: (top // b) % 2 for dim, b in BIT_OF.items()}
    bits["y"] = y
    partner = {dim: (dp + (1 - 2 * bits[dim]) * (b * low), y) for dim, b in BIT_OF.items()}
    partner["y"] = (dp, 1 - y)

    barrier = pltpu.get_barrier_semaphore()
    for where in partner.values():
        pl.semaphore_signal(barrier, inc=1, device_id=where, device_id_type=MESH)
    pl.semaphore_wait(barrier, len(partner))

    pending = {}
    stage_of = {}

    def start(s, i):
        order = plan[s][2]
        if i == 5:
            src = recvs[s].at[30]
            dst = recvs[s].at[31]
            where = partner["y"]
        else:
            half = 16 >> i
            dim = order[i]
            src_ref, base = (bufs[s], 0) if i == 0 else (recvs[s], OFFSETS[i - 1])
            src = src_ref.at[pl.ds(base + (1 - bits[dim]) * half, half)]
            dst = recvs[s].at[pl.ds(OFFSETS[i], half)]
            where = partner[dim]
        copy = pltpu.make_async_remote_copy(
            src_ref=src,
            dst_ref=dst,
            send_sem=send_sem.at[s, i],
            recv_sem=recv_sem.at[s, i],
            device_id=where,
            device_id_type=MESH,
        )
        copy.start()
        pending[s, i] = copy
        stage_of[s] = i

    def advance(s):
        i = stage_of[s]
        pending[s, i].wait_recv()
        if i == 5:
            res[s][y] = recvs[s][30]
            res[s][1 - y] = recvs[s][31]
            return
        half = 16 >> i
        dim = plan[s][2][i]
        src_ref, base = (bufs[s], 0) if i == 0 else (recvs[s], OFFSETS[i - 1])
        mine = base + bits[dim] * half

        def add(j, carry):
            recvs[s][OFFSETS[i] + j] = recvs[s][OFFSETS[i] + j] + src_ref[mine + j]
            return carry

        lax.fori_loop(0, half, add, 0)
        start(s, i + 1)

    rows = plan[3][0]
    ff_rows = plan[0][0]
    col = plan[0][1]

    def outer_rows(t, carry):
        span = pl.multiple_of(t * (2 * ff_rows), 128)
        part = contract_rows(act_ref[:, pl.ds(span, 2 * ff_rows)], db_ref[...]).astype(BF16)
        for e in range(2):
            owner = 2 * t + e
            for s in range(3):
                for h in range(2):
                    at = (2 * s + h) * col
                    bufs[s][block_index(owner, h, plan[s][2])] = part[e * ff_rows : (e + 1) * ff_rows, at : at + col]
        return carry

    lax.fori_loop(0, SPAN // 2, outer_rows, 0)
    for s in range(3):
        start(s, 0)

    def by_owner(s, h, left, right):
        for part in range(2):
            block = mat(left[part * 8 * rows : (part + 1) * 8 * rows, :], right()).astype(BF16)
            for o in range(8):
                bufs[s][block_index(part * 8 + o, h, plan[s][2])] = block[o * rows : (o + 1) * rows]

    turned[...] = n1_ref[...].T
    for s in range(3, 6):
        wide = plan[s][1]
        for h in range(2):
            at = ((s - 3) * 2 + h) * wide
            by_owner(s, h, turned, lambda: dpre_ref[:, at : at + wide])
        start(s, 0)
        advance(s - 3)

    turned[...] = ctx_ref[...].T
    for h in range(2):
        wide = plan[6][1]
        by_owner(6, h, turned, lambda: dattn_ref[:, h * wide : (h + 1) * wide])
    start(6, 0)
    for s in range(3, 6):
        advance(s)

    turned[...] = x_ref[...].T
    for s, right_ref in ((7, dq_ref), (8, dk_ref), (9, dv_ref)):
        wide = plan[s][1]
        for h in range(2):
            by_owner(s, h, turned, lambda: right_ref[:, h * wide : (h + 1) * wide])
        start(s, 0)
        advance(s - 1)

    for o in range(SPAN):
        tmp[...] = jnp.zeros_like(tmp)
        tmp[0:8, 0:rows] = vec_ref[:, o * rows : (o + 1) * rows]
        tmp[8:9, :] = ib_ref[:, o * ff_rows : o * ff_rows + 128]
        bufs[10][block_index(o, 0, plan[10][2])] = tmp[...].astype(BF16)
        tmp[...] = jnp.zeros_like(tmp)
        tmp[8:9, 0 : ff_rows - 128] = ib_ref[:, o * ff_rows + 128 : (o + 1) * ff_rows]
        bufs[10][block_index(o, 1, plan[10][2])] = tmp[...].astype(BF16)
    start(10, 0)
    advance(9)
    for s in range(3):
        advance(s)
    advance(10)
    done = {s: False for s in range(count)}
    while not all(done.values()):
        for s in sorted(range(count), key=lambda s: (stage_of[s], s)):
            if not done[s]:
                if stage_of[s] == 5:
                    done[s] = True
                advance(s)
    for copy in pending.values():
        copy.wait_send()


def reduce_grads(plan, low, args):
    count = len(plan)
    width = args[0].shape[1]
    tokens = args[0].shape[0]
    return pl.pallas_call(
        functools.partial(reduce_kernel, plan, low),
        out_shape=[jax.ShapeDtypeStruct((2, r, c), BF16) for r, c, _ in plan],
        in_specs=[pl.BlockSpec(memory_space=pltpu.VMEM)] * len(args),
        out_specs=[pl.BlockSpec(memory_space=pltpu.VMEM)] * count,
        scratch_shapes=[pltpu.VMEM((32, r, c), BF16) for r, c, _ in plan] * 2
        + [
            pltpu.VMEM((width, tokens), BF16),
            pltpu.VMEM((16, 128), F32),
            pltpu.SemaphoreType.DMA((count, 6)),
            pltpu.SemaphoreType.DMA((count, 6)),
        ],
        compiler_params=pltpu.CompilerParams(
            collective_id=0, has_side_effects=True, vmem_limit_bytes=VMEM_LIMIT
        ),
        name="reduce_grads",
    )(*args)


def finish_kernel(rows, ff_rows, *refs):
    res = refs[:11]
    (wq, bq, wk, wv, bv, wo, bo, gain, shift, wi, bi, wout, bout, fgain, fshift) = refs[11:]
    col = res[0].shape[2]
    for s in range(3):
        for h in range(2):
            at = (2 * s + h) * col
            wout[:, at : at + col] = res[s][h].astype(F32)
    wide = res[3].shape[2]
    for s in range(3):
        for h in range(2):
            at = (2 * s + h) * wide
            wi[:, at : at + wide] = res[3 + s][h].astype(F32)
    wide = res[6].shape[2]
    for s, ref in ((6, wo), (7, wq), (8, wk), (9, wv)):
        for h in range(2):
            ref[:, h * wide : (h + 1) * wide] = res[s][h].astype(F32)
    vec = res[10][0].astype(F32)
    rest = res[10][1].astype(F32)
    for i, ref in enumerate((bq, bv, bo, gain, shift, bout, fgain, fshift)):
        ref[...] = vec[i, 0:rows]
    bi[0:128] = vec[8, :]
    bi[128:ff_rows] = rest[8, 0 : ff_rows - 128]


def finish(res, width, ff):
    rows, ff_rows = width // SPAN, ff // SPAN
    square, line = (rows, width), (rows,)
    shapes = (
        square, line, square, square, line, square, line, line, line,
        (rows, ff), (ff_rows,), (ff_rows, width), line, line, line,
    )
    return pl.pallas_call(
        functools.partial(finish_kernel, rows, ff_rows),
        out_shape=[jax.ShapeDtypeStruct(s, F32) for s in shapes],
        in_specs=[pl.BlockSpec(memory_space=pltpu.VMEM)] * len(res),
        out_specs=[pl.BlockSpec(memory_space=pltpu.VMEM)] * len(shapes),
        name="finish",
    )(*res)


def per_device(
    dp_size,
    tokens,
    lengths,
    query_weight,
    query_bias,
    key_weight,
    value_weight,
    value_bias,
    out_weight,
    out_bias,
    norm_gain,
    norm_shift,
    inner_weight,
    inner_bias,
    outer_weight,
    outer_bias,
    final_gain,
    final_shift,
    cotangent,
):
    seqs, span, width = tokens.shape
    ff = inner_weight.shape[1]
    total = 2 * span
    y = lax.axis_index("blk")
    swap = [(0, 1), (1, 0)]
    factor = HEAD_DIM ** (-0.5)

    def own_sequence(arr):
        mine = lax.dynamic_index_in_dim(arr, y, 0, keepdims=False)
        other = lax.dynamic_index_in_dim(arr, 1 - y, 0, keepdims=False)
        return jnp.concatenate([mine, lax.ppermute(other, "blk", swap)], axis=0)

    def own_positions(rows):
        mine, other = rows[:span], lax.ppermute(rows[span:], "blk", swap)
        return jnp.where(y == 0, jnp.stack([mine, other]), jnp.stack([other, mine]))

    x = own_sequence(tokens)
    cot = own_sequence(cotangent)
    length = lax.dynamic_index_in_dim(lengths, y, 0, keepdims=False)
    place = jnp.arange(span, dtype=jnp.int32)
    place = jnp.concatenate([place + y * span, place + (1 - y) * span])
    key_mask = (place < length)[None, None, :]

    q = (mat(x, query_weight) + query_bias).astype(BF16)
    k = mat(x, key_weight).astype(BF16)
    v = (mat(x, value_weight) + value_bias).astype(BF16)

    def heads(m):
        return m.reshape(total, HEADS, HEAD_DIM)

    qh, kh, vh = heads(q), heads(k), heads(v)
    raw = jnp.einsum("qhd,khd->hqk", qh, kh, preferred_element_type=F32) * factor
    scores = jnp.where(key_mask, raw, jnp.float32(-1e30))
    row_max = jnp.max(scores, axis=-1, keepdims=True)
    expo = jnp.exp(scores - row_max)
    prob = expo / jnp.sum(expo, axis=-1, keepdims=True)
    prob_low = prob.astype(BF16)
    ctx = jnp.einsum("hqk,khd->qhd", prob_low, vh, preferred_element_type=F32).astype(BF16).reshape(total, width)

    h1 = x.astype(F32) + mat(ctx, out_weight) + out_bias
    n1, hat1, r1 = norm_rows(h1, norm_gain, norm_shift)
    n1_low = n1.astype(BF16)
    pre = mat(n1_low, inner_weight) + inner_bias
    act = jax.nn.gelu(pre, approximate=False).astype(BF16)
    h2 = n1 + mat(act, outer_weight) + outer_bias
    out, hat2, r2 = norm_rows(h2, final_gain, final_shift)
    layer_out = own_positions(out.astype(BF16))

    g = cot.astype(F32)
    final_gain_grad = jnp.sum(g * hat2, axis=0)
    final_shift_grad = jnp.sum(g, axis=0)
    dh2 = norm_back(g, hat2, r2, final_gain)
    dbranch = dh2.astype(BF16)
    outer_bias_grad = jnp.sum(dbranch.astype(F32), axis=0)
    dpre = (times_trans(dbranch, outer_weight) * gelu_slope(pre)).astype(BF16)
    inner_bias_grad = jnp.sum(dpre.astype(F32), axis=0)
    dn1 = dh2 + times_trans(dpre, inner_weight)
    norm_gain_grad = jnp.sum(dn1 * hat1, axis=0)
    norm_shift_grad = jnp.sum(dn1, axis=0)
    dh1 = norm_back(dn1, hat1, r1, norm_gain)
    dattn = dh1.astype(BF16)
    out_bias_grad = jnp.sum(dattn.astype(F32), axis=0)
    dctx = times_trans(dattn, out_weight).astype(BF16)
    dch = heads(dctx)
    dprob = jnp.einsum("qhd,khd->hqk", dch, vh, preferred_element_type=F32)
    dscore = (prob * (dprob - jnp.sum(prob * dprob, axis=-1, keepdims=True))).astype(BF16)
    dq = (jnp.einsum("hqk,khd->qhd", dscore, kh, preferred_element_type=F32) * factor).astype(BF16).reshape(total, width)
    dk = (jnp.einsum("hqk,qhd->khd", dscore, qh, preferred_element_type=F32) * factor).astype(BF16).reshape(total, width)
    dv = jnp.einsum("hqk,qhd->khd", prob_low, dch, preferred_element_type=F32).astype(BF16).reshape(total, width)
    query_bias_grad = jnp.sum(dq.astype(F32), axis=0)
    value_bias_grad = jnp.sum(dv.astype(F32), axis=0)
    dx = dh1 + times_trans(dq, query_weight) + times_trans(dk, key_weight) + times_trans(dv, value_weight)

    plan = slab_plan(width, ff)
    low = dp_size // SPAN
    vecs = jnp.stack(
        [
            query_bias_grad, value_bias_grad, out_bias_grad, norm_gain_grad,
            norm_shift_grad, outer_bias_grad, final_gain_grad, final_shift_grad,
        ]
    )
    res = reduce_grads(
        plan, low, (x, dq, dk, dv, ctx, dattn, n1_low, dpre, act, dbranch, vecs, inner_bias_grad[None])
    )
    grads = finish(res, width, ff)
    if low > 1:
        groups = [[t * low + i for i in range(low)] for t in range(SPAN)]
        grads = [
            lax.psum_scatter(g, "dp", scatter_dimension=0, axis_index_groups=groups, tiled=True)
            for g in grads
        ]
    input_grad = own_positions(dx.astype(BF16)).astype(F32)
    return (layer_out, input_grad, *grads)


def solution(mesh):
    rows3 = P("dp", "blk", None)
    grad2, grad1 = P("dp", None), P("dp")
    return jax.shard_map(
        functools.partial(per_device, mesh.shape["dp"]),
        mesh=mesh,
        in_specs=(rows3, P("dp")) + (P(),) * 15 + (rows3,),
        out_specs=(
            rows3, rows3, grad2, grad1, grad2, grad2, grad1, grad2, grad1,
            grad1, grad1, grad2, grad1, grad2, grad1, grad1, grad1,
        ),
        check_vma=False,
    )
```

```python
import functools

import jax
import jax.numpy as jnp
from jax import lax
from jax.experimental import pallas as pl
from jax.experimental.pallas import tpu as pltpu
from jax.sharding import PartitionSpec as P

HEADS = 12
HEAD_DIM = 64
HEAD_PAIR = 2 * HEAD_DIM
ROW_CHUNK = 64
EPS = 1e-12
HALF_ROOT = 0.7071067811865476
INV_ROOT_TAU = 0.3989422804014327
MESH = pl.DeviceIdType.MESH
BF16 = jnp.bfloat16
F32 = jnp.float32

ORDER_A = ("c", "x", "y", "zl", "zh")
ORDER_B = ("c", "y", "x", "zl", "zh")
ORDER_C = ("c", "zl", "x", "y", "zh")
BIT_OF = {"c": 1, "x": 2, "zl": 4, "zh": 8}
SPAN = 16
OFFSETS = (0, 16, 24, 28, 30, 31)
VMEM_LIMIT = 66_000_000


def contract_rows(left_mat, right_mat):
    return lax.dot_general(
        left_mat, right_mat, (((0,), (0,)), ((), ())), preferred_element_type=F32
    )


def times_trans(left_mat, right_mat):
    return lax.dot_general(
        left_mat, right_mat, (((1,), (1,)), ((), ())), preferred_element_type=F32
    )


def mat(left_mat, right_mat):
    return jnp.dot(left_mat, right_mat, preferred_element_type=F32)


def norm_rows(hidden, gain_vec, shift_vec):
    row_mean = jnp.mean(hidden, axis=-1, keepdims=True)
    centred = hidden - row_mean
    reciprocal = lax.rsqrt(jnp.mean(centred * centred, axis=-1, keepdims=True) + EPS)
    normed = centred * reciprocal
    return (normed * gain_vec + shift_vec, normed, reciprocal)


def norm_back(grad_in, normed, reciprocal, gain_vec):
    scaled = grad_in * gain_vec
    return reciprocal * (
        scaled
        - jnp.mean(scaled, axis=-1, keepdims=True)
        - normed * jnp.mean(scaled * normed, axis=-1, keepdims=True)
    )


def gelu_slope(pre_act):
    return (
        0.5 * (1.0 + lax.erf(pre_act * HALF_ROOT))
        + pre_act * jnp.exp(-0.5 * pre_act * pre_act) * INV_ROOT_TAU
    )


def block_index(owner, half, order):
    place = 0
    for dim in order:
        bit = half if dim == "y" else (owner // BIT_OF[dim]) % 2
        place = place * 2 + bit
    return place


def slab_plan(width, ff):
    rows, ff_rows = width // SPAN, ff // SPAN
    a, c = ORDER_A, ORDER_C
    plan = []
    for order in (a, c, a):
        plan.append((ff_rows, width // 6, order))
    for order in (c, a, c):
        plan.append((rows, ff // 6, order))
    for order in (a, c, a, c):
        plan.append((rows, width // 2, order))
    plan.append((16, 128, a))
    return tuple(plan)


def reduce_kernel(plan, low, *refs):
    count = len(plan)
    n_in = 18
    hbm = refs[:n_in]
    res = refs[n_in : n_in + count]
    dx_out, out_got = refs[n_in + count : n_in + count + 2]
    refs = refs[n_in + count + 2 :]
    bufs, recvs, refs = refs[:count], refs[count : 2 * count], refs[2 * count :]
    held, refs = refs[:n_in], refs[n_in:]
    (turned, tmp, dqt, dkt, dvt, dp0, dp1, ds0, ds1, dx_send, load_sem, prob_sem, send_sem, recv_sem, side_sem) = refs
    (act, db, n1, dpre, ctx, dattn, k, v, dctx, prob, q, x, wq, wk, wv, dh1, vec, out_send) = held
    prob_hbm = hbm[9]
    ib = None

    dp = lax.axis_index("dp")
    y = lax.axis_index("blk")
    top = dp // low
    bits = {dim: (top // b) % 2 for dim, b in BIT_OF.items()}
    bits["y"] = y
    partner = {dim: (dp + (1 - 2 * bits[dim]) * (b * low), y) for dim, b in BIT_OF.items()}
    partner["y"] = (dp, 1 - y)
    total, width = x.shape
    pairs = width // HEAD_PAIR
    span = total // 2

    def fetch(i):
        if i == 17:
            return pltpu.make_async_copy(hbm[i].at[pl.ds(span, span)], held[i], load_sem.at[i])
        return pltpu.make_async_copy(hbm[i], held[i], load_sem.at[i])

    def fetch_prob(p):
        return pltpu.make_async_copy(prob_hbm.at[pl.ds(2 * p, 2)], prob.at[p % 2], prob_sem.at[p])

    for i in (0, 1, 17, 2, 3, 4, 5, 6, 7, 8):
        fetch(i).start()
    fetch_prob(0).start()
    fetch_prob(1).start()
    for i in (10, 11, 16, 12, 13, 14, 15):
        fetch(i).start()
    waited = set()

    def need(*which):
        for i in which:
            if i not in waited:
                waited.add(i)
                fetch(i).wait()

    barrier = pltpu.get_barrier_semaphore()
    for where in partner.values():
        pl.semaphore_signal(barrier, inc=1, device_id=where, device_id_type=MESH)
    pl.semaphore_wait(barrier, len(partner))

    pending = {}
    stage_of = {}

    def remote(src, dst, send, recv, where):
        copy = pltpu.make_async_remote_copy(
            src_ref=src, dst_ref=dst, send_sem=send, recv_sem=recv, device_id=where, device_id_type=MESH
        )
        copy.start()
        return copy

    def start(s, i):
        if i == 5:
            src, dst = recvs[s].at[30], recvs[s].at[31]
            where = partner["y"]
        else:
            half = 16 >> i
            dim = plan[s][2][i]
            src_ref, base = (bufs[s], 0) if i == 0 else (recvs[s], OFFSETS[i - 1])
            src = src_ref.at[pl.ds(base + (1 - bits[dim]) * half, half)]
            dst = recvs[s].at[pl.ds(OFFSETS[i], half)]
            where = partner[dim]
        pending[s, i] = remote(src, dst, send_sem.at[s, i], recv_sem.at[s, i], where)
        stage_of[s] = i

    def advance(s):
        i = stage_of[s]
        pending[s, i].wait_recv()
        if i == 5:
            res[s][y] = recvs[s][30]
            res[s][1 - y] = recvs[s][31]
            stage_of[s] = 6
            return
        half = 16 >> i
        dim = plan[s][2][i]
        src_ref, base = (bufs[s], 0) if i == 0 else (recvs[s], OFFSETS[i - 1])
        mine = base + bits[dim] * half

        def add(j, carry):
            recvs[s][OFFSETS[i] + j] = recvs[s][OFFSETS[i] + j] + src_ref[mine + j]
            return carry

        lax.fori_loop(0, half, add, 0)
        start(s, i + 1)

    rows = plan[3][0]
    ff_rows = plan[0][0]
    col = plan[0][1]

    def outer_rows(t, carry):
        at_row = pl.multiple_of(t * (2 * ff_rows), 128)
        part = contract_rows(act[:, pl.ds(at_row, 2 * ff_rows)], db[...]).astype(BF16)
        for e in range(2):
            owner = 2 * t + e
            for s in range(3):
                for h in range(2):
                    at = (2 * s + h) * col
                    bufs[s][block_index(owner, h, plan[s][2])] = part[e * ff_rows : (e + 1) * ff_rows, at : at + col]
        return carry

    need(0, 1)
    lax.fori_loop(0, SPAN // 2, outer_rows, 0)
    for s in range(3):
        start(s, 0)
    need(17)
    side_out = remote(out_send, out_got, side_sem.at[0], side_sem.at[1], partner["y"])

    def by_owner(s, h, product):
        for part in range(2):
            block = product(turned[part * 8 * rows : (part + 1) * 8 * rows, :]).astype(BF16)
            for o in range(8):
                bufs[s][block_index(part * 8 + o, h, plan[s][2])] = block[o * rows : (o + 1) * rows]

    need(2, 3)
    turned[...] = n1[...].T
    for s in range(3, 6):
        wide = plan[s][1]
        for h in range(2):
            at = ((s - 3) * 2 + h) * wide
            by_owner(s, h, lambda left: mat(left, dpre[:, at : at + wide]))
        start(s, 0)
        advance(s - 3)

    need(4, 5)
    turned[...] = ctx[...].T
    wide = plan[6][1]
    for h in range(2):
        by_owner(6, h, lambda left: mat(left, dattn[:, h * wide : (h + 1) * wide]))
    start(6, 0)
    for s in range(3, 6):
        advance(s)

    need(6, 7, 8, 10)
    lane = lax.broadcasted_iota(jnp.int32, (1, HEAD_PAIR), 1)

    def pair(p, slot):
        at = pl.multiple_of(p * HEAD_PAIR, HEAD_PAIR)
        cols = pl.ds(at, HEAD_PAIR)
        qp, kp, vp, dop = q[:, cols], k[:, cols], v[:, cols], dctx[:, cols]
        first = lane < HEAD_DIM
        dp0[...] = times_trans(jnp.where(first, dop, 0).astype(BF16), vp)
        dp1[...] = times_trans(jnp.where(first, 0, dop).astype(BF16), vp)
        turned_q, turned_k, turned_do = qp.T, kp.T, dop.T
        both = dop.astype(F32) * ctx[:, cols].astype(F32)
        for e, dpe, dse in ((0, dp0, ds0), (1, dp1, ds1)):
            share = jnp.where(first, both, 0.0) if e == 0 else jnp.where(first, 0.0, both)
            delta = jnp.sum(share, axis=1, keepdims=True)
            for r in range(total // ROW_CHUNK):
                part = slice(r * ROW_CHUNK, (r + 1) * ROW_CHUNK)
                dse[part, :] = (prob[slot, e, part, :].astype(F32) * (dpe[part, :] - delta[part])).astype(BF16)
            here = slice(e * HEAD_DIM, (e + 1) * HEAD_DIM)
            there = pl.ds(pl.multiple_of(at + e * HEAD_DIM, HEAD_DIM), HEAD_DIM)
            dvt[there, :] = mat(turned_do[here], prob[slot, e]).astype(BF16)
            dqt[there, :] = (times_trans(turned_k[here], dse[...]) * HEAD_DIM ** (-0.5)).astype(BF16)
            dkt[there, :] = mat(turned_q[here], dse[...]).astype(BF16)

    for p in range(pairs):
        fetch_prob(p).wait()
        pair(p, p % 2)
        if p + 2 < pairs:
            fetch_prob(p + 2).start()
        if p == 0:
            advance(6)
        if p == 1:
            advance(0)
        if p == 2:
            advance(1)
        if p == 3:
            advance(2)

    need(11)
    turned[...] = x[...].T
    for s, right in ((7, dqt), (8, dkt), (9, dvt)):
        for h in range(2):
            by_owner(s, h, lambda left: times_trans(left, right[h * wide : (h + 1) * wide, :]))
        start(s, 0)
        advance(s - 4)

    need(16)
    ones = jnp.ones((8, total), BF16)
    vec[0:1, 0:width] = times_trans(ones, dqt[...])[0:1]
    vec[1:2, 0:width] = times_trans(ones, dvt[...])[0:1]
    for o in range(SPAN):
        tmp[...] = jnp.zeros_like(tmp)
        tmp[0:8, 0:rows] = vec[0:8, o * rows : (o + 1) * rows]
        tmp[8:9, :] = vec[8:9, o * ff_rows : o * ff_rows + 128]
        bufs[10][block_index(o, 0, plan[10][2])] = tmp[...].astype(BF16)
        tmp[...] = jnp.zeros_like(tmp)
        tmp[8:9, 0 : ff_rows - 128] = vec[8:9, o * ff_rows + 128 : (o + 1) * ff_rows]
        bufs[10][block_index(o, 1, plan[10][2])] = tmp[...].astype(BF16)
    start(10, 0)
    for s in (7, 8, 9, 10):
        advance(s)

    need(12, 13, 14, 15)
    for c in range(width // 256):
        part = slice(c * 256, (c + 1) * 256)
        dxt = mat(wq[part, :], dqt[...]) + mat(wk[part, :], dkt[...]) + mat(wv[part, :], dvt[...])
        dx = (dxt.T + dh1[:, part]).astype(BF16)
        dx_out[0, :, part] = dx[:span]
        dx_send[:, part] = dx[span:]
    side_dx = remote(dx_send, dx_out.at[1], side_sem.at[2], side_sem.at[3], partner["y"])

    while min(stage_of.values()) < 6:
        for s in sorted(range(count), key=lambda s: (stage_of[s], s)):
            if stage_of[s] < 6:
                advance(s)
    for side in (side_out, side_dx):
        side.wait()
    for copy in pending.values():
        copy.wait_send()


def reduce_grads(plan, low, args):
    count = len(plan)
    total, width = args[1].shape
    hbm = pl.BlockSpec(memory_space=pl.ANY)
    vm = pl.BlockSpec(memory_space=pltpu.VMEM)
    held = [pltpu.VMEM(a.shape, a.dtype) for a in args]
    held[9] = pltpu.VMEM((2, 2, total, total), BF16)
    held[17] = pltpu.VMEM((total // 2, width), BF16)
    return pl.pallas_call(
        functools.partial(reduce_kernel, plan, low),
        out_shape=[jax.ShapeDtypeStruct((2, r, c), BF16) for r, c, _ in plan]
        + [jax.ShapeDtypeStruct((2, total // 2, width), BF16), jax.ShapeDtypeStruct((total // 2, width), BF16)],
        in_specs=[hbm] * len(args),
        out_specs=[vm] * (count + 2),
        scratch_shapes=[pltpu.VMEM((32, r, c), BF16) for r, c, _ in plan] * 2
        + held
        + [
            pltpu.VMEM((width, total), BF16),
            pltpu.VMEM((16, 128), F32),
            pltpu.VMEM((width, total), BF16),
            pltpu.VMEM((width, total), BF16),
            pltpu.VMEM((width, total), BF16),
            pltpu.VMEM((total, total), F32),
            pltpu.VMEM((total, total), F32),
            pltpu.VMEM((total, total), BF16),
            pltpu.VMEM((total, total), BF16),
            pltpu.VMEM((total // 2, width), BF16),
            pltpu.SemaphoreType.DMA((len(args),)),
            pltpu.SemaphoreType.DMA((width // HEAD_PAIR,)),
            pltpu.SemaphoreType.DMA((count, 6)),
            pltpu.SemaphoreType.DMA((count, 6)),
            pltpu.SemaphoreType.DMA((4,)),
        ],
        compiler_params=pltpu.CompilerParams(
            collective_id=0, has_side_effects=True, vmem_limit_bytes=VMEM_LIMIT
        ),
        name="reduce_grads",
    )(*args)


def finish_kernel(rows, ff_rows, *refs):
    y_ref, out_own, out_got, dx_ref = refs[:4]
    res = refs[4:15]
    (out_ref, dx_full, wq, bq, wk, wv, bv, wo, bo, gain, shift, wi, bi, wout, bout, fgain, fshift) = refs[15:]
    y = y_ref[1]
    span = out_got.shape[0]
    out_ref[y] = out_own[0:span]
    out_ref[1 - y] = out_got[...]
    dx_full[y] = dx_ref[0].astype(F32)
    dx_full[1 - y] = dx_ref[1].astype(F32)
    col = res[0].shape[2]
    for s in range(3):
        for h in range(2):
            at = (2 * s + h) * col
            wout[:, at : at + col] = res[s][h].astype(F32)
    wide = res[3].shape[2]
    for s in range(3):
        for h in range(2):
            at = (2 * s + h) * wide
            wi[:, at : at + wide] = res[3 + s][h].astype(F32)
    wide = res[6].shape[2]
    for s, ref in ((6, wo), (7, wq), (8, wk), (9, wv)):
        for h in range(2):
            ref[:, h * wide : (h + 1) * wide] = res[s][h].astype(F32)
    vec = res[10][0].astype(F32)
    rest = res[10][1].astype(F32)
    for i, ref in enumerate((bq, bv, bo, gain, shift, bout, fgain, fshift)):
        ref[...] = vec[i, 0:rows]
    bi[0:128] = vec[8, :]
    bi[128:ff_rows] = rest[8, 0 : ff_rows - 128]


def finish(info, out, out_got, dx, res, width, ff):
    rows, ff_rows = width // SPAN, ff // SPAN
    square, line = (rows, width), (rows,)
    shapes = (
        square, line, square, square, line, square, line, line, line,
        (rows, ff), (ff_rows,), (ff_rows, width), line, line, line,
    )
    vm = pl.BlockSpec(memory_space=pltpu.VMEM)
    return pl.pallas_call(
        functools.partial(finish_kernel, rows, ff_rows),
        out_shape=[jax.ShapeDtypeStruct(dx.shape, BF16), jax.ShapeDtypeStruct(dx.shape, F32)]
        + [jax.ShapeDtypeStruct(s, F32) for s in shapes],
        in_specs=[pl.BlockSpec(memory_space=pltpu.SMEM)] + [vm] * (3 + len(res)),
        out_specs=[vm] * (2 + len(shapes)),
        name="finish",
    )(info, out, out_got, dx, *res)


def row_vec(ref):
    return ref[...].astype(F32).reshape(1, -1)


def attend_kernel(
    info_ref, x_ref, wq_ref, bq_ref, wk_ref, wv_ref, bv_ref,
    q_ref, k_ref, v_ref, ctx_ref, prob_ref, s0, s1,
):
    total, width = x_ref.shape
    span = total // 2
    wide = 256
    for w_ref, b_ref, out in ((wq_ref, bq_ref, q_ref), (wk_ref, None, k_ref), (wv_ref, bv_ref, v_ref)):
        bias = None if b_ref is None else row_vec(b_ref)
        for c in range(width // wide):
            cols = slice(c * wide, (c + 1) * wide)
            got = mat(x_ref[...], w_ref[:, cols])
            if bias is not None:
                got = got + bias[:, cols]
            got = got.astype(BF16)
            if out is q_ref:
                got = got * jnp.bfloat16(HEAD_DIM ** (-0.5))
            out[:, cols] = got

    length, y = info_ref[0], info_ref[1]
    at = lax.broadcasted_iota(jnp.int32, (1, total), 1)
    place = jnp.where(at < span, at + y * span, at - span + (1 - y) * span)
    bias = jnp.where(place < length, 0.0, -1e30).astype(F32)
    lane = lax.broadcasted_iota(jnp.int32, (1, HEAD_PAIR), 1)

    def pair(p, carry):
        cols = pl.ds(pl.multiple_of(p * HEAD_PAIR, HEAD_PAIR), HEAD_PAIR)
        qp, kp, vp = q_ref[:, cols], k_ref[:, cols], v_ref[:, cols]
        first = lane < HEAD_DIM
        s0[...] = times_trans(jnp.where(first, qp, 0).astype(BF16), kp)
        s1[...] = times_trans(jnp.where(first, 0, qp).astype(BF16), kp)
        parts = []
        for e, s in ((0, s0), (1, s1)):
            for r in range(total // ROW_CHUNK):
                rows = slice(r * ROW_CHUNK, (r + 1) * ROW_CHUNK)
                raw = s[rows, :] + bias
                expo = jnp.exp(raw - jnp.max(raw, axis=1, keepdims=True))
                scale = 1.0 / jnp.sum(expo, axis=1, keepdims=True)
                prob_ref[2 * p + e, rows, :] = (expo * scale).astype(BF16)
            parts.append(mat(prob_ref[2 * p + e], vp))
        ctx_ref[:, cols] = jnp.where(first, parts[0], parts[1]).astype(BF16)
        return carry

    lax.fori_loop(0, width // HEAD_PAIR, pair, 0)


def attend(info, x, wq, bq, wk, wv, bv):
    total, width = x.shape
    vm = pl.BlockSpec(memory_space=pltpu.VMEM)
    low = jax.ShapeDtypeStruct((total, width), BF16)
    return pl.pallas_call(
        attend_kernel,
        out_shape=[low, low, low, low, jax.ShapeDtypeStruct((width // HEAD_DIM, total, total), BF16)],
        in_specs=[pl.BlockSpec(memory_space=pltpu.SMEM)] + [vm] * 6,
        out_specs=[vm] * 5,
        scratch_shapes=[pltpu.VMEM((total, total), F32)] * 2,
        compiler_params=pltpu.CompilerParams(vmem_limit_bytes=VMEM_LIMIT),
        name="attend",
    )(info, x, wq, bq, wk, wv, bv)


def feed_kernel(
    ctx_ref, x_ref, cot_ref, wo_hbm, bo_ref, gain_ref, shift_ref, wi_hbm, bi_ref, wout_hbm, bout_ref, fgain_ref, fshift_ref,
    out_ref, act_ref, dpre_ref, db_ref, n1_ref, dattn_ref, dh1_ref, dctx_ref, vec_ref,
    wo, wi, wout, slope, hat1, r1, acc, pre_a, pre_b, sems,
):
    total, width = x_ref.shape
    ff = act_ref.shape[1]
    wide = pre_a.shape[1]
    loads = [
        pltpu.make_async_copy(src, dst, sems.at[i])
        for i, (src, dst) in enumerate(((wo_hbm, wo), (wi_hbm, wi), (wout_hbm, wout)))
    ]
    for load in loads:
        load.start()
    chunks = [slice(r * ROW_CHUNK, (r + 1) * ROW_CHUNK) for r in range(total // ROW_CHUNK)]

    loads[0].wait()
    acc[...] = mat(ctx_ref[...], wo[...])
    bo, gain, shift = row_vec(bo_ref), row_vec(gain_ref), row_vec(shift_ref)
    for rows in chunks:
        h1 = x_ref[rows, :].astype(F32) + acc[rows, :] + bo
        n1, hat, recip = norm_rows(h1, gain, shift)
        hat1[rows, :] = hat
        r1[rows, :] = jnp.broadcast_to(recip, (ROW_CHUNK, 128))
        n1_ref[rows, :] = n1.astype(BF16)

    loads[1].wait()
    loads[2].wait()

    def pre_of(j, into):
        cols = pl.ds(pl.multiple_of(j * wide, wide), wide)
        into[...] = mat(n1_ref[...], wi[:, cols])

    def activate(j, pre):
        cols = pl.ds(pl.multiple_of(j * wide, wide), wide)
        bias = bi_ref[:, cols].astype(F32)
        for rows in chunks:
            u = pre[rows, :] + bias
            half = 0.5 * (1.0 + lax.erf(u * HALF_ROOT))
            act_ref[rows, cols] = (u * half).astype(BF16)
            slope[rows, cols] = (half + u * jnp.exp(-0.5 * u * u) * INV_ROOT_TAU).astype(slope.dtype)

    steps = ff // wide
    pre_of(0, pre_a)

    def forward(i, carry):
        j = 2 * i
        pre_of(j + 1, pre_b)
        activate(j, pre_a)
        pre_of(lax.rem(j + 2, steps), pre_a)
        activate(j + 1, pre_b)
        return carry

    lax.fori_loop(0, steps // 2, forward, 0)

    acc[...] = mat(act_ref[...], wout[...])
    bout, fgain, fshift = row_vec(bout_ref), row_vec(fgain_ref), row_vec(fshift_ref)
    sums = [jnp.zeros((1, width), F32) for _ in range(6)]

    def down(v):
        return jnp.sum(v, axis=0, keepdims=True)

    for rows in chunks:
        n1 = hat1[rows, :] * gain + shift
        out, hat2, recip2 = norm_rows(n1 + acc[rows, :] + bout, fgain, fshift)
        out_ref[rows, :] = out.astype(BF16)
        g = cot_ref[rows, :].astype(F32)
        dh2 = norm_back(g, hat2, recip2, fgain)
        acc[rows, :] = dh2
        low = dh2.astype(BF16)
        db_ref[rows, :] = low
        sums[0] += down(g * hat2)
        sums[1] += down(g)
        sums[2] += down(low.astype(F32))

    def dact_of(j, into):
        cols = pl.ds(pl.multiple_of(j * wide, wide), wide)
        into[...] = times_trans(db_ref[...], wout[cols, :])

    def bend(j, dact):
        cols = pl.ds(pl.multiple_of(j * wide, wide), wide)
        total_sum = jnp.zeros((1, wide), F32)
        for rows in chunks:
            low = (dact[rows, :] * slope[rows, cols].astype(F32)).astype(BF16)
            dpre_ref[rows, cols] = low
            total_sum += down(low.astype(F32))
        vec_ref[8:9, cols] = total_sum

    dact_of(0, pre_a)

    def backward(i, carry):
        j = 2 * i
        dact_of(j + 1, pre_b)
        bend(j, pre_a)
        dact_of(lax.rem(j + 2, steps), pre_a)
        bend(j + 1, pre_b)
        return carry

    lax.fori_loop(0, steps // 2, backward, 0)

    acc[...] += times_trans(dpre_ref[...], wi[...])
    for rows in chunks:
        dn1 = acc[rows, :]
        hat = hat1[rows, :]
        dh1 = norm_back(dn1, hat, r1[rows, 0:1], gain)
        dh1_ref[rows, :] = dh1
        low = dh1.astype(BF16)
        dattn_ref[rows, :] = low
        sums[3] += down(dn1 * hat)
        sums[4] += down(dn1)
        sums[5] += down(low.astype(F32))
    for c in range(width // 256):
        cols = slice(c * 256, (c + 1) * 256)
        dctx_ref[:, cols] = times_trans(dattn_ref[...], wo[cols, :]).astype(BF16)
    zero = jnp.zeros((1, width), F32)
    for i, v in enumerate((zero, zero, sums[5], sums[3], sums[4], sums[2], sums[0], sums[1])):
        vec_ref[i : i + 1, 0:width] = v


def feed(ctx, x, cot, wo, bo, gain, shift, wi, bi, wout, bout, fgain, fshift):
    total, width = x.shape
    ff = wi.shape[1]
    vm = pl.BlockSpec(memory_space=pltpu.VMEM)
    hbm = pl.BlockSpec(memory_space=pl.ANY)
    low = jax.ShapeDtypeStruct((total, width), BF16)
    tall = jax.ShapeDtypeStruct((total, ff), BF16)
    wide = 256
    return pl.pallas_call(
        feed_kernel,
        out_shape=[
            low, tall, tall, low, low, low, jax.ShapeDtypeStruct((total, width), F32), low,
            jax.ShapeDtypeStruct((16, ff), F32),
        ],
        in_specs=[vm, vm, vm, hbm, vm, vm, vm, hbm, vm, hbm, vm, vm, vm],
        out_specs=[vm] * 9,
        scratch_shapes=[
            pltpu.VMEM((width, width), BF16),
            pltpu.VMEM((width, ff), BF16),
            pltpu.VMEM((ff, width), BF16),
            pltpu.VMEM((total, ff), F32),
            pltpu.VMEM((total, width), F32),
            pltpu.VMEM((total, 128), F32),
            pltpu.VMEM((total, width), F32),
            pltpu.VMEM((total, wide), F32),
            pltpu.VMEM((total, wide), F32),
            pltpu.SemaphoreType.DMA((3,)),
        ],
        compiler_params=pltpu.CompilerParams(vmem_limit_bytes=VMEM_LIMIT),
        name="feed",
    )(ctx, x, cot, wo, bo, gain, shift, wi, bi, wout, bout, fgain, fshift)


def per_device(
    dp_size,
    tokens,
    lengths,
    query_weight,
    query_bias,
    key_weight,
    value_weight,
    value_bias,
    out_weight,
    out_bias,
    norm_gain,
    norm_shift,
    inner_weight,
    inner_bias,
    outer_weight,
    outer_bias,
    final_gain,
    final_shift,
    cotangent,
):
    seqs, span, width = tokens.shape
    ff = inner_weight.shape[1]
    y = lax.axis_index("blk")
    swap = [(0, 1), (1, 0)]

    def own_sequence(arr):
        mine = lax.dynamic_index_in_dim(arr, y, 0, keepdims=False)
        other = lax.dynamic_index_in_dim(arr, 1 - y, 0, keepdims=False)
        return jnp.concatenate([mine, lax.ppermute(other, "blk", swap)], axis=0)

    x = own_sequence(tokens)
    cot = own_sequence(cotangent)
    length = lax.dynamic_index_in_dim(lengths, y, 0, keepdims=False)
    info = jnp.stack([length, y])
    q, k, v, ctx, prob = attend(info, x, query_weight, query_bias, key_weight, value_weight, value_bias)
    out, act, dpre, dbranch, n1_low, dattn, dh1, dctx, vecs = feed(
        ctx, x, cot, out_weight, out_bias, norm_gain, norm_shift, inner_weight, inner_bias[None],
        outer_weight, outer_bias, final_gain, final_shift,
    )
    plan = slab_plan(width, ff)
    low = dp_size // SPAN
    *res, dx, out_got = reduce_grads(
        plan, low,
        (act, dbranch, n1_low, dpre, ctx, dattn, k, v, dctx, prob, q, x, query_weight, key_weight, value_weight, dh1, vecs, out),
    )
    layer_out, input_grad, *grads = finish(info, out, out_got, dx, res, width, ff)
    if low > 1:
        groups = [[t * low + i for i in range(low)] for t in range(SPAN)]
        grads = [
            lax.psum_scatter(g, "dp", scatter_dimension=0, axis_index_groups=groups, tiled=True)
            for g in grads
        ]
    return (layer_out, input_grad, *grads)


def solution(mesh):
    rows3 = P("dp", "blk", None)
    grad2, grad1 = P("dp", None), P("dp")
    return jax.shard_map(
        functools.partial(per_device, mesh.shape["dp"]),
        mesh=mesh,
        in_specs=(rows3, P("dp")) + (P(),) * 15 + (rows3,),
        out_specs=(
            rows3, rows3, grad2, grad1, grad2, grad2, grad1, grad2, grad1,
            grad1, grad1, grad2, grad1, grad2, grad1, grad1, grad1,
        ),
        check_vma=False,
    )
```

```python
import functools

import jax
import jax.numpy as jnp
from jax import lax
from jax.experimental import pallas as pl
from jax.experimental.pallas import tpu as pltpu
from jax.sharding import PartitionSpec as P

HEADS = 12
HEAD_DIM = 64
HEAD_PAIR = 2 * HEAD_DIM
ROW_CHUNK = 64
EPS = 1e-12
HALF_ROOT = 0.7071067811865476
INV_ROOT_TAU = 0.3989422804014327
MESH = pl.DeviceIdType.MESH
BF16 = jnp.bfloat16
F32 = jnp.float32

ORDERS = {
    "A": ("c", "x", "y", "zl", "zh"),
    "C": ("c", "zl", "x", "y", "zh"),
    "E": ("c", "x", "zl", "y", "zh"),
    "G": ("c", "y", "x", "zl", "zh"),
    "H": ("c", "x", "zl", "zh", "y"),
    "M": ("c", "y", "zl", "zh", "x"),
}
SLAB_ORDERS = "ACMECGAGEHG"
EVENTS = (
    -1, -1, -1, 0, 1, -1, 2, -1, -1, -1, -1, 3, 4, -1, 5, 0, 1, -1, -1, 2,
    -1, -1, 3, 6, 4, -1, -1, 1, 5, 2, -1, -1, 0, 3, -1, 6, 1, -1, -1, 3,
    2, 4, -1, 7, 0, 8, 6, 9, 1, 4, 5, -1, 2, 3, -1, 10, 0, 6, 7, 1,
    8, 4, 2, 5, 3, 6, 8, 9, 5, 7, 10, 9, 0, 10, 7, 4, 6, 8, 10, 5,
    9, 7, 9, 8, 10, 7, 9, 8, 10,
)
BIT_OF = {"c": 1, "x": 2, "zl": 4, "zh": 8}
SPAN = 16
OFFSETS = (0, 16, 24, 28, 30, 31)
VMEM_LIMIT = 67_043_328


def contract_rows(left_mat, right_mat):
    return lax.dot_general(
        left_mat, right_mat, (((0,), (0,)), ((), ())), preferred_element_type=F32
    )


def times_trans(left_mat, right_mat):
    return lax.dot_general(
        left_mat, right_mat, (((1,), (1,)), ((), ())), preferred_element_type=F32
    )


def mat(left_mat, right_mat):
    return jnp.dot(left_mat, right_mat, preferred_element_type=F32)


def norm_rows(hidden, gain_vec, shift_vec):
    row_mean = jnp.mean(hidden, axis=-1, keepdims=True)
    centred = hidden - row_mean
    reciprocal = lax.rsqrt(jnp.mean(centred * centred, axis=-1, keepdims=True) + EPS)
    normed = centred * reciprocal
    return (normed * gain_vec + shift_vec, normed, reciprocal)


def norm_back(grad_in, normed, reciprocal, gain_vec):
    scaled = grad_in * gain_vec
    return reciprocal * (
        scaled
        - jnp.mean(scaled, axis=-1, keepdims=True)
        - normed * jnp.mean(scaled * normed, axis=-1, keepdims=True)
    )


def row_vec(ref):
    return ref[...].astype(F32).reshape(1, -1)


def block_index(owner, half, order):
    place = 0
    for dim in order:
        bit = half if dim == "y" else (owner // BIT_OF[dim]) % 2
        place = place * 2 + bit
    return place


def slab_plan(width, ff):
    rows, ff_rows = width // SPAN, ff // SPAN
    sizes = [(ff_rows, width // 6)] * 3 + [(rows, ff // 6)] * 3 + [(rows, width // 2)] * 4 + [(16, 128)]
    return tuple((r, c, ORDERS[o]) for (r, c), o in zip(sizes, SLAB_ORDERS))


def layer_kernel(plan, low, *refs):
    count = len(plan)
    (tokens, lengths, cot_in, wq, wk, wv, wo_in, wi_in, wout_in, bq, bv, bo, gain_in, shift_in, bi, bout_in, fgain_in, fshift_in) = refs[:18]
    res, refs = refs[18 : 18 + count], refs[18 + count :]
    dx_out, out_all, prob_hbm, qkv_hbm = refs[:4]
    refs = refs[4:]
    bufs, recvs, refs = refs[: count - 3], refs[count - 3 : 2 * count - 3], refs[2 * count - 3 :]
    (x, cot, ctx, db, n1, dattn, dctx, act, dpre, slope, wi, wout, wo, hat1, acc, r1, sa, sb, ds0, ds1) = refs[:20]
    (turned, dqt, dkt, dvt, tmp, vec, load_sem, prob_sem, send_sem, recv_sem, side_sem) = refs[20:]
    total, width = x.shape
    span = total // 2
    ff = act.shape[1]
    pairs = width // HEAD_PAIR
    wide = sa.shape[1]
    bufs = list(bufs[:7]) + [bufs[s].at[:, 0 : width // 2] for s in (3, 4, 5)] + [bufs[7]]

    dp = lax.axis_index("dp")
    y = lax.axis_index("blk")
    top = dp // low
    bits = {dim: (top // b) % 2 for dim, b in BIT_OF.items()}
    bits["y"] = y
    partner = {dim: (dp + (1 - 2 * bits[dim]) * (b * low), y) for dim, b in BIT_OF.items()}
    partner["y"] = (dp, 1 - y)

    loads = {}

    def load(name, src, dst, sem):
        loads[name] = pltpu.make_async_copy(src, dst, sem)
        loads[name].start()

    mine, theirs = pl.ds(0, span), pl.ds(span, span)
    load("x", tokens.at[y], x.at[mine], load_sem.at[0])
    for i, w in enumerate((wq, wk, wv)):
        load(i, w, wout.at[pl.ds(i * width, width)], load_sem.at[1 + i])
    load("wo", wo_in, wo, load_sem.at[4])
    load("cot", cot_in.at[y], cot.at[mine], load_sem.at[5])
    load("wi", wi_in, wi, load_sem.at[6])

    barrier = pltpu.get_barrier_semaphore()
    for where in partner.values():
        pl.semaphore_signal(barrier, inc=1, device_id=where, device_id_type=MESH)
    pl.semaphore_wait(barrier, len(partner))

    def remote(src, dst, send, recv, where):
        copy = pltpu.make_async_remote_copy(
            src_ref=src, dst_ref=dst, send_sem=send, recv_sem=recv, device_id=where, device_id_type=MESH
        )
        copy.start()
        return copy

    def side(i, src, dst):
        return remote(src, dst, side_sem.at[0, i], side_sem.at[1, i], partner["y"])

    x_swap = side(0, tokens.at[1 - y], x.at[theirs])
    cot_swap = side(1, cot_in.at[1 - y], cot.at[theirs])

    def down(v):
        return jnp.sum(v, axis=0, keepdims=True)

    loads["x"].wait()
    for half in (0, 1):
        rows = slice(half * span, (half + 1) * span)
        if half == 1:
            x_swap.wait_recv()
        for i, b_ref in enumerate((bq, None, bv)):
            if half == 0:
                loads[i].wait()
            bias = None if b_ref is None else row_vec(b_ref)
            for c in range(width // 256):
                cols = slice(c * 256, (c + 1) * 256)
                got = mat(x[rows, :], wout[i * width : (i + 1) * width, cols])
                if bias is not None:
                    got = got + bias[:, cols]
                got = got.astype(BF16)
                if i == 0:
                    got = got * jnp.bfloat16(HEAD_DIM ** (-0.5))
                act[rows, i * width + c * 256 : i * width + (c + 1) * 256] = got
    load("wout", wout_in, wout, load_sem.at[7])
    load("qkv", act.at[:, pl.ds(0, 3 * width)], qkv_hbm, load_sem.at[8])

    length = lengths[y]
    at = lax.broadcasted_iota(jnp.int32, (1, total), 1)
    place = jnp.where(at < span, at + y * span, at - span + (1 - y) * span)
    mask = jnp.where(place < length, 0.0, -1e30).astype(F32)
    first = lax.broadcasted_iota(jnp.int32, (1, HEAD_PAIR), 1) < HEAD_DIM

    def lanes(i, p):
        return pl.ds(pl.multiple_of(i * width + p * HEAD_PAIR, HEAD_PAIR), HEAD_PAIR)

    def prob_lanes(p, e):
        return pl.ds(pl.multiple_of((2 * p + e) * total, 128), total)

    def prob_copy(kept, p, base, e):
        return pltpu.make_async_copy(
            kept.at[0:total, prob_lanes(p, e)], prob_hbm.at[2 * (p + base) + e], prob_sem.at[0, 2 * (p + base) + e]
        )

    def prob_back(kept, p, base, e):
        return pltpu.make_async_copy(
            prob_hbm.at[2 * (p + base) + e], kept.at[0:total, prob_lanes(p, e)], prob_sem.at[1, 2 * (p + base) + e]
        )

    def attend(kept, base):
        def pair(p, carry):
            qp, kp, vp = act[:, lanes(0, p + base)], act[:, lanes(1, p + base)], act[:, lanes(2, p + base)]
            sa[...] = times_trans(jnp.where(first, qp, 0).astype(BF16), kp)
            sb[...] = times_trans(jnp.where(first, 0, qp).astype(BF16), kp)
            parts = []
            for e, s in ((0, sa), (1, sb)):
                for r in range(total // ROW_CHUNK):
                    rows = slice(r * ROW_CHUNK, (r + 1) * ROW_CHUNK)
                    raw = s[rows, :] + mask
                    expo = jnp.exp(raw - jnp.max(raw, axis=1, keepdims=True))
                    scale = 1.0 / jnp.sum(expo, axis=1, keepdims=True)
                    kept[rows, prob_lanes(p, e)] = (expo * scale).astype(BF16)
                parts.append(mat(kept[0:total, prob_lanes(p, e)], vp))
                prob_copy(kept, p, base, e).start()
            ctx[:, lanes(0, p + base)] = jnp.where(first, parts[0], parts[1]).astype(BF16)
            return carry

        lax.fori_loop(0, pairs // 2, pair, 0)

    attend(slope, 0)
    attend(dpre, pairs // 2)

    loads["wo"].wait()
    acc[...] = mat(ctx[...], wo[...])
    bo, gain, shift, bout = row_vec(bo), row_vec(gain_in), row_vec(shift_in), row_vec(bout_in)
    fgain, fshift = row_vec(fgain_in), row_vec(fshift_in)
    vec[9:10, :] = row_vec(bi)

    def chunk(r):
        return pl.ds(pl.multiple_of(r * ROW_CHUNK, ROW_CHUNK), ROW_CHUNK)

    def norm_one(r, carry):
        rows = chunk(r)
        normed, hat, recip = norm_rows(x[rows, :].astype(F32) + acc[rows, :] + bo, gain, shift)
        hat1[rows, :] = hat
        r1[rows, :] = jnp.broadcast_to(recip, (ROW_CHUNK, 128))
        n1[rows, :] = normed.astype(BF16)
        acc[rows, :] = normed + bout
        return carry

    lax.fori_loop(0, total // ROW_CHUNK, norm_one, 0)

    for p in range(pairs // 2):
        for e in range(2):
            prob_copy(slope, p, 0, e).wait()
    loads["qkv"].wait()
    loads["wi"].wait()
    loads["wout"].wait()

    def span_of(j):
        return pl.ds(pl.multiple_of(j * wide, wide), wide)

    def pre_of(j, into):
        into[...] = mat(n1[...], wi[:, span_of(j)])

    def activate(j, pre):
        bias = vec[9:10, span_of(j)]
        for r in range(total // ROW_CHUNK):
            rows = slice(r * ROW_CHUNK, (r + 1) * ROW_CHUNK)
            u = pre[rows, :] + bias
            half = 0.5 * (1.0 + lax.erf(u * HALF_ROOT))
            act[rows, span_of(j)] = (u * half).astype(BF16)
            slope[rows, span_of(j)] = (half + u * jnp.exp(-0.5 * u * u) * INV_ROOT_TAU).astype(BF16)

    def second(j):
        acc[...] += mat(act[:, span_of(j)], wout[span_of(j), :])

    steps = ff // wide
    pre_of(0, sa)

    def forward(i, carry):
        pre_of(2 * i + 1, sb)
        activate(2 * i, sa)
        second(2 * i)
        pre_of(lax.rem(2 * i + 2, steps), sa)
        activate(2 * i + 1, sb)
        second(2 * i + 1)
        return carry

    lax.fori_loop(0, steps // 2, forward, 0)

    loads["cot"].wait()
    cot_swap.wait_recv()
    zero = jnp.zeros((1, width), F32)

    def norm_two(r, sums):
        rows = chunk(r)
        out, hat2, recip2 = norm_rows(acc[rows, :], fgain, fshift)
        g = cot[rows, :].astype(F32)
        cot[rows, :] = out.astype(BF16)
        dh2 = norm_back(g, hat2, recip2, fgain)
        acc[rows, :] = dh2
        low_dh2 = dh2.astype(BF16)
        db[rows, :] = low_dh2
        return (sums[0] + down(g * hat2), sums[1] + down(g), sums[2] + down(low_dh2.astype(F32)))

    fgain_sum, fshift_sum, bout_sum = lax.fori_loop(0, total // ROW_CHUNK, norm_two, (zero, zero, zero))
    vec[5:6, 0:width] = bout_sum
    vec[6:7, 0:width] = fgain_sum
    vec[7:8, 0:width] = fshift_sum
    out_all[0] = cot[0:span, :]

    pending = {}
    stage_of = {}
    sent = set()

    def blocks(s, base, n):
        size = plan[s][0]
        return pl.ds(pl.multiple_of(base * size, 16), n * size)

    def start(s, i):
        if i == 5:
            src, dst, where = recvs[s].at[blocks(s, 30, 1)], recvs[s].at[blocks(s, 31, 1)], partner["y"]
        else:
            half = 16 >> i
            dim = plan[s][2][i]
            src_ref, base = (bufs[s], 0) if i == 0 else (recvs[s], OFFSETS[i - 1])
            src = src_ref.at[blocks(s, base + (1 - bits[dim]) * half, half)]
            dst = recvs[s].at[blocks(s, OFFSETS[i], half)]
            where = partner[dim]
        pending[s, i] = remote(src, dst, send_sem.at[s, i], recv_sem.at[s, i], where)
        stage_of[s] = i

    def advance(s):
        i = stage_of[s]
        pending[s, i].wait_recv()
        if i == 5:
            res[s][y] = recvs[s][blocks(s, 30, 1)]
            res[s][1 - y] = recvs[s][blocks(s, 31, 1)]
            stage_of[s] = 6
            return
        half = 16 >> i
        src_ref, base = (bufs[s], 0) if i == 0 else (recvs[s], OFFSETS[i - 1])
        mine = base + bits[plan[s][2][i]] * half

        def add(j, carry):
            got = blocks(s, OFFSETS[i] + j, 1)
            recvs[s][got] = recvs[s][got] + src_ref[blocks(s, mine + j, 1)]
            return carry

        lax.fori_loop(0, half, add, 0)
        start(s, i + 1)

    def put(s, owner, h, value):
        bufs[s][blocks(s, block_index(owner, h, plan[s][2]), 1)] = value

    rows_of, ff_rows, col = plan[3][0], plan[0][0], plan[0][1]

    def outer_rows(t, carry):
        at_row = pl.multiple_of(t * (2 * ff_rows), 128)
        part = contract_rows(act[:, pl.ds(at_row, 2 * ff_rows)], db[...]).astype(BF16)
        for e in range(2):
            for s in range(3):
                for h in range(2):
                    at = (2 * s + h) * col
                    put(s, 2 * t + e, h, part[e * ff_rows : (e + 1) * ff_rows, at : at + col])
        return carry

    def by_owner(s, h, product):
        for part in range(2):
            block = product(turned[part * 8 * rows_of : (part + 1) * 8 * rows_of, :]).astype(BF16)
            for o in range(8):
                put(s, part * 8 + o, h, block[o * rows_of : (o + 1) * rows_of])

    sides = []

    def outer_slabs():
        lax.fori_loop(0, SPAN // 2, outer_rows, 0)
        for s in range(3):
            start(s, 0)
        sides.append(side(2, cot.at[theirs], out_all.at[1]))
        load("qkv", qkv_hbm, act.at[:, pl.ds(0, 3 * width)], load_sem.at[8])
        dact_of(0, sa)

    def dact_of(j, into):
        into[...] = times_trans(db[...], wout[span_of(j), :])

    def bend(j, dact):
        sums = jnp.zeros((1, wide), F32)
        for r in range(total // ROW_CHUNK):
            rows = slice(r * ROW_CHUNK, (r + 1) * ROW_CHUNK)
            value = (dact[rows, :] * slope[rows, span_of(j)].astype(F32)).astype(BF16)
            dpre[rows, span_of(j)] = value
            sums += down(value.astype(F32))
        vec[8:9, span_of(j)] = sums

    def backward(i):
        if i == 0:
            for p in range(pairs // 2):
                for e in range(2):
                    prob_copy(dpre, p, pairs // 2, e).wait()
        dact_of(2 * i + 1, sb)
        bend(2 * i, sa)
        if 2 * i + 2 < steps:
            dact_of(2 * i + 2, sa)
        bend(2 * i + 1, sb)
        if i == steps // 2 - 1:
            for j, w in enumerate((wq, wk, wv)):
                load(j, w, wout.at[pl.ds(j * width, width)], load_sem.at[1 + j])
            turned[...] = n1[...].T

    def inner_slab(s):
        c = plan[s][1]
        for h in range(2):
            at = ((s - 3) * 2 + h) * c
            by_owner(s, h, lambda left: mat(left, dpre[:, at : at + c]))
        start(s, 0)

    def dn1_part(c):
        cols = slice(c * 256, (c + 1) * 256)
        acc[:, cols] += times_trans(dpre[...], wi[cols, :])

    def norm_one_back():
        for p in range(pairs // 2):
            for e in range(2):
                prob_back(wi, p, 0, e).start()
                prob_back(dpre, p, pairs // 2, e).start()

        def step(r, sums):
            rows = chunk(r)
            dn1, hat = acc[rows, :], hat1[rows, :]
            dh1 = norm_back(dn1, hat, r1[rows, 0:1], gain)
            acc[rows, :] = dh1
            low_dh1 = dh1.astype(BF16)
            dattn[rows, :] = low_dh1
            return (sums[0] + down(dn1 * hat), sums[1] + down(dn1), sums[2] + down(low_dh1.astype(F32)))

        a, b, c = lax.fori_loop(0, total // ROW_CHUNK, step, (zero, zero, zero))
        vec[3:4, 0:width] = a
        vec[4:5, 0:width] = b
        vec[2:3, 0:width] = c

    half_width = width // 2

    def out_slab():
        turned[...] = ctx[...].T
        for h in range(2):
            by_owner(6, h, lambda left: mat(left, dattn[:, h * half_width : (h + 1) * half_width]))
        start(6, 0)
        for c in range(width // 256):
            cols = slice(c * 256, (c + 1) * 256)
            dctx[:, cols] = times_trans(dattn[...], wo[cols, :]).astype(BF16)

    def pair_back(p):
        if p == 0:
            loads["qkv"].wait()
        kept, base = (wi, 0) if p < pairs // 2 else (dpre, pairs // 2)
        for e in range(2):
            prob_back(kept, p - base, base, e).wait()
        qp, kp, vp, dop = act[:, lanes(0, p)], act[:, lanes(1, p)], act[:, lanes(2, p)], dctx[:, lanes(0, p)]
        sa[...] = times_trans(jnp.where(first, dop, 0).astype(BF16), vp)
        sb[...] = times_trans(jnp.where(first, 0, dop).astype(BF16), vp)
        turned_q, turned_k, turned_do = qp.T, kp.T, dop.T
        both = dop.astype(F32) * ctx[:, lanes(0, p)].astype(F32)
        for e, dpe, dse in ((0, sa, ds0), (1, sb, ds1)):
            share = jnp.where(first, both, 0.0) if e == 0 else jnp.where(first, 0.0, both)
            delta = jnp.sum(share, axis=1, keepdims=True)
            for r in range(total // ROW_CHUNK):
                part = slice(r * ROW_CHUNK, (r + 1) * ROW_CHUNK)
                dse[part, :] = (kept[part, prob_lanes(p - base, e)].astype(F32) * (dpe[part, :] - delta[part])).astype(BF16)
            here = slice(e * HEAD_DIM, (e + 1) * HEAD_DIM)
            there = pl.ds(p * HEAD_PAIR + e * HEAD_DIM, HEAD_DIM)
            dvt[there, :] = mat(turned_do[here], kept[0:total, prob_lanes(p - base, e)]).astype(BF16)
            dqt[there, :] = (times_trans(turned_k[here], dse[...]) * HEAD_DIM ** (-0.5)).astype(BF16)
            dkt[there, :] = mat(turned_q[here], dse[...]).astype(BF16)

    def head_slab(s, right):
        if s == 7:
            turned[...] = x[...].T
        pending[s - 4, 0].wait_send()
        sent.add((s - 4, 0))
        for h in range(2):
            by_owner(s, h, lambda left: times_trans(left, right[h * half_width : (h + 1) * half_width, :]))
        start(s, 0)

    def vectors():
        ones = jnp.ones((8, total), BF16)
        vec[0:1, 0:width] = times_trans(ones, dqt[...])[0:1]
        vec[1:2, 0:width] = times_trans(ones, dvt[...])[0:1]
        for o in range(SPAN):
            tmp[...] = jnp.zeros_like(tmp)
            tmp[0:8, 0:rows_of] = vec[0:8, o * rows_of : (o + 1) * rows_of]
            tmp[8:9, :] = vec[8:9, o * ff_rows : o * ff_rows + 128]
            put(10, o, 0, tmp[...].astype(BF16))
            tmp[...] = jnp.zeros_like(tmp)
            tmp[8:9, 0 : ff_rows - 128] = vec[8:9, o * ff_rows + 128 : (o + 1) * ff_rows]
            put(10, o, 1, tmp[...].astype(BF16))
        start(10, 0)

    def input_part():
        for i in range(3):
            loads[i].wait()
        for c in range(width // 256):
            cols = slice(c * 256, (c + 1) * 256)
            dxt = sum(
                mat(wout[i * width + c * 256 : i * width + (c + 1) * 256, :], d[...])
                for i, d in enumerate((dqt, dkt, dvt))
            )
            dx = (dxt.T + acc[:, cols]).astype(BF16)
            dx_out[0, :, cols] = dx[:span]
            db[0:span, cols] = dx[span:]
        sides.append(side(3, db.at[mine], dx_out.at[1]))

    pieces = [outer_slabs]
    pieces += [functools.partial(backward, i) for i in range(steps // 2)]
    pieces += [functools.partial(inner_slab, s) for s in (3, 4, 5)]
    pieces += [functools.partial(dn1_part, c) for c in range(width // 256)]
    pieces += [norm_one_back, out_slab]
    pieces += [functools.partial(pair_back, p) for p in range(pairs)]
    pieces += [functools.partial(head_slab, s, r) for s, r in ((7, dqt), (8, dkt), (9, dvt))]
    pieces += [vectors, input_part]
    for event in EVENTS:
        if event < 0:
            pieces.pop(0)()
        else:
            advance(event)
    for wait in (x_swap, cot_swap):
        wait.wait_send()
    for wait in sides:
        wait.wait()
    for key, copy in pending.items():
        if key not in sent:
            copy.wait_send()


def run_layer(plan, low, args):
    count = len(plan)
    tokens = args[0]
    _, span, width = tokens.shape
    total = 2 * span
    ff = args[7].shape[1]
    hbm = pl.BlockSpec(memory_space=pl.ANY)
    vm = pl.BlockSpec(memory_space=pltpu.VMEM)
    smem = pl.BlockSpec(memory_space=pltpu.SMEM)
    low_shape, tall = pltpu.VMEM((total, width), BF16), pltpu.VMEM((total, ff), BF16)
    turned = pltpu.VMEM((width, total), BF16)
    own = [s for s in range(count) if s not in (7, 8, 9)]
    return pl.pallas_call(
        functools.partial(layer_kernel, plan, low),
        out_shape=[jax.ShapeDtypeStruct((2, r, c), BF16) for r, c, _ in plan]
        + [
            jax.ShapeDtypeStruct((2, span, width), BF16),
            jax.ShapeDtypeStruct((2, span, width), BF16),
            jax.ShapeDtypeStruct((width // HEAD_DIM, total, total), BF16),
            jax.ShapeDtypeStruct((total, 3 * width), BF16),
        ],
        in_specs=[hbm, smem] + [hbm] * 7 + [vm] * 9,
        out_specs=[vm] * (count + 2) + [hbm] * 2,
        scratch_shapes=[pltpu.VMEM((32 * plan[s][0], plan[s][1]), BF16) for s in own]
        + [pltpu.VMEM((32 * r, c), BF16) for r, c, _ in plan]
        + [low_shape] * 7
        + [tall] * 3
        + [
            pltpu.VMEM((width, ff), BF16),
            pltpu.VMEM((ff, width), BF16),
            pltpu.VMEM((width, width), BF16),
            pltpu.VMEM((total, width), F32),
            pltpu.VMEM((total, width), F32),
            pltpu.VMEM((total, 128), F32),
            pltpu.VMEM((total, total), F32),
            pltpu.VMEM((total, total), F32),
            pltpu.VMEM((total, total), BF16),
            pltpu.VMEM((total, total), BF16),
            turned, turned, turned, turned,
            pltpu.VMEM((16, 128), F32),
            pltpu.VMEM((16, ff), F32),
            pltpu.SemaphoreType.DMA((9,)),
            pltpu.SemaphoreType.DMA((2, width // HEAD_DIM)),
            pltpu.SemaphoreType.DMA((count, 6)),
            pltpu.SemaphoreType.DMA((count, 6)),
            pltpu.SemaphoreType.DMA((2, 4)),
        ],
        compiler_params=pltpu.CompilerParams(
            collective_id=0, has_side_effects=True, vmem_limit_bytes=VMEM_LIMIT
        ),
        name="layer",
    )(*args)


def finish_kernel(rows, ff_rows, *refs):
    y = lax.axis_index("blk")
    out_in, dx_in = refs[:2]
    res = refs[2:13]
    (out_ref, dx_full, wq, bq, wk, wv, bv, wo, bo, gain, shift, wi, bi, wout, bout, fgain, fshift) = refs[13:]
    out_ref[y] = out_in[0]
    out_ref[1 - y] = out_in[1]
    dx_full[y] = dx_in[0].astype(F32)
    dx_full[1 - y] = dx_in[1].astype(F32)
    col = res[0].shape[2]
    for s in range(3):
        for h in range(2):
            at = (2 * s + h) * col
            wout[:, at : at + col] = res[s][h].astype(F32)
    wide = res[3].shape[2]
    for s in range(3):
        for h in range(2):
            at = (2 * s + h) * wide
            wi[:, at : at + wide] = res[3 + s][h].astype(F32)
    wide = res[6].shape[2]
    for s, ref in ((6, wo), (7, wq), (8, wk), (9, wv)):
        for h in range(2):
            ref[:, h * wide : (h + 1) * wide] = res[s][h].astype(F32)
    vec = res[10][0].astype(F32)
    rest = res[10][1].astype(F32)
    for i, ref in enumerate((bq, bv, bo, gain, shift, bout, fgain, fshift)):
        ref[...] = vec[i, 0:rows]
    bi[0:128] = vec[8, :]
    bi[128:ff_rows] = rest[8, 0 : ff_rows - 128]


def finish(out, dx, res, width, ff):
    rows, ff_rows = width // SPAN, ff // SPAN
    square, line = (rows, width), (rows,)
    shapes = (
        square, line, square, square, line, square, line, line, line,
        (rows, ff), (ff_rows,), (ff_rows, width), line, line, line,
    )
    vm = pl.BlockSpec(memory_space=pltpu.VMEM)
    return pl.pallas_call(
        functools.partial(finish_kernel, rows, ff_rows),
        out_shape=[jax.ShapeDtypeStruct(dx.shape, BF16), jax.ShapeDtypeStruct(dx.shape, F32)]
        + [jax.ShapeDtypeStruct(s, F32) for s in shapes],
        in_specs=[vm] * (2 + len(res)),
        out_specs=[vm] * (2 + len(shapes)),
        name="finish",
    )(out, dx, *res)


def per_device(
    dp_size,
    tokens,
    lengths,
    query_weight,
    query_bias,
    key_weight,
    value_weight,
    value_bias,
    out_weight,
    out_bias,
    norm_gain,
    norm_shift,
    inner_weight,
    inner_bias,
    outer_weight,
    outer_bias,
    final_gain,
    final_shift,
    cotangent,
):
    width, ff = inner_weight.shape
    plan = slab_plan(width, ff)
    low = dp_size // SPAN
    *res, dx, out, _, _ = run_layer(
        plan, low,
        (
            tokens, lengths, cotangent, query_weight, key_weight, value_weight, out_weight, inner_weight, outer_weight,
            query_bias, value_bias, out_bias, norm_gain, norm_shift, inner_bias, outer_bias, final_gain, final_shift,
        ),
    )
    layer_out, input_grad, *grads = finish(out, dx, res, width, ff)
    if low > 1:
        groups = [[t * low + i for i in range(low)] for t in range(SPAN)]
        grads = [
            lax.psum_scatter(g, "dp", scatter_dimension=0, axis_index_groups=groups, tiled=True)
            for g in grads
        ]
    return (layer_out, input_grad, *grads)


def solution(mesh):
    rows3 = P("dp", "blk", None)
    grad2, grad1 = P("dp", None), P("dp")
    return jax.shard_map(
        functools.partial(per_device, mesh.shape["dp"]),
        mesh=mesh,
        in_specs=(rows3, P("dp")) + (P(),) * 15 + (rows3,),
        out_specs=(
            rows3, rows3, grad2, grad1, grad2, grad2, grad1, grad2, grad1,
            grad1, grad1, grad2, grad1, grad2, grad1, grad1, grad1,
        ),
        check_vma=False,
    )
```

```python
import functools

import jax
import jax.numpy as jnp
from jax import lax
from jax.experimental import pallas as pl
from jax.experimental.pallas import tpu as pltpu
from jax.sharding import PartitionSpec as P

HEADS = 12
HEAD_DIM = 64
HEAD_PAIR = 2 * HEAD_DIM
ROW_CHUNK = 64
NORM_CHUNK = 256
EPS = 1e-12
HALF_ROOT = 0.7071067811865476
INV_ROOT_TAU = 0.3989422804014327
MESH = pl.DeviceIdType.MESH
BF16 = jnp.bfloat16
F32 = jnp.float32

ORDERS = {
    "A": ("c", "x", "y", "zl", "zh"),
    "B": ("c", "y", "zl", "x", "zh"),
    "C": ("c", "zl", "x", "y", "zh"),
    "E": ("c", "x", "zl", "y", "zh"),
    "F": ("c", "zl", "y", "x", "zh"),
    "G": ("c", "y", "x", "zl", "zh"),
    "H": ("c", "x", "zl", "zh", "y"),
    "M": ("c", "y", "zl", "zh", "x"),
}
SLAB_ORDERS = ("HC", "BM", "EC", "EA", "FE", "MG", "MH", "AH", "EC", "EA", "AC")
EVENTS = (
    -1, -1, -1, 0, -1, 1, 2, -1, -1, -1, 0, 3, -1, 4, 5, -1, -1, 2, 0, -1,
    -1, 1, -1, -1, -1, 6, -1, -1, -1, 3, -1, -1, -1, -1, -1, 1, 5, -1, 4, -1,
    0, -1, -1, 2, 1, 7, -1, 8, 3, 9, 6, 10, -1, 4, -1, 0, -1, 2, 5, 1,
    0, 3, 6, 7, 8, 2, 5, 3, 1, 6, 9, 7, 10, 2, 3, 8, 4, 10, 5, 9,
    6, 7, 8, 10, 5, 4, 9, 7, 6, 8, 10, 4, 7, 9, 8, 10, 9,
)
BIT_OF = {"c": 1, "x": 2, "zl": 4, "zh": 8}
SPAN = 16
OFFSETS = (0, 16, 24, 28, 30, 31)
VMEM_LIMIT = 67_043_328


def contract_rows(left_mat, right_mat):
    return lax.dot_general(
        left_mat, right_mat, (((0,), (0,)), ((), ())), preferred_element_type=F32
    )


def times_trans(left_mat, right_mat):
    return lax.dot_general(
        left_mat, right_mat, (((1,), (1,)), ((), ())), preferred_element_type=F32
    )


def mat(left_mat, right_mat):
    return jnp.dot(left_mat, right_mat, preferred_element_type=F32)


def norm_rows(hidden, gain_vec, shift_vec):
    row_mean = jnp.mean(hidden, axis=-1, keepdims=True)
    centred = hidden - row_mean
    reciprocal = lax.rsqrt(jnp.mean(centred * centred, axis=-1, keepdims=True) + EPS)
    normed = centred * reciprocal
    return (normed * gain_vec + shift_vec, normed, reciprocal)


def norm_back(grad_in, normed, reciprocal, gain_vec):
    scaled = grad_in * gain_vec
    return reciprocal * (
        scaled
        - jnp.mean(scaled, axis=-1, keepdims=True)
        - normed * jnp.mean(scaled * normed, axis=-1, keepdims=True)
    )


def row_vec(ref):
    return ref[...].astype(F32).reshape(1, -1)


def block_index(owner, half, order):
    place = 0
    for dim in order:
        bit = half if dim == "y" else (owner // BIT_OF[dim]) % 2
        place = place * 2 + bit
    return place


def slab_plan(width, ff):
    rows, ff_rows = width // SPAN, ff // SPAN
    sizes = [(ff_rows, width // 6)] * 3 + [(rows, ff // 6)] * 3 + [(rows, width // 2)] * 4 + [(16, 128)]
    return tuple((r, c, (ORDERS[o[0]], ORDERS[o[1]])) for (r, c), o in zip(sizes, SLAB_ORDERS))


def layer_kernel(plan, low, *refs):
    count = len(plan)
    (tokens, lengths, cot_in, wq, wk, wv, wo_in, wi_in, wout_in, bq, bv, bo, gain_in, shift_in, bi, bout_in, fgain_in, fshift_in) = refs[:18]
    res, refs = refs[18 : 18 + count], refs[18 + count :]
    dx_out, out_all, prob_hbm, qkv_hbm = refs[:4]
    refs = refs[4:]
    bufs, recvs, refs = refs[: count - 3], refs[count - 3 : 2 * count - 3], refs[2 * count - 3 :]
    (x, cot, ctx, db, n1, act, dpre, slope, wi, wout, wo, hat1, acc, r1, sa, sb) = refs[:16]
    (turned, dqt, dkt, dvt, tmp, vec, load_sem, prob_sem, send_sem, recv_sem, side_sem) = refs[16:]
    dattn, dctx = n1, db
    total, width = x.shape
    span = total // 2
    ff = act.shape[1]
    pairs = width // HEAD_PAIR
    wide = sa.shape[1]
    bufs = list(bufs[:7]) + [bufs[s].at[:, 0 : width // 2] for s in (3, 4, 5)] + [bufs[7]]

    dp = lax.axis_index("dp")
    y = lax.axis_index("blk")
    top = dp // low
    bits = {dim: (top // b) % 2 for dim, b in BIT_OF.items()}
    bits["y"] = y
    partner = {dim: (dp + (1 - 2 * bits[dim]) * (b * low), y) for dim, b in BIT_OF.items()}
    partner["y"] = (dp, 1 - y)

    loads = {}

    def load(name, src, dst, sem):
        loads[name] = pltpu.make_async_copy(src, dst, sem)
        loads[name].start()

    mine, theirs = pl.ds(0, span), pl.ds(span, span)
    load("x", tokens.at[y], x.at[mine], load_sem.at[0])
    for i, w in enumerate((wq, wk, wv)):
        load(i, w, wout.at[pl.ds(i * width, width)], load_sem.at[1 + i])
    load("wo", wo_in, wo, load_sem.at[4])
    load("cot", cot_in.at[y], cot.at[mine], load_sem.at[5])
    load("wi", wi_in, wi, load_sem.at[6])

    barrier = pltpu.get_barrier_semaphore()
    for where in partner.values():
        pl.semaphore_signal(barrier, inc=1, device_id=where, device_id_type=MESH)
    pl.semaphore_wait(barrier, len(partner))

    def remote(src, dst, send, recv, where):
        copy = pltpu.make_async_remote_copy(
            src_ref=src, dst_ref=dst, send_sem=send, recv_sem=recv, device_id=where, device_id_type=MESH
        )
        copy.start()
        return copy

    def side(i, src, dst):
        return remote(src, dst, side_sem.at[0, i], side_sem.at[1, i], partner["y"])

    part = span // 2
    x_swaps = [
        side(i, tokens.at[1 - y, pl.ds(i * part, part)], x.at[pl.ds(span + i * part, part)]) for i in range(2)
    ]
    cot_swap = side(2, cot_in.at[1 - y], cot.at[theirs])

    def down(v):
        return jnp.sum(v, axis=0, keepdims=True)

    loads["x"].wait()
    for half in range(3):
        rows = slice(0, span) if half == 0 else slice(span + (half - 1) * part, span + half * part)
        if half > 0:
            x_swaps[half - 1].wait_recv()
        for i, b_ref in enumerate((bq, None, bv)):
            if half == 0:
                loads[i].wait()
            bias = None if b_ref is None else row_vec(b_ref)
            for c in range(width // 256):
                cols = slice(c * 256, (c + 1) * 256)
                got = mat(x[rows, :], wout[i * width : (i + 1) * width, cols])
                if bias is not None:
                    got = got + bias[:, cols]
                got = got.astype(BF16)
                if i == 0:
                    got = got * jnp.bfloat16(HEAD_DIM ** (-0.5))
                act[rows, i * width + c * 256 : i * width + (c + 1) * 256] = got
    load("wout", wout_in, wout, load_sem.at[7])
    load("qkv", act.at[:, pl.ds(0, 3 * width)], qkv_hbm, load_sem.at[8])

    length = lengths[y]
    at = lax.broadcasted_iota(jnp.int32, (1, total), 1)
    place = jnp.where(at < span, at + y * span, at - span + (1 - y) * span)
    mask = jnp.where(place < length, 0.0, -1e30).astype(F32)
    first = lax.broadcasted_iota(jnp.int32, (1, HEAD_PAIR), 1) < HEAD_DIM

    def lanes(i, p):
        return pl.ds(pl.multiple_of(i * width + p * HEAD_PAIR, HEAD_PAIR), HEAD_PAIR)

    def prob_lanes(p, e):
        return pl.ds(pl.multiple_of((2 * p + e) * total, 128), total)

    def prob_copy(kept, p, base, e):
        return pltpu.make_async_copy(
            kept.at[0:total, prob_lanes(p, e)], prob_hbm.at[2 * (p + base) + e], prob_sem.at[0, 2 * (p + base) + e]
        )

    def prob_back(kept, p, base, e):
        return pltpu.make_async_copy(
            prob_hbm.at[2 * (p + base) + e], kept.at[0:total, prob_lanes(p, e)], prob_sem.at[1, 2 * (p + base) + e]
        )

    def scores(p, e, into):
        qp, kp = act[:, lanes(0, p)], act[:, lanes(1, p)]
        keep = jnp.where(first, qp, 0) if e == 0 else jnp.where(first, 0, qp)
        into[...] = times_trans(keep.astype(BF16), kp)

    def soften(kept, p, base, e, s):
        for r in range(total // ROW_CHUNK):
            rows = slice(r * ROW_CHUNK, (r + 1) * ROW_CHUNK)
            raw = s[rows, :] + mask
            expo = jnp.exp(raw - jnp.max(raw, axis=1, keepdims=True))
            scale = 1.0 / jnp.sum(expo, axis=1, keepdims=True)
            kept[rows, prob_lanes(p, e)] = (expo * scale).astype(BF16)
        prob_copy(kept, p, base, e).start()

    scores(0, 0, sa)
    for p in range(pairs):
        kept, base = (slope, 0) if p < pairs // 2 else (dpre, pairs // 2)
        vp = act[:, lanes(2, p)]
        scores(p, 1, sb)
        soften(kept, p - base, base, 0, sa)
        if p + 1 < pairs:
            scores(p + 1, 0, sa)
        even = mat(kept[0:total, prob_lanes(p - base, 0)], vp)
        soften(kept, p - base, base, 1, sb)
        odd = mat(kept[0:total, prob_lanes(p - base, 1)], vp)
        ctx[:, lanes(0, p)] = jnp.where(first, even, odd).astype(BF16)

    loads["wo"].wait()
    acc[...] = mat(ctx[...], wo[...])
    bo, gain, shift, bout = row_vec(bo), row_vec(gain_in), row_vec(shift_in), row_vec(bout_in)
    fgain, fshift = row_vec(fgain_in), row_vec(fshift_in)
    vec[9:10, :] = row_vec(bi)

    def chunk(r):
        return pl.ds(pl.multiple_of(r * NORM_CHUNK, NORM_CHUNK), NORM_CHUNK)

    def norm_one(r, carry):
        rows = chunk(r)
        normed, hat, recip = norm_rows(x[rows, :].astype(F32) + acc[rows, :] + bo, gain, shift)
        hat1[rows, :] = hat
        r1[rows, :] = jnp.broadcast_to(recip, (NORM_CHUNK, 128))
        n1[rows, :] = normed.astype(BF16)
        acc[rows, :] = normed + bout
        return carry

    lax.fori_loop(0, total // NORM_CHUNK, norm_one, 0)

    for p in range(pairs // 2):
        for e in range(2):
            prob_copy(slope, p, 0, e).wait()
    loads["qkv"].wait()
    loads["wi"].wait()
    loads["wout"].wait()

    def span_of(j):
        return pl.ds(pl.multiple_of(j * wide, wide), wide)

    def pre_of(j, into):
        into[...] = mat(n1[...], wi[:, span_of(j)])

    def activate(j, pre):
        bias = vec[9:10, span_of(j)]
        for r in range(total // ROW_CHUNK):
            rows = slice(r * ROW_CHUNK, (r + 1) * ROW_CHUNK)
            u = pre[rows, :] + bias
            half = 0.5 * (1.0 + lax.erf(u * HALF_ROOT))
            act[rows, span_of(j)] = (u * half).astype(BF16)
            slope[rows, span_of(j)] = (half + u * jnp.exp(-0.5 * u * u) * INV_ROOT_TAU).astype(BF16)

    def second(j):
        acc[...] += mat(act[:, span_of(j)], wout[span_of(j), :])

    steps = ff // wide
    pre_of(0, sa)

    for i in range(steps // 2):
        pre_of(2 * i + 1, sb)
        activate(2 * i, sa)
        if i > 0:
            second(2 * i - 1)
        if i + 1 < steps // 2:
            pre_of(2 * i + 2, sa)
        activate(2 * i + 1, sb)
        second(2 * i)
    second(steps - 1)

    loads["cot"].wait()
    cot_swap.wait_recv()
    zero = jnp.zeros((1, width), F32)

    def norm_two(r, sums):
        rows = chunk(r)
        out, hat2, recip2 = norm_rows(acc[rows, :], fgain, fshift)
        g = cot[rows, :].astype(F32)
        cot[rows, :] = out.astype(BF16)
        dh2 = norm_back(g, hat2, recip2, fgain)
        acc[rows, :] = dh2
        low_dh2 = dh2.astype(BF16)
        db[rows, :] = low_dh2
        return (sums[0] + down(g * hat2), sums[1] + down(g), sums[2] + down(low_dh2.astype(F32)))

    fgain_sum, fshift_sum, bout_sum = lax.fori_loop(0, total // NORM_CHUNK, norm_two, (zero, zero, zero))
    vec[5:6, 0:width] = bout_sum
    vec[6:7, 0:width] = fgain_sum
    vec[7:8, 0:width] = fshift_sum
    out_all[0] = cot[0:span, :]

    pending = {}
    stage_of = {}
    sent = set()

    def blocks(s, base, n):
        size = plan[s][0]
        return pl.ds(pl.multiple_of(base * size, 16), n * size)

    def step_of(s, i):
        even, odd = (plan[s][2][c][i] for c in range(2))
        if even == odd:
            return bits[even], partner[even]
        own = bits["c"]
        return (
            bits[even] + own * (bits[odd] - bits[even]),
            tuple(a + own * (b - a) for a, b in zip(partner[even], partner[odd])),
        )

    def start(s, i):
        if i == 5:
            src, dst, where = recvs[s].at[blocks(s, 30, 1)], recvs[s].at[blocks(s, 31, 1)], partner["y"]
        else:
            half = 16 >> i
            bit, where = step_of(s, i)
            src_ref, base = (bufs[s], 0) if i == 0 else (recvs[s], OFFSETS[i - 1])
            src = src_ref.at[blocks(s, base + (1 - bit) * half, half)]
            dst = recvs[s].at[blocks(s, OFFSETS[i], half)]
        pending[s, i] = remote(src, dst, send_sem.at[s, i], recv_sem.at[s, i], where)
        stage_of[s] = i

    def advance(s):
        i = stage_of[s]
        pending[s, i].wait_recv()
        if i == 5:
            res[s][y] = recvs[s][blocks(s, 30, 1)]
            res[s][1 - y] = recvs[s][blocks(s, 31, 1)]
            stage_of[s] = 6
            return
        half = 16 >> i
        src_ref, base = (bufs[s], 0) if i == 0 else (recvs[s], OFFSETS[i - 1])
        mine = base + step_of(s, i)[0] * half

        def add(j, carry):
            got = blocks(s, OFFSETS[i] + j, 1)
            recvs[s][got] = recvs[s][got] + src_ref[blocks(s, mine + j, 1)]
            return carry

        lax.fori_loop(0, half, add, 0)
        start(s, i + 1)

    def put(s, owner, core, h, value):
        bufs[s][blocks(s, block_index(owner, h, plan[s][2][core]), 1)] = value

    rows_of, ff_rows, col = plan[3][0], plan[0][0], plan[0][1]

    def turn_outer(t):
        n = 2 * ff_rows
        turned[t % 2 * n : t % 2 * n + n, :] = act[:, t * n : (t + 1) * n].T

    def outer_rows(t):
        n = 2 * ff_rows
        part = mat(turned[t % 2 * n : t % 2 * n + n, :], db[...]).astype(BF16)
        for e in range(2):
            for s in range(3):
                for h in range(2):
                    at = (2 * s + h) * col
                    put(s, 2 * t + e, e, h, part[e * ff_rows : (e + 1) * ff_rows, at : at + col])

    def by_owner(s, h, product):
        for part in range(2):
            block = product(turned[part * 8 * rows_of : (part + 1) * 8 * rows_of, :]).astype(BF16)
            for o in range(8):
                put(s, part * 8 + o, o % 2, h, block[o * rows_of : (o + 1) * rows_of])

    sides = []

    def outer_slabs():
        turn_outer(0)
        for t in range(SPAN // 2):
            if t + 1 < SPAN // 2:
                turn_outer(t + 1)
            outer_rows(t)
        for s in range(3):
            start(s, 0)
        sides.append(side(3, cot.at[theirs], out_all.at[1]))
        load("qkv", qkv_hbm, act.at[:, pl.ds(0, 3 * width)], load_sem.at[8])
        dact_of(0, sa)

    def dact_of(j, into):
        into[...] = times_trans(db[...], wout[span_of(j), :])

    def bend(j, dact):
        sums = jnp.zeros((1, wide), F32)
        for r in range(total // ROW_CHUNK):
            rows = slice(r * ROW_CHUNK, (r + 1) * ROW_CHUNK)
            value = (dact[rows, :] * slope[rows, span_of(j)].astype(F32)).astype(BF16)
            dpre[rows, span_of(j)] = value
            sums += down(value.astype(F32))
        vec[8:9, span_of(j)] = sums

    def backward(i):
        if i == 0:
            for p in range(pairs // 2):
                for e in range(2):
                    prob_copy(dpre, p, pairs // 2, e).wait()
        dact_of(2 * i + 1, sb)
        bend(2 * i, sa)
        if 2 * i + 2 < steps:
            dact_of(2 * i + 2, sa)
        bend(2 * i + 1, sb)
        if i == steps // 2 - 1:
            for j, w in enumerate((wq, wk, wv)):
                load(j, w, wout.at[pl.ds(j * width, width)], load_sem.at[1 + j])
            turned[...] = n1[...].T

    def inner_slab(s):
        c = plan[s][1]
        for h in range(2):
            at = ((s - 3) * 2 + h) * c
            by_owner(s, h, lambda left: mat(left, dpre[:, at : at + c]))
        start(s, 0)

    def dn1_part(c):
        cols = slice(c * 256, (c + 1) * 256)
        acc[:, cols] += times_trans(dpre[...], wi[cols, :])

    def norm_one_back():
        for p in range(pairs // 2):
            for e in range(2):
                prob_back(wi, p, 0, e).start()
                prob_back(dpre, p, pairs // 2, e).start()

        def step(r, sums):
            rows = chunk(r)
            dn1, hat = acc[rows, :], hat1[rows, :]
            dh1 = norm_back(dn1, hat, r1[rows, 0:1], gain)
            acc[rows, :] = dh1
            low_dh1 = dh1.astype(BF16)
            dattn[rows, :] = low_dh1
            return (sums[0] + down(dn1 * hat), sums[1] + down(dn1), sums[2] + down(low_dh1.astype(F32)))

        a, b, c = lax.fori_loop(0, total // NORM_CHUNK, step, (zero, zero, zero))
        vec[3:4, 0:width] = a
        vec[4:5, 0:width] = b
        vec[2:3, 0:width] = c

    half_width = width // 2

    def out_slab():
        turned[...] = ctx[...].T
        for h in range(2):
            by_owner(6, h, lambda left: mat(left, dattn[:, h * half_width : (h + 1) * half_width]))
        start(6, 0)
        for c in range(width // 256):
            cols = slice(c * 256, (c + 1) * 256)
            dctx[:, cols] = times_trans(dattn[...], wo[cols, :]).astype(BF16)

    def head_back(head):
        p, e = head // 2, head % 2
        if head == 0:
            loads["qkv"].wait()
        kept, base = (wi, 0) if p < pairs // 2 else (dpre, pairs // 2)
        prob_back(kept, p - base, base, e).wait()
        qp, kp, vp, dop = act[:, lanes(0, p)], act[:, lanes(1, p)], act[:, lanes(2, p)], dctx[:, lanes(0, p)]
        dpe, dse = (sa, slope.at[:, 0:total]) if e == 0 else (sb, slope.at[:, total : 2 * total])
        mine_only = (lambda v: jnp.where(first, v, 0)) if e == 0 else (lambda v: jnp.where(first, 0, v))
        dpe[...] = times_trans(mine_only(dop).astype(BF16), vp)
        here = slice(e * HEAD_DIM, (e + 1) * HEAD_DIM)
        turned_q, turned_k, turned_do = qp.T[here], kp.T[here], dop.T[here]
        delta = jnp.sum(mine_only(dop.astype(F32) * ctx[:, lanes(0, p)].astype(F32)), axis=1, keepdims=True)
        for r in range(total // ROW_CHUNK):
            rows = slice(r * ROW_CHUNK, (r + 1) * ROW_CHUNK)
            dse[rows, :] = (kept[rows, prob_lanes(p - base, e)].astype(F32) * (dpe[rows, :] - delta[rows])).astype(BF16)
        there = pl.ds(head * HEAD_DIM, HEAD_DIM)
        dvt[there, :] = mat(turned_do, kept[0:total, prob_lanes(p - base, e)]).astype(BF16)
        dqt[there, :] = (times_trans(turned_k, dse[...]) * HEAD_DIM ** (-0.5)).astype(BF16)
        dkt[there, :] = mat(turned_q, dse[...]).astype(BF16)

    def head_slab(s, right):
        if s == 7:
            turned[...] = x[...].T
        pending[s - 4, 0].wait_send()
        sent.add((s - 4, 0))
        for h in range(2):
            by_owner(s, h, lambda left: times_trans(left, right[h * half_width : (h + 1) * half_width, :]))
        start(s, 0)

    def vectors():
        ones = jnp.ones((8, total), BF16)
        vec[0:1, 0:width] = times_trans(ones, dqt[...])[0:1]
        vec[1:2, 0:width] = times_trans(ones, dvt[...])[0:1]
        for o in range(SPAN):
            tmp[...] = jnp.zeros_like(tmp)
            tmp[0:8, 0:rows_of] = vec[0:8, o * rows_of : (o + 1) * rows_of]
            tmp[8:9, :] = vec[8:9, o * ff_rows : o * ff_rows + 128]
            put(10, o, o % 2, 0, tmp[...].astype(BF16))
            tmp[...] = jnp.zeros_like(tmp)
            tmp[8:9, 0 : ff_rows - 128] = vec[8:9, o * ff_rows + 128 : (o + 1) * ff_rows]
            put(10, o, o % 2, 1, tmp[...].astype(BF16))
        start(10, 0)

    def input_part(c):
        if c == 0:
            for i in range(3):
                loads[i].wait()
        cols = slice(c * 256, (c + 1) * 256)
        dxt = sum(
            mat(wout[i * width + c * 256 : i * width + (c + 1) * 256, :], d[...]) for i, d in enumerate((dqt, dkt, dvt))
        )
        dx = (dxt.T + acc[:, cols]).astype(BF16)
        dx_out[0, :, cols] = dx[:span]
        db[0:span, cols] = dx[span:]
        if c == width // 256 - 1:
            sides.append(side(4, db.at[mine], dx_out.at[1]))

    pieces = [outer_slabs]
    pieces += [functools.partial(backward, i) for i in range(steps // 2)]
    pieces += [functools.partial(inner_slab, s) for s in (3, 4, 5)]
    pieces += [functools.partial(dn1_part, c) for c in range(width // 256)]
    pieces += [norm_one_back, out_slab]
    pieces += [functools.partial(head_back, h) for h in range(2 * pairs)]
    pieces += [functools.partial(head_slab, s, r) for s, r in ((7, dqt), (8, dkt), (9, dvt))]
    pieces += [vectors] + [functools.partial(input_part, c) for c in range(width // 256)]
    for event in EVENTS:
        if event < 0:
            pieces.pop(0)()
        else:
            advance(event)
    for wait in (*x_swaps, cot_swap):
        wait.wait_send()
    for wait in sides:
        wait.wait()
    for key, copy in pending.items():
        if key not in sent:
            copy.wait_send()


def run_layer(plan, low, args):
    count = len(plan)
    tokens = args[0]
    _, span, width = tokens.shape
    total = 2 * span
    ff = args[7].shape[1]
    hbm = pl.BlockSpec(memory_space=pl.ANY)
    vm = pl.BlockSpec(memory_space=pltpu.VMEM)
    smem = pl.BlockSpec(memory_space=pltpu.SMEM)
    low_shape, tall = pltpu.VMEM((total, width), BF16), pltpu.VMEM((total, ff), BF16)
    turned = pltpu.VMEM((width, total), BF16)
    own = [s for s in range(count) if s not in (7, 8, 9)]
    return pl.pallas_call(
        functools.partial(layer_kernel, plan, low),
        out_shape=[jax.ShapeDtypeStruct((2, r, c), BF16) for r, c, _ in plan]
        + [
            jax.ShapeDtypeStruct((2, span, width), BF16),
            jax.ShapeDtypeStruct((2, span, width), BF16),
            jax.ShapeDtypeStruct((width // HEAD_DIM, total, total), BF16),
            jax.ShapeDtypeStruct((total, 3 * width), BF16),
        ],
        in_specs=[hbm, smem] + [hbm] * 7 + [vm] * 9,
        out_specs=[vm] * (count + 2) + [hbm] * 2,
        scratch_shapes=[pltpu.VMEM((32 * plan[s][0], plan[s][1]), BF16) for s in own]
        + [pltpu.VMEM((32 * r, c), BF16) for r, c, _ in plan]
        + [low_shape] * 5
        + [tall] * 3
        + [
            pltpu.VMEM((width, ff), BF16),
            pltpu.VMEM((ff, width), BF16),
            pltpu.VMEM((width, width), BF16),
            pltpu.VMEM((total, width), F32),
            pltpu.VMEM((total, width), F32),
            pltpu.VMEM((total, 128), F32),
            pltpu.VMEM((total, total), F32),
            pltpu.VMEM((total, total), F32),
            turned, turned, turned, turned,
            pltpu.VMEM((16, 128), F32),
            pltpu.VMEM((16, ff), F32),
            pltpu.SemaphoreType.DMA((9,)),
            pltpu.SemaphoreType.DMA((2, width // HEAD_DIM)),
            pltpu.SemaphoreType.DMA((count, 6)),
            pltpu.SemaphoreType.DMA((count, 6)),
            pltpu.SemaphoreType.DMA((2, 5)),
        ],
        compiler_params=pltpu.CompilerParams(
            collective_id=0, has_side_effects=True, vmem_limit_bytes=VMEM_LIMIT
        ),
        name="layer",
    )(*args)


def finish_kernel(rows, ff_rows, *refs):
    y = lax.axis_index("blk")
    out_in, dx_in = refs[:2]
    res = refs[2:13]
    (out_ref, dx_full, wq, bq, wk, wv, bv, wo, bo, gain, shift, wi, bi, wout, bout, fgain, fshift) = refs[13:]
    out_ref[y] = out_in[0]
    out_ref[1 - y] = out_in[1]
    dx_full[y] = dx_in[0].astype(F32)
    dx_full[1 - y] = dx_in[1].astype(F32)
    col = res[0].shape[2]
    for s in range(3):
        for h in range(2):
            at = (2 * s + h) * col
            wout[:, at : at + col] = res[s][h].astype(F32)
    wide = res[3].shape[2]
    for s in range(3):
        for h in range(2):
            at = (2 * s + h) * wide
            wi[:, at : at + wide] = res[3 + s][h].astype(F32)
    wide = res[6].shape[2]
    for s, ref in ((6, wo), (7, wq), (8, wk), (9, wv)):
        for h in range(2):
            ref[:, h * wide : (h + 1) * wide] = res[s][h].astype(F32)
    vec = res[10][0].astype(F32)
    rest = res[10][1].astype(F32)
    for i, ref in enumerate((bq, bv, bo, gain, shift, bout, fgain, fshift)):
        ref[...] = vec[i, 0:rows]
    bi[0:128] = vec[8, :]
    bi[128:ff_rows] = rest[8, 0 : ff_rows - 128]


def finish(out, dx, res, width, ff):
    rows, ff_rows = width // SPAN, ff // SPAN
    square, line = (rows, width), (rows,)
    shapes = (
        square, line, square, square, line, square, line, line, line,
        (rows, ff), (ff_rows,), (ff_rows, width), line, line, line,
    )
    vm = pl.BlockSpec(memory_space=pltpu.VMEM)
    return pl.pallas_call(
        functools.partial(finish_kernel, rows, ff_rows),
        out_shape=[jax.ShapeDtypeStruct(dx.shape, BF16), jax.ShapeDtypeStruct(dx.shape, F32)]
        + [jax.ShapeDtypeStruct(s, F32) for s in shapes],
        in_specs=[vm] * (2 + len(res)),
        out_specs=[vm] * (2 + len(shapes)),
        name="finish",
    )(out, dx, *res)


def per_device(
    dp_size,
    tokens,
    lengths,
    query_weight,
    query_bias,
    key_weight,
    value_weight,
    value_bias,
    out_weight,
    out_bias,
    norm_gain,
    norm_shift,
    inner_weight,
    inner_bias,
    outer_weight,
    outer_bias,
    final_gain,
    final_shift,
    cotangent,
):
    width, ff = inner_weight.shape
    plan = slab_plan(width, ff)
    low = dp_size // SPAN
    *res, dx, out, _, _ = run_layer(
        plan, low,
        (
            tokens, lengths, cotangent, query_weight, key_weight, value_weight, out_weight, inner_weight, outer_weight,
            query_bias, value_bias, out_bias, norm_gain, norm_shift, inner_bias, outer_bias, final_gain, final_shift,
        ),
    )
    layer_out, input_grad, *grads = finish(out, dx, res, width, ff)
    if low > 1:
        groups = [[t * low + i for i in range(low)] for t in range(SPAN)]
        grads = [
            lax.psum_scatter(g, "dp", scatter_dimension=0, axis_index_groups=groups, tiled=True)
            for g in grads
        ]
    return (layer_out, input_grad, *grads)


def solution(mesh):
    rows3 = P("dp", "blk", None)
    grad2, grad1 = P("dp", None), P("dp")
    return jax.shard_map(
        functools.partial(per_device, mesh.shape["dp"]),
        mesh=mesh,
        in_specs=(rows3, P("dp")) + (P(),) * 15 + (rows3,),
        out_specs=(
            rows3, rows3, grad2, grad1, grad2, grad2, grad1, grad2, grad1,
            grad1, grad1, grad2, grad1, grad2, grad1, grad1, grad1,
        ),
        check_vma=False,
    )
```

```python
import functools

import jax
import jax.numpy as jnp
from jax import lax
from jax.experimental import pallas as pl
from jax.experimental.pallas import tpu as pltpu
from jax.sharding import PartitionSpec as P

HEADS = 12
HEAD_DIM = 64
HEAD_PAIR = 2 * HEAD_DIM
ROW_CHUNK = 64
NORM_CHUNK = 256
EPS = 1e-12
HALF_ROOT = 0.7071067811865476
INV_ROOT_TAU = 0.3989422804014327
MESH = pl.DeviceIdType.MESH
BF16 = jnp.bfloat16
F32 = jnp.float32

ORDERS = {
    "A": ("c", "x", "y", "zl", "zh"),
    "B": ("c", "y", "zl", "x", "zh"),
    "C": ("c", "zl", "x", "y", "zh"),
    "E": ("c", "x", "zl", "y", "zh"),
    "F": ("c", "zl", "y", "x", "zh"),
    "G": ("c", "y", "x", "zl", "zh"),
    "H": ("c", "x", "zl", "zh", "y"),
    "I": ("c", "zl", "zh", "x", "y"),
    "L": ("c", "zl", "x", "zh", "y"),
    "M": ("c", "y", "zl", "zh", "x"),
}
SLAB_ORDERS = ("EI", "HF", "MG", "AB", "CH", "AG", "HA", "BC", "AE", "LE", "AE")
EVENTS = (
    -1, -1, -1, 0, -1, 1, 2, -1, -1, -1, 0, 3, -1, 4, 5, -1, -1, 1, -1, -1,
    2, 0, -1, 6, 4, -1, 3, -1, -1, 2, -1, 0, -1, 5, 3, -1, 7, 1, 8, 2,
    0, -1, 9, -1, 10, 6, -1, -1, 5, 7, 4, 0, 3, 1, 6, 2, 5, 8, 4, 1,
    2, 9, 10, 3, 6, 7, 8, 5, 1, 9, 10, 4, 3, 7, 6, 8, 5, 9, 10, 4,
    7, 6, 8, 7, 9, 10, 8, 9, 10,
)
BIT_OF = {"c": 1, "x": 2, "zl": 4, "zh": 8}
SPAN = 16
OFFSETS = (0, 16, 24, 28, 30, 31)
VMEM_LIMIT = 67_043_328


def contract_rows(left_mat, right_mat):
    return lax.dot_general(
        left_mat, right_mat, (((0,), (0,)), ((), ())), preferred_element_type=F32
    )


def times_trans(left_mat, right_mat):
    return lax.dot_general(
        left_mat, right_mat, (((1,), (1,)), ((), ())), preferred_element_type=F32
    )


def mat(left_mat, right_mat):
    return jnp.dot(left_mat, right_mat, preferred_element_type=F32)


def norm_rows(hidden, gain_vec, shift_vec):
    row_mean = jnp.mean(hidden, axis=-1, keepdims=True)
    centred = hidden - row_mean
    reciprocal = lax.rsqrt(jnp.mean(centred * centred, axis=-1, keepdims=True) + EPS)
    normed = centred * reciprocal
    return (normed * gain_vec + shift_vec, normed, reciprocal)


def norm_back(grad_in, normed, reciprocal, gain_vec):
    scaled = grad_in * gain_vec
    return reciprocal * (
        scaled
        - jnp.mean(scaled, axis=-1, keepdims=True)
        - normed * jnp.mean(scaled * normed, axis=-1, keepdims=True)
    )


def row_vec(ref):
    return ref[...].astype(F32).reshape(1, -1)


def block_index(owner, half, order):
    place = 0
    for dim in order:
        bit = half if dim == "y" else (owner // BIT_OF[dim]) % 2
        place = place * 2 + bit
    return place


def slab_plan(width, ff):
    rows, ff_rows = width // SPAN, ff // SPAN
    sizes = [(ff_rows, width // 6)] * 3 + [(rows, ff // 6)] * 3 + [(rows, width // 2)] * 4 + [(16, 128)]
    return tuple((r, c, (ORDERS[o[0]], ORDERS[o[1]])) for (r, c), o in zip(sizes, SLAB_ORDERS))


def layer_kernel(plan, low, *refs):
    count = len(plan)
    (tokens, lengths, cot_in, wq, wk, wv, wo_in, wi_in, wout_in, bq, bv, bo, gain_in, shift_in, bi, bout_in, fgain_in, fshift_in) = refs[:18]
    res, refs = refs[18 : 18 + count], refs[18 + count :]
    dx_out, out_all, prob_hbm, qkv_hbm = refs[:4]
    refs = refs[4:]
    bufs, recvs, refs = refs[: count - 3], refs[count - 3 : 2 * count - 3], refs[2 * count - 3 :]
    (x, cot, ctx, db, n1, act, dpre, slope, wi, wout, wo, hat1, acc, r1, sa, sb) = refs[:16]
    (turned, dqt, dkt, dvt, tmp, vec, load_sem, prob_sem, send_sem, recv_sem, side_sem) = refs[16:]
    dattn, dctx = n1, db
    total, width = x.shape
    span = total // 2
    ff = act.shape[1]
    pairs = width // HEAD_PAIR
    wide = sa.shape[1]
    bufs = list(bufs[:7]) + [bufs[s].at[:, 0 : width // 2] for s in (3, 4, 5)] + [bufs[7]]

    dp = lax.axis_index("dp")
    y = lax.axis_index("blk")
    top = dp // low
    bits = {dim: (top // b) % 2 for dim, b in BIT_OF.items()}
    bits["y"] = y
    partner = {dim: (dp + (1 - 2 * bits[dim]) * (b * low), y) for dim, b in BIT_OF.items()}
    partner["y"] = (dp, 1 - y)

    loads = {}

    def load(name, src, dst, sem):
        loads[name] = pltpu.make_async_copy(src, dst, sem)
        loads[name].start()

    mine, theirs = pl.ds(0, span), pl.ds(span, span)
    load("x", tokens.at[y], x.at[mine], load_sem.at[0])
    for i, w in enumerate((wq, wk, wv)):
        load(i, w, wout.at[pl.ds(i * width, width)], load_sem.at[1 + i])
    load("wo", wo_in, wo, load_sem.at[4])
    load("cot", cot_in.at[y], cot.at[mine], load_sem.at[5])
    load("wi", wi_in, wi, load_sem.at[6])

    barrier = pltpu.get_barrier_semaphore()
    for where in partner.values():
        pl.semaphore_signal(barrier, inc=1, device_id=where, device_id_type=MESH)
    pl.semaphore_wait(barrier, len(partner))

    def remote(src, dst, send, recv, where):
        copy = pltpu.make_async_remote_copy(
            src_ref=src, dst_ref=dst, send_sem=send, recv_sem=recv, device_id=where, device_id_type=MESH
        )
        copy.start()
        return copy

    def side(i, src, dst):
        return remote(src, dst, side_sem.at[0, i], side_sem.at[1, i], partner["y"])

    part = span // 2
    x_swaps = [
        side(i, tokens.at[1 - y, pl.ds(i * part, part)], x.at[pl.ds(span + i * part, part)]) for i in range(2)
    ]
    cot_swap = side(2, cot_in.at[1 - y], cot.at[theirs])

    def down(v):
        return jnp.sum(v, axis=0, keepdims=True)

    loads["x"].wait()
    for half in range(3):
        rows = slice(0, span) if half == 0 else slice(span + (half - 1) * part, span + half * part)
        if half > 0:
            x_swaps[half - 1].wait_recv()
        for i, b_ref in enumerate((bq, None, bv)):
            if half == 0:
                loads[i].wait()
            bias = None if b_ref is None else row_vec(b_ref)
            for c in range(width // 256):
                cols = slice(c * 256, (c + 1) * 256)
                got = mat(x[rows, :], wout[i * width : (i + 1) * width, cols])
                if bias is not None:
                    got = got + bias[:, cols]
                got = got.astype(BF16)
                if i == 0:
                    got = got * jnp.bfloat16(HEAD_DIM ** (-0.5))
                act[rows, i * width + c * 256 : i * width + (c + 1) * 256] = got
    load("wout", wout_in, wout, load_sem.at[7])
    load("qkv", act.at[:, pl.ds(0, 3 * width)], qkv_hbm, load_sem.at[8])

    length = lengths[y]
    at = lax.broadcasted_iota(jnp.int32, (1, total), 1)
    place = jnp.where(at < span, at + y * span, at - span + (1 - y) * span)
    mask = jnp.where(place < length, 0.0, -1e30).astype(F32)
    first = lax.broadcasted_iota(jnp.int32, (1, HEAD_PAIR), 1) < HEAD_DIM

    def lanes(i, p):
        return pl.ds(pl.multiple_of(i * width + p * HEAD_PAIR, HEAD_PAIR), HEAD_PAIR)

    def prob_lanes(p, e):
        return pl.ds(pl.multiple_of((2 * p + e) * total, 128), total)

    def prob_copy(kept, p, base, e):
        return pltpu.make_async_copy(
            kept.at[0:total, prob_lanes(p, e)], prob_hbm.at[2 * (p + base) + e], prob_sem.at[0, 2 * (p + base) + e]
        )

    def prob_back(kept, p, base, e):
        return pltpu.make_async_copy(
            prob_hbm.at[2 * (p + base) + e], kept.at[0:total, prob_lanes(p, e)], prob_sem.at[1, 2 * (p + base) + e]
        )

    def scores(p, e, into):
        qp, kp = act[:, lanes(0, p)], act[:, lanes(1, p)]
        keep = jnp.where(first, qp, 0) if e == 0 else jnp.where(first, 0, qp)
        into[...] = times_trans(keep.astype(BF16), kp)

    def soften(kept, p, base, e, s):
        for r in range(total // ROW_CHUNK):
            rows = slice(r * ROW_CHUNK, (r + 1) * ROW_CHUNK)
            raw = s[rows, :] + mask
            expo = jnp.exp(raw - jnp.max(raw, axis=1, keepdims=True))
            scale = 1.0 / jnp.sum(expo, axis=1, keepdims=True)
            kept[rows, prob_lanes(p, e)] = (expo * scale).astype(BF16)
        prob_copy(kept, p, base, e).start()

    scores(0, 0, sa)
    for p in range(pairs):
        kept, base = (slope, 0) if p < pairs // 2 else (dpre, pairs // 2)
        vp = act[:, lanes(2, p)]
        scores(p, 1, sb)
        soften(kept, p - base, base, 0, sa)
        if p + 1 < pairs:
            scores(p + 1, 0, sa)
        even = mat(kept[0:total, prob_lanes(p - base, 0)], vp)
        soften(kept, p - base, base, 1, sb)
        odd = mat(kept[0:total, prob_lanes(p - base, 1)], vp)
        ctx[:, lanes(0, p)] = jnp.where(first, even, odd).astype(BF16)

    loads["wo"].wait()
    acc[...] = mat(ctx[...], wo[...])
    bo, gain, shift, bout = row_vec(bo), row_vec(gain_in), row_vec(shift_in), row_vec(bout_in)
    fgain, fshift = row_vec(fgain_in), row_vec(fshift_in)
    vec[9:10, :] = row_vec(bi)

    def chunk(r):
        return pl.ds(pl.multiple_of(r * NORM_CHUNK, NORM_CHUNK), NORM_CHUNK)

    def norm_one(r, carry):
        rows = chunk(r)
        normed, hat, recip = norm_rows(x[rows, :].astype(F32) + acc[rows, :] + bo, gain, shift)
        hat1[rows, :] = hat
        r1[rows, :] = jnp.broadcast_to(recip, (NORM_CHUNK, 128))
        n1[rows, :] = normed.astype(BF16)
        acc[rows, :] = normed + bout
        return carry

    lax.fori_loop(0, total // NORM_CHUNK, norm_one, 0)

    for p in range(pairs // 2):
        for e in range(2):
            prob_copy(slope, p, 0, e).wait()
    loads["qkv"].wait()
    loads["wi"].wait()
    loads["wout"].wait()

    def span_of(j):
        return pl.ds(pl.multiple_of(j * wide, wide), wide)

    def pre_of(j, into):
        into[...] = mat(n1[...], wi[:, span_of(j)])

    def activate(j, pre):
        bias = vec[9:10, span_of(j)]
        for r in range(total // ROW_CHUNK):
            rows = slice(r * ROW_CHUNK, (r + 1) * ROW_CHUNK)
            u = pre[rows, :] + bias
            half = 0.5 * (1.0 + lax.erf(u * HALF_ROOT))
            act[rows, span_of(j)] = (u * half).astype(BF16)
            slope[rows, span_of(j)] = (half + u * jnp.exp(-0.5 * u * u) * INV_ROOT_TAU).astype(BF16)

    def second(j):
        acc[...] += mat(act[:, span_of(j)], wout[span_of(j), :])

    steps = ff // wide
    pre_of(0, sa)

    for i in range(steps // 2):
        pre_of(2 * i + 1, sb)
        activate(2 * i, sa)
        if i > 0:
            second(2 * i - 1)
        if i + 1 < steps // 2:
            pre_of(2 * i + 2, sa)
        activate(2 * i + 1, sb)
        second(2 * i)
    second(steps - 1)

    loads["cot"].wait()
    cot_swap.wait_recv()
    zero = jnp.zeros((1, width), F32)

    def norm_two(r, sums):
        rows = chunk(r)
        out, hat2, recip2 = norm_rows(acc[rows, :], fgain, fshift)
        g = cot[rows, :].astype(F32)
        cot[rows, :] = out.astype(BF16)
        dh2 = norm_back(g, hat2, recip2, fgain)
        acc[rows, :] = dh2
        low_dh2 = dh2.astype(BF16)
        db[rows, :] = low_dh2
        return (sums[0] + down(g * hat2), sums[1] + down(g), sums[2] + down(low_dh2.astype(F32)))

    fgain_sum, fshift_sum, bout_sum = lax.fori_loop(0, total // NORM_CHUNK, norm_two, (zero, zero, zero))
    vec[5:6, 0:width] = bout_sum
    vec[6:7, 0:width] = fgain_sum
    vec[7:8, 0:width] = fshift_sum
    out_all[0] = cot[0:span, :]

    pending = {}
    stage_of = {}
    sent = set()

    def blocks(s, base, n):
        size = plan[s][0]
        return pl.ds(pl.multiple_of(base * size, 16), n * size)

    def step_of(s, i):
        even, odd = (plan[s][2][c][i] for c in range(2))
        if even == odd:
            return bits[even], partner[even]
        own = bits["c"]
        return (
            bits[even] + own * (bits[odd] - bits[even]),
            tuple(a + own * (b - a) for a, b in zip(partner[even], partner[odd])),
        )

    def start(s, i):
        if i == 5:
            src, dst, where = recvs[s].at[blocks(s, 30, 1)], recvs[s].at[blocks(s, 31, 1)], partner["y"]
        else:
            half = 16 >> i
            bit, where = step_of(s, i)
            src_ref, base = (bufs[s], 0) if i == 0 else (recvs[s], OFFSETS[i - 1])
            src = src_ref.at[blocks(s, base + (1 - bit) * half, half)]
            dst = recvs[s].at[blocks(s, OFFSETS[i], half)]
        pending[s, i] = remote(src, dst, send_sem.at[s, i], recv_sem.at[s, i], where)
        stage_of[s] = i

    def advance(s):
        i = stage_of[s]
        pending[s, i].wait_recv()
        if i == 5:
            res[s][y] = recvs[s][blocks(s, 30, 1)]
            res[s][1 - y] = recvs[s][blocks(s, 31, 1)]
            stage_of[s] = 6
            return
        half = 16 >> i
        src_ref, base = (bufs[s], 0) if i == 0 else (recvs[s], OFFSETS[i - 1])
        mine = base + step_of(s, i)[0] * half

        def add(j, carry):
            got = blocks(s, OFFSETS[i] + j, 1)
            recvs[s][got] = recvs[s][got] + src_ref[blocks(s, mine + j, 1)]
            return carry

        lax.fori_loop(0, half, add, 0)
        start(s, i + 1)

    def put(s, owner, core, h, value):
        bufs[s][blocks(s, block_index(owner, h, plan[s][2][core]), 1)] = value

    rows_of, ff_rows, col = plan[3][0], plan[0][0], plan[0][1]

    two = 2 * ff_rows

    def turn_outer(t, slot):
        turned[slot * two : (slot + 1) * two, :] = act[:, pl.ds(pl.multiple_of(t * two, 128), two)].T

    def outer_rows(t, slot):
        part = mat(turned[slot * two : (slot + 1) * two, :], db[...]).astype(BF16)
        for e in range(2):
            for s in range(3):
                for h in range(2):
                    at = (2 * s + h) * col
                    put(s, 2 * t + e, e, h, part[e * ff_rows : (e + 1) * ff_rows, at : at + col])

    def outer_four(i, carry):
        turn_outer(2 * i + 1, 1)
        outer_rows(2 * i, 0)
        turn_outer(lax.rem(2 * i + 2, SPAN // 2), 0)
        outer_rows(2 * i + 1, 1)
        return carry

    def by_owner(s, h, product):
        tall = 8 * rows_of

        def some(part, carry):
            block = product(turned[pl.ds(pl.multiple_of(part * tall, tall), tall), :]).astype(BF16)
            for o in range(8):
                put(s, part * 8 + o, o % 2, h, block[o * rows_of : (o + 1) * rows_of])
            return carry

        lax.fori_loop(0, 2, some, 0)

    sides = []

    def outer_slabs():
        turn_outer(0, 0)
        lax.fori_loop(0, SPAN // 4, outer_four, 0)
        for s in range(3):
            start(s, 0)
        sides.append(side(3, cot.at[theirs], out_all.at[1]))
        load("qkv", qkv_hbm, act.at[:, pl.ds(0, 3 * width)], load_sem.at[8])
        dact_of(0, sa)

    def dact_of(j, into):
        into[...] = times_trans(db[...], wout[span_of(j), :])

    def bend(j, dact):
        sums = jnp.zeros((1, wide), F32)
        for r in range(total // ROW_CHUNK):
            rows = slice(r * ROW_CHUNK, (r + 1) * ROW_CHUNK)
            value = (dact[rows, :] * slope[rows, span_of(j)].astype(F32)).astype(BF16)
            dpre[rows, span_of(j)] = value
            sums += down(value.astype(F32))
        vec[8:9, span_of(j)] = sums

    def backward(i):
        if i == 0:
            for p in range(pairs // 2):
                for e in range(2):
                    prob_copy(dpre, p, pairs // 2, e).wait()
        dact_of(2 * i + 1, sb)
        bend(2 * i, sa)
        if 2 * i + 2 < steps:
            dact_of(2 * i + 2, sa)
        bend(2 * i + 1, sb)
        if i == steps // 2 - 1:
            for j, w in enumerate((wq, wk, wv)):
                load(j, w, wout.at[pl.ds(j * width, width)], load_sem.at[1 + j])
            turned[...] = n1[...].T

    def inner_slab(s):
        c = plan[s][1]
        for h in range(2):
            at = ((s - 3) * 2 + h) * c
            by_owner(s, h, lambda left: mat(left, dpre[:, at : at + c]))
        start(s, 0)

    def dn1_part(c):
        cols = slice(c * 256, (c + 1) * 256)
        acc[:, cols] += times_trans(dpre[...], wi[cols, :])

    def norm_one_back():
        for p in range(pairs // 2):
            for e in range(2):
                prob_back(wi, p, 0, e).start()
                prob_back(dpre, p, pairs // 2, e).start()

        def step(r, sums):
            rows = chunk(r)
            dn1, hat = acc[rows, :], hat1[rows, :]
            dh1 = norm_back(dn1, hat, r1[rows, 0:1], gain)
            acc[rows, :] = dh1
            low_dh1 = dh1.astype(BF16)
            dattn[rows, :] = low_dh1
            return (sums[0] + down(dn1 * hat), sums[1] + down(dn1), sums[2] + down(low_dh1.astype(F32)))

        a, b, c = lax.fori_loop(0, total // NORM_CHUNK, step, (zero, zero, zero))
        vec[3:4, 0:width] = a
        vec[4:5, 0:width] = b
        vec[2:3, 0:width] = c

    half_width = width // 2

    def out_slab():
        turned[...] = ctx[...].T
        for h in range(2):
            by_owner(6, h, lambda left: mat(left, dattn[:, h * half_width : (h + 1) * half_width]))
        start(6, 0)
        for c in range(width // 256):
            cols = slice(c * 256, (c + 1) * 256)
            dctx[:, cols] = times_trans(dattn[...], wo[cols, :]).astype(BF16)

    def head_back(kept, base, p, e):
        prob_back(kept, p, base, e).wait()
        pair = p + base
        qp, kp, vp, dop = act[:, lanes(0, pair)], act[:, lanes(1, pair)], act[:, lanes(2, pair)], dctx[:, lanes(0, pair)]
        dpe, dse = (sa, slope.at[:, 0:total]) if e == 0 else (sb, slope.at[:, total : 2 * total])
        mine_only = (lambda v: jnp.where(first, v, 0)) if e == 0 else (lambda v: jnp.where(first, 0, v))
        dpe[...] = times_trans(mine_only(dop).astype(BF16), vp)
        here = slice(e * HEAD_DIM, (e + 1) * HEAD_DIM)
        turned_q, turned_k, turned_do = qp.T[here], kp.T[here], dop.T[here]
        delta = jnp.sum(mine_only(dop.astype(F32) * ctx[:, lanes(0, pair)].astype(F32)), axis=1, keepdims=True)
        for r in range(total // ROW_CHUNK):
            rows = slice(r * ROW_CHUNK, (r + 1) * ROW_CHUNK)
            dse[rows, :] = (kept[rows, prob_lanes(p, e)].astype(F32) * (dpe[rows, :] - delta[rows])).astype(BF16)
        there = pl.ds(pl.multiple_of((2 * pair + e) * HEAD_DIM, HEAD_DIM), HEAD_DIM)
        dvt[there, :] = mat(turned_do, kept[0:total, prob_lanes(p, e)]).astype(BF16)
        dqt[there, :] = (times_trans(turned_k, dse[...]) * HEAD_DIM ** (-0.5)).astype(BF16)
        dkt[there, :] = mat(turned_q, dse[...]).astype(BF16)

    def pairs_back(low_pair, high_pair):
        if low_pair == 0:
            loads["qkv"].wait()
        kept, base = (wi, 0) if low_pair < pairs // 2 else (dpre, pairs // 2)

        def pair_back(p, carry):
            head_back(kept, base, p, 0)
            head_back(kept, base, p, 1)
            return carry

        lax.fori_loop(low_pair - base, high_pair - base, pair_back, 0)

    def head_slab(s, right):
        if s == 7:
            turned[...] = x[...].T
        pending[s - 4, 0].wait_send()
        sent.add((s - 4, 0))
        for h in range(2):
            by_owner(s, h, lambda left: times_trans(left, right[h * half_width : (h + 1) * half_width, :]))
        start(s, 0)

    def vectors():
        ones = jnp.ones((8, total), BF16)
        vec[0:1, 0:width] = times_trans(ones, dqt[...])[0:1]
        vec[1:2, 0:width] = times_trans(ones, dvt[...])[0:1]
        for o in range(SPAN):
            tmp[...] = jnp.zeros_like(tmp)
            tmp[0:8, 0:rows_of] = vec[0:8, o * rows_of : (o + 1) * rows_of]
            tmp[8:9, :] = vec[8:9, o * ff_rows : o * ff_rows + 128]
            put(10, o, o % 2, 0, tmp[...].astype(BF16))
            tmp[...] = jnp.zeros_like(tmp)
            tmp[8:9, 0 : ff_rows - 128] = vec[8:9, o * ff_rows + 128 : (o + 1) * ff_rows]
            put(10, o, o % 2, 1, tmp[...].astype(BF16))
        start(10, 0)

    def input_part(c):
        if c == 0:
            for i in range(3):
                loads[i].wait()
        cols = slice(c * 256, (c + 1) * 256)
        dxt = sum(
            mat(wout[i * width + c * 256 : i * width + (c + 1) * 256, :], d[...]) for i, d in enumerate((dqt, dkt, dvt))
        )
        dx = (dxt.T + acc[:, cols]).astype(BF16)
        dx_out[0, :, cols] = dx[:span]
        db[0:span, cols] = dx[span:]
        if c == width // 256 - 1:
            sides.append(side(4, db.at[mine], dx_out.at[1]))

    pieces = [outer_slabs]
    pieces += [functools.partial(backward, i) for i in range(steps // 2)]
    pieces += [functools.partial(inner_slab, s) for s in (3, 4, 5)]
    pieces += [functools.partial(dn1_part, c) for c in range(width // 256)]
    pieces += [norm_one_back, out_slab]
    half_pairs = pairs // 2
    for at in (0, half_pairs):
        cut = at + half_pairs // 2 + 1
        pieces += [functools.partial(pairs_back, at, cut), functools.partial(pairs_back, cut, at + half_pairs)]
    pieces += [functools.partial(head_slab, s, r) for s, r in ((7, dqt), (8, dkt), (9, dvt))]
    pieces += [vectors] + [functools.partial(input_part, c) for c in range(width // 256)]
    for event in EVENTS:
        if event < 0:
            pieces.pop(0)()
        else:
            advance(event)
    for wait in (*x_swaps, cot_swap):
        wait.wait_send()
    for wait in sides:
        wait.wait()
    for key, copy in pending.items():
        if key not in sent:
            copy.wait_send()


def run_layer(plan, low, args):
    count = len(plan)
    tokens = args[0]
    _, span, width = tokens.shape
    total = 2 * span
    ff = args[7].shape[1]
    hbm = pl.BlockSpec(memory_space=pl.ANY)
    vm = pl.BlockSpec(memory_space=pltpu.VMEM)
    smem = pl.BlockSpec(memory_space=pltpu.SMEM)
    low_shape, tall = pltpu.VMEM((total, width), BF16), pltpu.VMEM((total, ff), BF16)
    turned = pltpu.VMEM((width, total), BF16)
    own = [s for s in range(count) if s not in (7, 8, 9)]
    return pl.pallas_call(
        functools.partial(layer_kernel, plan, low),
        out_shape=[jax.ShapeDtypeStruct((2, r, c), BF16) for r, c, _ in plan]
        + [
            jax.ShapeDtypeStruct((2, span, width), BF16),
            jax.ShapeDtypeStruct((2, span, width), BF16),
            jax.ShapeDtypeStruct((width // HEAD_DIM, total, total), BF16),
            jax.ShapeDtypeStruct((total, 3 * width), BF16),
        ],
        in_specs=[hbm, smem] + [hbm] * 7 + [vm] * 9,
        out_specs=[vm] * (count + 2) + [hbm] * 2,
        scratch_shapes=[pltpu.VMEM((32 * plan[s][0], plan[s][1]), BF16) for s in own]
        + [pltpu.VMEM((32 * r, c), BF16) for r, c, _ in plan]
        + [low_shape] * 5
        + [tall] * 3
        + [
            pltpu.VMEM((width, ff), BF16),
            pltpu.VMEM((ff, width), BF16),
            pltpu.VMEM((width, width), BF16),
            pltpu.VMEM((total, width), F32),
            pltpu.VMEM((total, width), F32),
            pltpu.VMEM((total, 128), F32),
            pltpu.VMEM((total, total), F32),
            pltpu.VMEM((total, total), F32),
            turned, turned, turned, turned,
            pltpu.VMEM((16, 128), F32),
            pltpu.VMEM((16, ff), F32),
            pltpu.SemaphoreType.DMA((9,)),
            pltpu.SemaphoreType.DMA((2, width // HEAD_DIM)),
            pltpu.SemaphoreType.DMA((count, 6)),
            pltpu.SemaphoreType.DMA((count, 6)),
            pltpu.SemaphoreType.DMA((2, 5)),
        ],
        compiler_params=pltpu.CompilerParams(
            collective_id=0, has_side_effects=True, vmem_limit_bytes=VMEM_LIMIT
        ),
        name="layer",
    )(*args)


def finish_kernel(rows, ff_rows, *refs):
    y = lax.axis_index("blk")
    out_in, dx_in = refs[:2]
    res = refs[2:13]
    (out_ref, dx_full, wq, bq, wk, wv, bv, wo, bo, gain, shift, wi, bi, wout, bout, fgain, fshift) = refs[13:]
    out_ref[y] = out_in[0]
    out_ref[1 - y] = out_in[1]
    dx_full[y] = dx_in[0].astype(F32)
    dx_full[1 - y] = dx_in[1].astype(F32)
    col = res[0].shape[2]
    for s in range(3):
        for h in range(2):
            at = (2 * s + h) * col
            wout[:, at : at + col] = res[s][h].astype(F32)
    wide = res[3].shape[2]
    for s in range(3):
        for h in range(2):
            at = (2 * s + h) * wide
            wi[:, at : at + wide] = res[3 + s][h].astype(F32)
    wide = res[6].shape[2]
    for s, ref in ((6, wo), (7, wq), (8, wk), (9, wv)):
        for h in range(2):
            ref[:, h * wide : (h + 1) * wide] = res[s][h].astype(F32)
    vec = res[10][0].astype(F32)
    rest = res[10][1].astype(F32)
    for i, ref in enumerate((bq, bv, bo, gain, shift, bout, fgain, fshift)):
        ref[...] = vec[i, 0:rows]
    bi[0:128] = vec[8, :]
    bi[128:ff_rows] = rest[8, 0 : ff_rows - 128]


def finish(out, dx, res, width, ff):
    rows, ff_rows = width // SPAN, ff // SPAN
    square, line = (rows, width), (rows,)
    shapes = (
        square, line, square, square, line, square, line, line, line,
        (rows, ff), (ff_rows,), (ff_rows, width), line, line, line,
    )
    vm = pl.BlockSpec(memory_space=pltpu.VMEM)
    return pl.pallas_call(
        functools.partial(finish_kernel, rows, ff_rows),
        out_shape=[jax.ShapeDtypeStruct(dx.shape, BF16), jax.ShapeDtypeStruct(dx.shape, F32)]
        + [jax.ShapeDtypeStruct(s, F32) for s in shapes],
        in_specs=[vm] * (2 + len(res)),
        out_specs=[vm] * (2 + len(shapes)),
        name="finish",
    )(out, dx, *res)


def per_device(
    dp_size,
    tokens,
    lengths,
    query_weight,
    query_bias,
    key_weight,
    value_weight,
    value_bias,
    out_weight,
    out_bias,
    norm_gain,
    norm_shift,
    inner_weight,
    inner_bias,
    outer_weight,
    outer_bias,
    final_gain,
    final_shift,
    cotangent,
):
    width, ff = inner_weight.shape
    plan = slab_plan(width, ff)
    low = dp_size // SPAN
    *res, dx, out, _, _ = run_layer(
        plan, low,
        (
            tokens, lengths, cotangent, query_weight, key_weight, value_weight, out_weight, inner_weight, outer_weight,
            query_bias, value_bias, out_bias, norm_gain, norm_shift, inner_bias, outer_bias, final_gain, final_shift,
        ),
    )
    layer_out, input_grad, *grads = finish(out, dx, res, width, ff)
    if low > 1:
        groups = [[t * low + i for i in range(low)] for t in range(SPAN)]
        grads = [
            lax.psum_scatter(g, "dp", scatter_dimension=0, axis_index_groups=groups, tiled=True)
            for g in grads
        ]
    return (layer_out, input_grad, *grads)


def solution(mesh):
    rows3 = P("dp", "blk", None)
    grad2, grad1 = P("dp", None), P("dp")
    return jax.shard_map(
        functools.partial(per_device, mesh.shape["dp"]),
        mesh=mesh,
        in_specs=(rows3, P("dp")) + (P(),) * 15 + (rows3,),
        out_specs=(
            rows3, rows3, grad2, grad1, grad2, grad2, grad1, grad2, grad1,
            grad1, grad1, grad2, grad1, grad2, grad1, grad1, grad1,
        ),
        check_vma=False,
    )
```

```python
import functools

import jax
import jax.numpy as jnp
from jax import lax
from jax.experimental import pallas as pl
from jax.experimental.pallas import tpu as pltpu
from jax.sharding import PartitionSpec as P

HEADS = 12
HEAD_DIM = 64
HEAD_PAIR = 2 * HEAD_DIM
ROW_CHUNK = 64
NORM_CHUNK = 256
EPS = 1e-12
HALF_ROOT = 0.7071067811865476
INV_ROOT_TAU = 0.3989422804014327
MESH = pl.DeviceIdType.MESH
BF16 = jnp.bfloat16
F32 = jnp.float32

ORDERS = {
    "A": ("c", "x", "y", "zl", "zh"),
    "B": ("c", "y", "zl", "x", "zh"),
    "C": ("c", "zl", "x", "y", "zh"),
    "E": ("c", "x", "zl", "y", "zh"),
    "F": ("c", "zl", "y", "x", "zh"),
    "G": ("c", "y", "x", "zl", "zh"),
    "H": ("c", "x", "zl", "zh", "y"),
    "L": ("c", "zl", "x", "zh", "y"),
}
SLAB_ORDERS = ("CA", "GH", "LG", "BF", "AE", "CG", "AC", "EL", "BC", "AE", "EA")
EVENTS = (
    -1, -1, -1, 0, -1, 1, 2, -1, -1, -1, 0, 3, -1, 4, 5, -1, -1, -1, -1, 1,
    2, -1, -1, 6, -1, 0, -1, 4, -1, -1, 3, 1, -1, 0, -1, 2, -1, 5, 7, 8,
    6, 4, -1, 9, 3, -1, 1, 10, -1, 0, 5, -1, 2, 4, 6, 1, 0, 7, 8, 5,
    9, 6, 4, 3, 7, 10, 2, 1, 5, 8, 10, 9, 6, 4, 3, 8, 7, 9, 2, 8,
    5, 10, 6, 3, 7, 8, 9, 10, 7, 9, 10,
)
BIT_OF = {"c": 1, "x": 2, "zl": 4, "zh": 8}
SPAN = 16
OFFSETS = (0, 16, 24, 28, 30, 31)
VMEM_LIMIT = 67_043_328


def contract_rows(left_mat, right_mat):
    return lax.dot_general(
        left_mat, right_mat, (((0,), (0,)), ((), ())), preferred_element_type=F32
    )


def times_trans(left_mat, right_mat):
    return lax.dot_general(
        left_mat, right_mat, (((1,), (1,)), ((), ())), preferred_element_type=F32
    )


def mat(left_mat, right_mat):
    return jnp.dot(left_mat, right_mat, preferred_element_type=F32)


def norm_rows(hidden, gain_vec, shift_vec):
    row_mean = jnp.mean(hidden, axis=-1, keepdims=True)
    centred = hidden - row_mean
    reciprocal = lax.rsqrt(jnp.mean(centred * centred, axis=-1, keepdims=True) + EPS)
    normed = centred * reciprocal
    return (normed * gain_vec + shift_vec, normed, reciprocal)


def norm_back(grad_in, normed, reciprocal, gain_vec):
    scaled = grad_in * gain_vec
    return reciprocal * (
        scaled
        - jnp.mean(scaled, axis=-1, keepdims=True)
        - normed * jnp.mean(scaled * normed, axis=-1, keepdims=True)
    )


def row_vec(ref):
    return ref[...].astype(F32).reshape(1, -1)


def block_index(owner, half, order):
    place = 0
    for dim in order:
        bit = half if dim == "y" else (owner // BIT_OF[dim]) % 2
        place = place * 2 + bit
    return place


def slab_plan(width, ff):
    rows, ff_rows = width // SPAN, ff // SPAN
    sizes = [(ff_rows, width // 6)] * 3 + [(rows, ff // 6)] * 3 + [(rows, width // 2)] * 4 + [(16, 128)]
    return tuple((r, c, (ORDERS[o[0]], ORDERS[o[1]])) for (r, c), o in zip(sizes, SLAB_ORDERS))


def layer_kernel(plan, low, *refs):
    count = len(plan)
    (tokens, lengths, cot_in, wq, wk, wv, wo_in, wi_in, wout_in, bq, bv, bo, gain_in, shift_in, bi, bout_in, fgain_in, fshift_in) = refs[:18]
    res, refs = refs[18 : 18 + count], refs[18 + count :]
    dx_hbm, out_hbm, prob_hbm, qkv_hbm = refs[:4]
    refs = refs[4:]
    bufs, recvs, refs = refs[: count - 3], refs[count - 3 : 2 * count - 3], refs[2 * count - 3 :]
    (x, cot, ctx, db, n1, act, dpre, slope, wi, wout, wo, hat1, acc, r1, sa, sb) = refs[:16]
    (turned, dqt, dkt, dvt, tmp, vec, load_sem, prob_sem, send_sem, recv_sem, side_sem, keep_sem) = refs[16:]
    dattn, dctx = n1, db
    total, width = x.shape
    span = total // 2
    ff = act.shape[1]
    pairs = width // HEAD_PAIR
    wide = sa.shape[1]
    bufs = list(bufs[:7]) + [bufs[s].at[:, 0 : width // 2] for s in (3, 4, 5)] + [bufs[7]]

    dp = lax.axis_index("dp")
    y = lax.axis_index("blk")
    top = dp // low
    bits = {dim: (top // b) % 2 for dim, b in BIT_OF.items()}
    bits["y"] = y
    partner = {dim: (dp + (1 - 2 * bits[dim]) * (b * low), y) for dim, b in BIT_OF.items()}
    partner["y"] = (dp, 1 - y)

    loads = {}

    def load(name, src, dst, sem):
        loads[name] = pltpu.make_async_copy(src, dst, sem)
        loads[name].start()

    mine, theirs = pl.ds(0, span), pl.ds(span, span)
    load("x", tokens.at[y], x.at[mine], load_sem.at[0])
    for i, w in enumerate((wq, wk, wv)):
        load(i, w, wout.at[pl.ds(i * width, width)], load_sem.at[1 + i])
    load("wo", wo_in, wo, load_sem.at[4])
    load("cot", cot_in.at[y], cot.at[mine], load_sem.at[5])
    load("wi", wi_in, wi, load_sem.at[6])

    barrier = pltpu.get_barrier_semaphore()
    for where in partner.values():
        pl.semaphore_signal(barrier, inc=1, device_id=where, device_id_type=MESH)
    pl.semaphore_wait(barrier, len(partner))

    def remote(src, dst, send, recv, where):
        copy = pltpu.make_async_remote_copy(
            src_ref=src, dst_ref=dst, send_sem=send, recv_sem=recv, device_id=where, device_id_type=MESH
        )
        copy.start()
        return copy

    def side(i, src, dst):
        return remote(src, dst, side_sem.at[0, i], side_sem.at[1, i], partner["y"])

    part = span // 2
    x_swaps = [
        side(i, tokens.at[1 - y, pl.ds(i * part, part)], x.at[pl.ds(span + i * part, part)]) for i in range(2)
    ]
    cot_swap = side(2, cot_in.at[1 - y], cot.at[theirs])

    def down(v):
        return jnp.sum(v, axis=0, keepdims=True)

    loads["x"].wait()
    for half in range(3):
        rows = slice(0, span) if half == 0 else slice(span + (half - 1) * part, span + half * part)
        if half > 0:
            x_swaps[half - 1].wait_recv()
        for i, b_ref in enumerate((bq, None, bv)):
            if half == 0:
                loads[i].wait()
            bias = None if b_ref is None else row_vec(b_ref)
            for c in range(width // 256):
                cols = slice(c * 256, (c + 1) * 256)
                got = mat(x[rows, :], wout[i * width : (i + 1) * width, cols])
                if bias is not None:
                    got = got + bias[:, cols]
                got = got.astype(BF16)
                if i == 0:
                    got = got * jnp.bfloat16(HEAD_DIM ** (-0.5))
                act[rows, i * width + c * 256 : i * width + (c + 1) * 256] = got
    load("wout", wout_in, wout, load_sem.at[7])
    load("qkv", act.at[:, pl.ds(0, 3 * width)], qkv_hbm, load_sem.at[8])

    length = lengths[y]
    at = lax.broadcasted_iota(jnp.int32, (1, total), 1)
    place = jnp.where(at < span, at + y * span, at - span + (1 - y) * span)
    mask = jnp.where(place < length, 0.0, -1e30).astype(F32)
    first = lax.broadcasted_iota(jnp.int32, (1, HEAD_PAIR), 1) < HEAD_DIM

    def lanes(i, p):
        return pl.ds(pl.multiple_of(i * width + p * HEAD_PAIR, HEAD_PAIR), HEAD_PAIR)

    def prob_lanes(p, e):
        return pl.ds(pl.multiple_of((2 * p + e) * total, 128), total)

    def prob_copy(kept, p, base, e):
        return pltpu.make_async_copy(
            kept.at[0:total, prob_lanes(p, e)], prob_hbm.at[2 * (p + base) + e], prob_sem.at[0, 2 * (p + base) + e]
        )

    def prob_back(kept, p, base, e):
        return pltpu.make_async_copy(
            prob_hbm.at[2 * (p + base) + e], kept.at[0:total, prob_lanes(p, e)], prob_sem.at[1, 2 * (p + base) + e]
        )

    def scores(p, e, into):
        qp, kp = act[:, lanes(0, p)], act[:, lanes(1, p)]
        keep = jnp.where(first, qp, 0) if e == 0 else jnp.where(first, 0, qp)
        into[...] = times_trans(keep.astype(BF16), kp)

    def soften(kept, p, base, e, s):
        for r in range(total // ROW_CHUNK):
            rows = slice(r * ROW_CHUNK, (r + 1) * ROW_CHUNK)
            raw = s[rows, :] + mask
            expo = jnp.exp(raw - jnp.max(raw, axis=1, keepdims=True))
            scale = 1.0 / jnp.sum(expo, axis=1, keepdims=True)
            kept[rows, prob_lanes(p, e)] = (expo * scale).astype(BF16)
        prob_copy(kept, p, base, e).start()

    scores(0, 0, sa)
    for p in range(pairs):
        kept, base = (slope, 0) if p < pairs // 2 else (dpre, pairs // 2)
        vp = act[:, lanes(2, p)]
        scores(p, 1, sb)
        soften(kept, p - base, base, 0, sa)
        if p + 1 < pairs:
            scores(p + 1, 0, sa)
        even = mat(kept[0:total, prob_lanes(p - base, 0)], vp)
        soften(kept, p - base, base, 1, sb)
        odd = mat(kept[0:total, prob_lanes(p - base, 1)], vp)
        ctx[:, lanes(0, p)] = jnp.where(first, even, odd).astype(BF16)

    loads["wo"].wait()
    acc[...] = mat(ctx[...], wo[...])
    bo, gain, shift, bout = row_vec(bo), row_vec(gain_in), row_vec(shift_in), row_vec(bout_in)
    fgain, fshift = row_vec(fgain_in), row_vec(fshift_in)
    vec[9:10, :] = row_vec(bi)

    def chunk(r):
        return pl.ds(pl.multiple_of(r * NORM_CHUNK, NORM_CHUNK), NORM_CHUNK)

    def norm_one(r, carry):
        rows = chunk(r)
        normed, hat, recip = norm_rows(x[rows, :].astype(F32) + acc[rows, :] + bo, gain, shift)
        hat1[rows, :] = hat
        r1[rows, :] = jnp.broadcast_to(recip, (NORM_CHUNK, 128))
        n1[rows, :] = normed.astype(BF16)
        acc[rows, :] = normed + bout
        return carry

    lax.fori_loop(0, total // NORM_CHUNK, norm_one, 0)

    for p in range(pairs // 2):
        for e in range(2):
            prob_copy(slope, p, 0, e).wait()
    loads["qkv"].wait()
    loads["wi"].wait()
    loads["wout"].wait()

    def span_of(j):
        return pl.ds(pl.multiple_of(j * wide, wide), wide)

    def pre_of(j, into):
        into[...] = mat(n1[...], wi[:, span_of(j)])

    def activate(j, pre):
        bias = vec[9:10, span_of(j)]
        for r in range(total // ROW_CHUNK):
            rows = slice(r * ROW_CHUNK, (r + 1) * ROW_CHUNK)
            u = pre[rows, :] + bias
            half = 0.5 * (1.0 + lax.erf(u * HALF_ROOT))
            act[rows, span_of(j)] = (u * half).astype(BF16)
            slope[rows, span_of(j)] = (half + u * jnp.exp(-0.5 * u * u) * INV_ROOT_TAU).astype(BF16)

    def second(j):
        acc[...] += mat(act[:, span_of(j)], wout[span_of(j), :])

    steps = ff // wide
    pre_of(0, sa)

    for i in range(steps // 2):
        pre_of(2 * i + 1, sb)
        activate(2 * i, sa)
        if i > 0:
            second(2 * i - 1)
        if i + 1 < steps // 2:
            pre_of(2 * i + 2, sa)
        activate(2 * i + 1, sb)
        second(2 * i)
    second(steps - 1)

    loads["cot"].wait()
    cot_swap.wait_recv()
    zero = jnp.zeros((1, width), F32)

    def norm_two(r, sums):
        rows = chunk(r)
        out, hat2, recip2 = norm_rows(acc[rows, :], fgain, fshift)
        g = cot[rows, :].astype(F32)
        cot[rows, :] = out.astype(BF16)
        dh2 = norm_back(g, hat2, recip2, fgain)
        acc[rows, :] = dh2
        low_dh2 = dh2.astype(BF16)
        db[rows, :] = low_dh2
        return (sums[0] + down(g * hat2), sums[1] + down(g), sums[2] + down(low_dh2.astype(F32)))

    fgain_sum, fshift_sum, bout_sum = lax.fori_loop(0, total // NORM_CHUNK, norm_two, (zero, zero, zero))
    vec[5:6, 0:width] = bout_sum
    vec[6:7, 0:width] = fgain_sum
    vec[7:8, 0:width] = fshift_sum
    load("out", cot.at[mine], out_hbm.at[y], load_sem.at[9])

    pending = {}
    stage_of = {}
    sent = set()

    def blocks(s, base, n):
        size = plan[s][0]
        return pl.ds(pl.multiple_of(base * size, 16), n * size)

    def step_of(s, i):
        even, odd = (plan[s][2][c][i] for c in range(2))
        if even == odd:
            return bits[even], partner[even]
        own = bits["c"]
        return (
            bits[even] + own * (bits[odd] - bits[even]),
            tuple(a + own * (b - a) for a, b in zip(partner[even], partner[odd])),
        )

    def start(s, i):
        if i == 5:
            src, dst, where = recvs[s].at[blocks(s, 30, 1)], recvs[s].at[blocks(s, 31, 1)], partner["y"]
        else:
            half = 16 >> i
            bit, where = step_of(s, i)
            src_ref, base = (bufs[s], 0) if i == 0 else (recvs[s], OFFSETS[i - 1])
            src = src_ref.at[blocks(s, base + (1 - bit) * half, half)]
            dst = recvs[s].at[blocks(s, OFFSETS[i], half)]
        pending[s, i] = remote(src, dst, send_sem.at[s, i], recv_sem.at[s, i], where)
        stage_of[s] = i

    kept_copies = []

    def keep(s, which):
        to = y + which * (1 - 2 * y)
        copy = pltpu.make_async_copy(recvs[s].at[blocks(s, 30 + which, 1)], res[s].at[to], keep_sem.at[s, which])
        copy.start()
        kept_copies.append(copy)

    def advance(s):
        i = stage_of[s]
        pending[s, i].wait_recv()
        if i == 5:
            keep(s, 1)
            stage_of[s] = 6
            return
        half = 16 >> i
        src_ref, base = (bufs[s], 0) if i == 0 else (recvs[s], OFFSETS[i - 1])
        mine = base + step_of(s, i)[0] * half

        def add(j, carry):
            got = blocks(s, OFFSETS[i] + j, 1)
            recvs[s][got] = recvs[s][got] + src_ref[blocks(s, mine + j, 1)]
            return carry

        lax.fori_loop(0, half, add, 0)
        start(s, i + 1)
        if i == 4:
            keep(s, 0)

    def put(s, owner, core, h, value):
        bufs[s][blocks(s, block_index(owner, h, plan[s][2][core]), 1)] = value

    rows_of, ff_rows, col = plan[3][0], plan[0][0], plan[0][1]

    two = 2 * ff_rows

    def turn_outer(t, slot):
        turned[slot * two : (slot + 1) * two, :] = act[:, pl.ds(pl.multiple_of(t * two, 128), two)].T

    def outer_rows(t, slot):
        part = mat(turned[slot * two : (slot + 1) * two, :], db[...]).astype(BF16)
        for e in range(2):
            for s in range(3):
                for h in range(2):
                    at = (2 * s + h) * col
                    put(s, 2 * t + e, e, h, part[e * ff_rows : (e + 1) * ff_rows, at : at + col])

    def outer_four(i, carry):
        turn_outer(2 * i + 1, 1)
        outer_rows(2 * i, 0)
        turn_outer(lax.rem(2 * i + 2, SPAN // 2), 0)
        outer_rows(2 * i + 1, 1)
        return carry

    def by_owner(s, h, product):
        tall = 8 * rows_of

        def some(part, carry):
            block = product(turned[pl.ds(pl.multiple_of(part * tall, tall), tall), :]).astype(BF16)
            for o in range(8):
                put(s, part * 8 + o, o % 2, h, block[o * rows_of : (o + 1) * rows_of])
            return carry

        lax.fori_loop(0, 2, some, 0)

    sides = []

    def outer_slabs():
        turn_outer(0, 0)
        lax.fori_loop(0, SPAN // 4, outer_four, 0)
        for s in range(3):
            start(s, 0)
        sides.append(side(3, cot.at[theirs], out_hbm.at[y]))
        load("qkv", qkv_hbm, act.at[:, pl.ds(0, 3 * width)], load_sem.at[8])
        dact_of(0, sa)

    def dact_of(j, into):
        into[...] = times_trans(db[...], wout[span_of(j), :])

    def bend(j, dact):
        sums = jnp.zeros((1, wide), F32)
        for r in range(total // ROW_CHUNK):
            rows = slice(r * ROW_CHUNK, (r + 1) * ROW_CHUNK)
            value = (dact[rows, :] * slope[rows, span_of(j)].astype(F32)).astype(BF16)
            dpre[rows, span_of(j)] = value
            sums += down(value.astype(F32))
        vec[8:9, span_of(j)] = sums

    def backward(i):
        if i == 0:
            for p in range(pairs // 2):
                for e in range(2):
                    prob_copy(dpre, p, pairs // 2, e).wait()
        dact_of(2 * i + 1, sb)
        bend(2 * i, sa)
        if 2 * i + 2 < steps:
            dact_of(2 * i + 2, sa)
        bend(2 * i + 1, sb)
        if i == steps // 2 - 1:
            for j, w in enumerate((wq, wk, wv)):
                load(j, w, wout.at[pl.ds(j * width, width)], load_sem.at[1 + j])
            turned[...] = n1[...].T

    def inner_slab(s):
        c = plan[s][1]
        for h in range(2):
            at = ((s - 3) * 2 + h) * c
            by_owner(s, h, lambda left: mat(left, dpre[:, at : at + c]))
        start(s, 0)

    def dn1_part(c):
        cols = slice(c * 256, (c + 1) * 256)
        acc[:, cols] += times_trans(dpre[...], wi[cols, :])

    def norm_one_back():
        for p in range(pairs // 2):
            for e in range(2):
                prob_back(wi, p, 0, e).start()
                prob_back(dpre, p, pairs // 2, e).start()

        def step(r, sums):
            rows = chunk(r)
            dn1, hat = acc[rows, :], hat1[rows, :]
            dh1 = norm_back(dn1, hat, r1[rows, 0:1], gain)
            acc[rows, :] = dh1
            low_dh1 = dh1.astype(BF16)
            dattn[rows, :] = low_dh1
            return (sums[0] + down(dn1 * hat), sums[1] + down(dn1), sums[2] + down(low_dh1.astype(F32)))

        a, b, c = lax.fori_loop(0, total // NORM_CHUNK, step, (zero, zero, zero))
        vec[3:4, 0:width] = a
        vec[4:5, 0:width] = b
        vec[2:3, 0:width] = c

    half_width = width // 2

    def out_slab():
        turned[...] = ctx[...].T
        for h in range(2):
            by_owner(6, h, lambda left: mat(left, dattn[:, h * half_width : (h + 1) * half_width]))
        start(6, 0)
        for c in range(width // 256):
            cols = slice(c * 256, (c + 1) * 256)
            dctx[:, cols] = times_trans(dattn[...], wo[cols, :]).astype(BF16)

    def head_back(kept, base, p, e):
        prob_back(kept, p, base, e).wait()
        pair = p + base
        qp, kp, vp, dop = act[:, lanes(0, pair)], act[:, lanes(1, pair)], act[:, lanes(2, pair)], dctx[:, lanes(0, pair)]
        dpe, dse = (sa, slope.at[:, 0:total]) if e == 0 else (sb, slope.at[:, total : 2 * total])
        mine_only = (lambda v: jnp.where(first, v, 0)) if e == 0 else (lambda v: jnp.where(first, 0, v))
        dpe[...] = times_trans(mine_only(dop).astype(BF16), vp)
        here = slice(e * HEAD_DIM, (e + 1) * HEAD_DIM)
        turned_q, turned_k, turned_do = qp.T[here], kp.T[here], dop.T[here]
        delta = jnp.sum(mine_only(dop.astype(F32) * ctx[:, lanes(0, pair)].astype(F32)), axis=1, keepdims=True)
        for r in range(total // ROW_CHUNK):
            rows = slice(r * ROW_CHUNK, (r + 1) * ROW_CHUNK)
            dse[rows, :] = (kept[rows, prob_lanes(p, e)].astype(F32) * (dpe[rows, :] - delta[rows])).astype(BF16)
        there = pl.ds(pl.multiple_of((2 * pair + e) * HEAD_DIM, HEAD_DIM), HEAD_DIM)
        dvt[there, :] = mat(turned_do, kept[0:total, prob_lanes(p, e)]).astype(BF16)
        dqt[there, :] = (times_trans(turned_k, dse[...]) * HEAD_DIM ** (-0.5)).astype(BF16)
        dkt[there, :] = mat(turned_q, dse[...]).astype(BF16)

    def pairs_back(low_pair, high_pair):
        if low_pair == 0:
            loads["qkv"].wait()
        kept, base = (wi, 0) if low_pair < pairs // 2 else (dpre, pairs // 2)

        def pair_back(p, carry):
            head_back(kept, base, p, 0)
            head_back(kept, base, p, 1)
            return carry

        for p in range(low_pair - base, high_pair - base):
            pair_back(p, 0)

    def head_slab(s, right):
        if s == 7:
            turned[...] = x[...].T
        pending[s - 4, 0].wait_send()
        sent.add((s - 4, 0))
        for h in range(2):
            by_owner(s, h, lambda left: times_trans(left, right[h * half_width : (h + 1) * half_width, :]))
        start(s, 0)

    def vectors():
        ones = jnp.ones((8, total), BF16)
        vec[0:1, 0:width] = times_trans(ones, dqt[...])[0:1]
        vec[1:2, 0:width] = times_trans(ones, dvt[...])[0:1]
        for o in range(SPAN):
            tmp[...] = jnp.zeros_like(tmp)
            tmp[0:8, 0:rows_of] = vec[0:8, o * rows_of : (o + 1) * rows_of]
            tmp[8:9, :] = vec[8:9, o * ff_rows : o * ff_rows + 128]
            put(10, o, o % 2, 0, tmp[...].astype(BF16))
            tmp[...] = jnp.zeros_like(tmp)
            tmp[8:9, 0 : ff_rows - 128] = vec[8:9, o * ff_rows + 128 : (o + 1) * ff_rows]
            put(10, o, o % 2, 1, tmp[...].astype(BF16))
        start(10, 0)

    def input_part(c):
        if c == 0:
            for i in range(3):
                loads[i].wait()
        cols = slice(c * 256, (c + 1) * 256)
        dxt = sum(
            mat(wout[i * width + c * 256 : i * width + (c + 1) * 256, :], d[...]) for i, d in enumerate((dqt, dkt, dvt))
        )
        dx = (dxt.T + acc[:, cols]).astype(BF16)
        db[:, cols] = dx
        if c == width // 256 - 1:
            sides.append(side(4, db.at[theirs], dx_hbm.at[y]))
            load("dx", db.at[mine], dx_hbm.at[y], load_sem.at[10])

    pieces = [outer_slabs]
    pieces += [functools.partial(backward, i) for i in range(steps // 2)]
    pieces += [functools.partial(inner_slab, s) for s in (3, 4, 5)]
    pieces += [functools.partial(dn1_part, c) for c in range(width // 256)]
    pieces += [norm_one_back, out_slab]
    pieces += [functools.partial(pairs_back, p, p + 1) for p in range(pairs)]
    pieces += [functools.partial(head_slab, s, r) for s, r in ((7, dqt), (8, dkt), (9, dvt))]
    pieces += [vectors] + [functools.partial(input_part, c) for c in range(width // 256)]
    for event in EVENTS:
        if event < 0:
            pieces.pop(0)()
        else:
            advance(event)
    for wait in (*x_swaps, cot_swap):
        wait.wait_send()
    for wait in (*sides, *kept_copies, loads["out"], loads["dx"]):
        wait.wait()
    for key, copy in pending.items():
        if key not in sent:
            copy.wait_send()


def run_layer(plan, low, args):
    count = len(plan)
    tokens = args[0]
    _, span, width = tokens.shape
    total = 2 * span
    ff = args[7].shape[1]
    hbm = pl.BlockSpec(memory_space=pl.ANY)
    vm = pl.BlockSpec(memory_space=pltpu.VMEM)
    smem = pl.BlockSpec(memory_space=pltpu.SMEM)
    low_shape, tall = pltpu.VMEM((total, width), BF16), pltpu.VMEM((total, ff), BF16)
    turned = pltpu.VMEM((width, total), BF16)
    own = [s for s in range(count) if s not in (7, 8, 9)]
    return pl.pallas_call(
        functools.partial(layer_kernel, plan, low),
        out_shape=[jax.ShapeDtypeStruct((2, r, c), BF16) for r, c, _ in plan]
        + [
            jax.ShapeDtypeStruct((2, span, width), BF16),
            jax.ShapeDtypeStruct((2, span, width), BF16),
            jax.ShapeDtypeStruct((width // HEAD_DIM, total, total), BF16),
            jax.ShapeDtypeStruct((total, 3 * width), BF16),
        ],
        in_specs=[hbm, smem] + [hbm] * 7 + [vm] * 9,
        out_specs=[hbm] * (count + 4),
        scratch_shapes=[pltpu.VMEM((32 * plan[s][0], plan[s][1]), BF16) for s in own]
        + [pltpu.VMEM((32 * r, c), BF16) for r, c, _ in plan]
        + [low_shape] * 5
        + [tall] * 3
        + [
            pltpu.VMEM((width, ff), BF16),
            pltpu.VMEM((ff, width), BF16),
            pltpu.VMEM((width, width), BF16),
            pltpu.VMEM((total, width), F32),
            pltpu.VMEM((total, width), F32),
            pltpu.VMEM((total, 128), F32),
            pltpu.VMEM((total, total), F32),
            pltpu.VMEM((total, total), F32),
            turned, turned, turned, turned,
            pltpu.VMEM((16, 128), F32),
            pltpu.VMEM((16, ff), F32),
            pltpu.SemaphoreType.DMA((11,)),
            pltpu.SemaphoreType.DMA((2, width // HEAD_DIM)),
            pltpu.SemaphoreType.DMA((count, 6)),
            pltpu.SemaphoreType.DMA((count, 6)),
            pltpu.SemaphoreType.DMA((2, 5)),
            pltpu.SemaphoreType.DMA((count, 2)),
        ],
        compiler_params=pltpu.CompilerParams(
            collective_id=0, has_side_effects=True, vmem_limit_bytes=VMEM_LIMIT
        ),
        name="layer",
    )(*args)


def finish_kernel(rows, ff_rows, *refs):
    inputs, refs = refs[:13], refs[13:]
    (out_ref, dx_ref, wq, bq, wk, wv, bv, wo, bo, gain, shift, wi, bi, wout, bout, fgain, fshift), refs = refs[:17], refs[17:]
    held, (dx_full, square, wide_full, tall_full, in_sem, out_sem) = refs[:13], refs[13:]
    gets = [pltpu.make_async_copy(src, dst, in_sem.at[i]) for i, (src, dst) in enumerate(zip(inputs, held))]
    order = (1, 0, 2, 3, 4, 5, 6, 7, 8, 9, 10, 11, 12)
    for i in order:
        gets[i].start()
    puts = []

    def put(src, dst):
        copy = pltpu.make_async_copy(src, dst, out_sem.at[len(puts)])
        copy.start()
        puts.append(copy)

    gets[1].wait()
    for n in range(2):
        dx_full[n] = held[1][n].astype(F32)
        put(dx_full.at[n], dx_ref.at[n])
    gets[0].wait()
    put(held[0], out_ref)
    res = held[2:]
    col = res[0].shape[2]
    for s in range(3):
        gets[2 + s].wait()
        for h in range(2):
            at = (2 * s + h) * col
            tall_full[:, at : at + col] = res[s][h].astype(F32)
    put(tall_full, wout)
    wide = res[3].shape[2]
    for s in range(3):
        gets[5 + s].wait()
        for h in range(2):
            at = (2 * s + h) * wide
            wide_full[:, at : at + wide] = res[3 + s][h].astype(F32)
    put(wide_full, wi)
    wide = res[6].shape[2]
    for n, ref in enumerate((wo, wq, wk, wv)):
        gets[8 + n].wait()
        for h in range(2):
            square[n, :, h * wide : (h + 1) * wide] = res[6 + n][h].astype(F32)
        put(square.at[n], ref)
    gets[12].wait()
    vec = res[10][0].astype(F32)
    rest = res[10][1].astype(F32)
    for i, ref in enumerate((bq, bv, bo, gain, shift, bout, fgain, fshift)):
        ref[...] = vec[i, 0:rows]
    bi[0:128] = vec[8, :]
    bi[128:ff_rows] = rest[8, 0 : ff_rows - 128]
    for copy in puts:
        copy.wait()


def finish(out, dx, res, width, ff):
    rows, ff_rows = width // SPAN, ff // SPAN
    square, line = (rows, width), (rows,)
    shapes = (
        square, line, square, square, line, square, line, line, line,
        (rows, ff), (ff_rows,), (ff_rows, width), line, line, line,
    )
    vm = pl.BlockSpec(memory_space=pltpu.VMEM)
    hbm = pl.BlockSpec(memory_space=pl.ANY)
    inputs = (out, dx, *res)
    return pl.pallas_call(
        functools.partial(finish_kernel, rows, ff_rows),
        out_shape=[jax.ShapeDtypeStruct(dx.shape, BF16), jax.ShapeDtypeStruct(dx.shape, F32)]
        + [jax.ShapeDtypeStruct(s, F32) for s in shapes],
        in_specs=[hbm] * len(inputs),
        out_specs=[hbm] * 2 + [hbm if len(s) == 2 else vm for s in shapes],
        scratch_shapes=[pltpu.VMEM(a.shape, a.dtype) for a in inputs]
        + [
            pltpu.VMEM(dx.shape, F32),
            pltpu.VMEM((4, rows, width), F32),
            pltpu.VMEM((rows, ff), F32),
            pltpu.VMEM((ff_rows, width), F32),
            pltpu.SemaphoreType.DMA((len(inputs),)),
            pltpu.SemaphoreType.DMA((9,)),
        ],
        name="finish",
    )(*inputs)


def per_device(
    dp_size,
    tokens,
    lengths,
    query_weight,
    query_bias,
    key_weight,
    value_weight,
    value_bias,
    out_weight,
    out_bias,
    norm_gain,
    norm_shift,
    inner_weight,
    inner_bias,
    outer_weight,
    outer_bias,
    final_gain,
    final_shift,
    cotangent,
):
    width, ff = inner_weight.shape
    plan = slab_plan(width, ff)
    low = dp_size // SPAN
    *res, dx, out, _, _ = run_layer(
        plan, low,
        (
            tokens, lengths, cotangent, query_weight, key_weight, value_weight, out_weight, inner_weight, outer_weight,
            query_bias, value_bias, out_bias, norm_gain, norm_shift, inner_bias, outer_bias, final_gain, final_shift,
        ),
    )
    layer_out, input_grad, *grads = finish(out, dx, res, width, ff)
    if low > 1:
        groups = [[t * low + i for i in range(low)] for t in range(SPAN)]
        grads = [
            lax.psum_scatter(g, "dp", scatter_dimension=0, axis_index_groups=groups, tiled=True)
            for g in grads
        ]
    return (layer_out, input_grad, *grads)


def solution(mesh):
    rows3 = P("dp", "blk", None)
    grad2, grad1 = P("dp", None), P("dp")
    return jax.shard_map(
        functools.partial(per_device, mesh.shape["dp"]),
        mesh=mesh,
        in_specs=(rows3, P("dp")) + (P(),) * 15 + (rows3,),
        out_specs=(
            rows3, rows3, grad2, grad1, grad2, grad2, grad1, grad2, grad1,
            grad1, grad1, grad2, grad1, grad2, grad1, grad1, grad1,
        ),
        check_vma=False,
    )
```

```python
import functools

import jax
import jax.numpy as jnp
from jax import lax
from jax.experimental import pallas as pl
from jax.experimental.pallas import tpu as pltpu
from jax.sharding import PartitionSpec as P

HEADS = 12
HEAD_DIM = 64
HEAD_PAIR = 2 * HEAD_DIM
ROW_CHUNK = 64
NORM_CHUNK = 256
EPS = 1e-12
HALF_ROOT = 0.7071067811865476
INV_ROOT_TAU = 0.3989422804014327
MESH = pl.DeviceIdType.MESH
BF16 = jnp.bfloat16
F32 = jnp.float32

ORDERS = {
    "A": ("c", "x", "y", "zl", "zh"),
    "B": ("c", "y", "zl", "x", "zh"),
    "C": ("c", "zl", "x", "y", "zh"),
    "E": ("c", "x", "zl", "y", "zh"),
    "F": ("c", "zl", "y", "x", "zh"),
    "G": ("c", "y", "x", "zl", "zh"),
    "L": ("c", "zl", "x", "zh", "y"),
}
SLAB_ORDERS = ("CA", "AF", "CG", "BA", "LE", "GL", "GE", "CG", "EA", "GL", "BF")
EVENTS = (
    -1, -1, -1, 0, -1, 1, 2, -1, -1, -1, 3, -1, 4, 0, 5, -1, -1, 1, -1, -1,
    0, 3, 2, -1, 6, -1, -1, -1, -1, 5, 4, -1, 2, 1, -1, 0, 3, -1, -1, 7,
    -1, 8, 2, 6, 9, 10, -1, 0, 4, -1, -1, 5, 3, 7, 1, 2, 4, 0, 8, 9,
    10, 6, 5, 7, 3, 1, 2, 9, 8, 10, 4, 10, 6, 7, 5, 9, 3, 10, 1, 8,
    6, 4, 7, 9, 5, 10, 6, 8, 7, 9, 8,
)
BIT_OF = {"c": 1, "x": 2, "zl": 4, "zh": 8}
SPAN = 16
OFFSETS = (0, 16, 24, 28, 30, 31)
VMEM_LIMIT = 67_043_328


def contract_rows(left_mat, right_mat):
    return lax.dot_general(
        left_mat, right_mat, (((0,), (0,)), ((), ())), preferred_element_type=F32
    )


def times_trans(left_mat, right_mat):
    return lax.dot_general(
        left_mat, right_mat, (((1,), (1,)), ((), ())), preferred_element_type=F32
    )


def mat(left_mat, right_mat):
    return jnp.dot(left_mat, right_mat, preferred_element_type=F32)


def norm_rows(hidden, gain_vec, shift_vec):
    row_mean = jnp.mean(hidden, axis=-1, keepdims=True)
    centred = hidden - row_mean
    reciprocal = lax.rsqrt(jnp.mean(centred * centred, axis=-1, keepdims=True) + EPS)
    normed = centred * reciprocal
    return (normed * gain_vec + shift_vec, normed, reciprocal)


def norm_back(grad_in, normed, reciprocal, gain_vec):
    scaled = grad_in * gain_vec
    return reciprocal * (
        scaled
        - jnp.mean(scaled, axis=-1, keepdims=True)
        - normed * jnp.mean(scaled * normed, axis=-1, keepdims=True)
    )


def row_vec(ref):
    return ref[...].astype(F32).reshape(1, -1)


def block_index(owner, half, order):
    place = 0
    for dim in order:
        bit = half if dim == "y" else (owner // BIT_OF[dim]) % 2
        place = place * 2 + bit
    return place


def slab_plan(width, ff):
    rows, ff_rows = width // SPAN, ff // SPAN
    sizes = [(ff_rows, width // 6)] * 3 + [(rows, ff // 6)] * 3 + [(rows, width // 2)] * 4 + [(16, 128)]
    return tuple((r, c, (ORDERS[o[0]], ORDERS[o[1]])) for (r, c), o in zip(sizes, SLAB_ORDERS))


def layer_kernel(plan, low, *refs):
    count = len(plan)
    (tokens, lengths, cot_in, wq, wk, wv, wo_in, wi_in, wout_in, bq, bv, bo, gain_in, shift_in, bi, bout_in, fgain_in, fshift_in) = refs[:18]
    res, refs = refs[18 : 18 + count], refs[18 + count :]
    dx_hbm, out_hbm, prob_hbm, qkv_hbm = refs[:4]
    refs = refs[4:]
    bufs, recvs, refs = refs[: count - 3], refs[count - 3 : 2 * count - 3], refs[2 * count - 3 :]
    (x, cot, ctx, db, n1, act, dpre, slope, wi, wout, wo, hat1, acc, r1, sa, sb) = refs[:16]
    (turned, dqt, dkt, dvt, tmp, vec, load_sem, prob_sem, send_sem, recv_sem, side_sem, keep_sem) = refs[16:]
    dattn, dctx = n1, db
    total, width = x.shape
    span = total // 2
    ff = act.shape[1]
    pairs = width // HEAD_PAIR
    wide = sa.shape[1]
    bufs = list(bufs[:7]) + [bufs[s].at[:, 0 : width // 2] for s in (3, 4, 5)] + [bufs[7]]

    dp = lax.axis_index("dp")
    y = lax.axis_index("blk")
    top = dp // low
    bits = {dim: (top // b) % 2 for dim, b in BIT_OF.items()}
    bits["y"] = y
    partner = {dim: (dp + (1 - 2 * bits[dim]) * (b * low), y) for dim, b in BIT_OF.items()}
    partner["y"] = (dp, 1 - y)

    loads = {}

    def load(name, src, dst, sem):
        loads[name] = pltpu.make_async_copy(src, dst, sem)
        loads[name].start()

    mine, theirs = pl.ds(0, span), pl.ds(span, span)
    load("x", tokens.at[y], x.at[mine], load_sem.at[0])
    for i, w in enumerate((wq, wk, wv)):
        load(i, w, wout.at[pl.ds(i * width, width)], load_sem.at[1 + i])
    load("wo", wo_in, wo, load_sem.at[4])
    load("cot", cot_in.at[y], cot.at[mine], load_sem.at[5])
    load("wi", wi_in, wi, load_sem.at[6])

    barrier = pltpu.get_barrier_semaphore()
    for where in partner.values():
        pl.semaphore_signal(barrier, inc=1, device_id=where, device_id_type=MESH)
    pl.semaphore_wait(barrier, len(partner))

    def remote(src, dst, send, recv, where):
        copy = pltpu.make_async_remote_copy(
            src_ref=src, dst_ref=dst, send_sem=send, recv_sem=recv, device_id=where, device_id_type=MESH
        )
        copy.start()
        return copy

    def side(i, src, dst):
        return remote(src, dst, side_sem.at[0, i], side_sem.at[1, i], partner["y"])

    part = span // 2
    x_swaps = [
        side(i, tokens.at[1 - y, pl.ds(i * part, part)], x.at[pl.ds(span + i * part, part)]) for i in range(2)
    ]
    cot_swap = side(2, cot_in.at[1 - y], cot.at[theirs])

    def down(v):
        return jnp.sum(v, axis=0, keepdims=True)

    loads["x"].wait()
    for half in range(3):
        rows = slice(0, span) if half == 0 else slice(span + (half - 1) * part, span + half * part)
        if half > 0:
            x_swaps[half - 1].wait_recv()
        for i, b_ref in enumerate((bq, None, bv)):
            if half == 0:
                loads[i].wait()
            bias = None if b_ref is None else row_vec(b_ref)
            for c in range(width // 256):
                cols = slice(c * 256, (c + 1) * 256)
                got = mat(x[rows, :], wout[i * width : (i + 1) * width, cols])
                if bias is not None:
                    got = got + bias[:, cols]
                got = got.astype(BF16)
                if i == 0:
                    got = got * jnp.bfloat16(HEAD_DIM ** (-0.5))
                act[rows, i * width + c * 256 : i * width + (c + 1) * 256] = got
    load("wout", wout_in, wout, load_sem.at[7])
    load("qkv", act.at[:, pl.ds(0, 3 * width)], qkv_hbm, load_sem.at[8])

    length = lengths[y]
    at = lax.broadcasted_iota(jnp.int32, (1, total), 1)
    place = jnp.where(at < span, at + y * span, at - span + (1 - y) * span)
    mask = jnp.where(place < length, 0.0, -1e30).astype(F32)
    first = lax.broadcasted_iota(jnp.int32, (1, HEAD_PAIR), 1) < HEAD_DIM

    def lanes(i, p):
        return pl.ds(pl.multiple_of(i * width + p * HEAD_PAIR, HEAD_PAIR), HEAD_PAIR)

    def prob_lanes(p, e):
        return pl.ds(pl.multiple_of((2 * p + e) * total, 128), total)

    def prob_copy(kept, p, base, e):
        return pltpu.make_async_copy(
            kept.at[0:total, prob_lanes(p, e)], prob_hbm.at[2 * (p + base) + e], prob_sem.at[0, 2 * (p + base) + e]
        )

    def prob_back(kept, p, base, e):
        return pltpu.make_async_copy(
            prob_hbm.at[2 * (p + base) + e], kept.at[0:total, prob_lanes(p, e)], prob_sem.at[1, 2 * (p + base) + e]
        )

    def scores(p, e, into):
        qp, kp = act[:, lanes(0, p)], act[:, lanes(1, p)]
        keep = jnp.where(first, qp, 0) if e == 0 else jnp.where(first, 0, qp)
        into[...] = times_trans(keep.astype(BF16), kp)

    def soften(kept, p, base, e, s):
        for r in range(total // ROW_CHUNK):
            rows = slice(r * ROW_CHUNK, (r + 1) * ROW_CHUNK)
            raw = s[rows, :] + mask
            expo = jnp.exp(raw - jnp.max(raw, axis=1, keepdims=True))
            scale = 1.0 / jnp.sum(expo, axis=1, keepdims=True)
            kept[rows, prob_lanes(p, e)] = (expo * scale).astype(BF16)
        prob_copy(kept, p, base, e).start()

    scores(0, 0, sa)
    for p in range(pairs):
        kept, base = (slope, 0) if p < pairs // 2 else (dpre, pairs // 2)
        vp = act[:, lanes(2, p)]
        scores(p, 1, sb)
        soften(kept, p - base, base, 0, sa)
        if p + 1 < pairs:
            scores(p + 1, 0, sa)
        even = mat(kept[0:total, prob_lanes(p - base, 0)], vp)
        soften(kept, p - base, base, 1, sb)
        odd = mat(kept[0:total, prob_lanes(p - base, 1)], vp)
        ctx[:, lanes(0, p)] = jnp.where(first, even, odd).astype(BF16)

    loads["wo"].wait()
    acc[...] = mat(ctx[...], wo[...])
    bo, gain, shift, bout = row_vec(bo), row_vec(gain_in), row_vec(shift_in), row_vec(bout_in)
    fgain, fshift = row_vec(fgain_in), row_vec(fshift_in)
    vec[9:10, :] = row_vec(bi)

    def chunk(r):
        return pl.ds(pl.multiple_of(r * NORM_CHUNK, NORM_CHUNK), NORM_CHUNK)

    def norm_one(r, carry):
        rows = chunk(r)
        normed, hat, recip = norm_rows(x[rows, :].astype(F32) + acc[rows, :] + bo, gain, shift)
        hat1[rows, :] = hat
        r1[rows, :] = jnp.broadcast_to(recip, (NORM_CHUNK, 128))
        n1[rows, :] = normed.astype(BF16)
        acc[rows, :] = normed + bout
        return carry

    lax.fori_loop(0, total // NORM_CHUNK, norm_one, 0)

    for p in range(pairs // 2):
        for e in range(2):
            prob_copy(slope, p, 0, e).wait()
    loads["qkv"].wait()
    loads["wi"].wait()
    loads["wout"].wait()

    def span_of(j):
        return pl.ds(pl.multiple_of(j * wide, wide), wide)

    def pre_of(j, into):
        into[...] = mat(n1[...], wi[:, span_of(j)])

    def activate(j, pre):
        bias = vec[9:10, span_of(j)]
        for r in range(total // ROW_CHUNK):
            rows = slice(r * ROW_CHUNK, (r + 1) * ROW_CHUNK)
            u = pre[rows, :] + bias
            half = 0.5 * (1.0 + lax.erf(u * HALF_ROOT))
            act[rows, span_of(j)] = (u * half).astype(BF16)
            slope[rows, span_of(j)] = (half + u * jnp.exp(-0.5 * u * u) * INV_ROOT_TAU).astype(BF16)

    def second(j):
        acc[...] += mat(act[:, span_of(j)], wout[span_of(j), :])

    steps = ff // wide
    pre_of(0, sa)

    for i in range(steps // 2):
        pre_of(2 * i + 1, sb)
        activate(2 * i, sa)
        if i > 0:
            second(2 * i - 1)
        if i + 1 < steps // 2:
            pre_of(2 * i + 2, sa)
        activate(2 * i + 1, sb)
        second(2 * i)
    second(steps - 1)

    loads["cot"].wait()
    cot_swap.wait_recv()
    zero = jnp.zeros((1, width), F32)

    def norm_two(i, sums):
        rows = chunk(total // NORM_CHUNK - 1 - i)
        out, hat2, recip2 = norm_rows(acc[rows, :], fgain, fshift)
        g = cot[rows, :].astype(F32)
        cot[rows, :] = out.astype(BF16)
        dh2 = norm_back(g, hat2, recip2, fgain)
        acc[rows, :] = dh2
        low_dh2 = dh2.astype(BF16)
        db[rows, :] = low_dh2
        return (sums[0] + down(g * hat2), sums[1] + down(g), sums[2] + down(low_dh2.astype(F32)))

    half_way = total // NORM_CHUNK // 2
    part_sums = lax.fori_loop(0, half_way, norm_two, (zero, zero, zero))
    sides = [side(3, cot.at[theirs], out_hbm.at[y])]
    fgain_sum, fshift_sum, bout_sum = lax.fori_loop(half_way, 2 * half_way, norm_two, part_sums)
    vec[5:6, 0:width] = bout_sum
    vec[6:7, 0:width] = fgain_sum
    vec[7:8, 0:width] = fshift_sum
    load("out", cot.at[mine], out_hbm.at[y], load_sem.at[9])

    pending = {}
    stage_of = {}
    sent = set()

    def blocks(s, base, n):
        size = plan[s][0]
        return pl.ds(pl.multiple_of(base * size, 16), n * size)

    def step_of(s, i):
        even, odd = (plan[s][2][c][i] for c in range(2))
        if even == odd:
            return bits[even], partner[even]
        own = bits["c"]
        return (
            bits[even] + own * (bits[odd] - bits[even]),
            tuple(a + own * (b - a) for a, b in zip(partner[even], partner[odd])),
        )

    def start(s, i):
        if i == 5:
            src, dst, where = recvs[s].at[blocks(s, 30, 1)], recvs[s].at[blocks(s, 31, 1)], partner["y"]
        else:
            half = 16 >> i
            bit, where = step_of(s, i)
            src_ref, base = (bufs[s], 0) if i == 0 else (recvs[s], OFFSETS[i - 1])
            src = src_ref.at[blocks(s, base + (1 - bit) * half, half)]
            dst = recvs[s].at[blocks(s, OFFSETS[i], half)]
        pending[s, i] = remote(src, dst, send_sem.at[s, i], recv_sem.at[s, i], where)
        stage_of[s] = i

    kept_copies = []

    def keep(s, which):
        to = y + which * (1 - 2 * y)
        copy = pltpu.make_async_copy(recvs[s].at[blocks(s, 30 + which, 1)], res[s].at[to], keep_sem.at[s, which])
        copy.start()
        kept_copies.append(copy)

    def advance(s):
        i = stage_of[s]
        pending[s, i].wait_recv()
        if i == 5:
            keep(s, 1)
            stage_of[s] = 6
            return
        half = 16 >> i
        src_ref, base = (bufs[s], 0) if i == 0 else (recvs[s], OFFSETS[i - 1])
        mine = base + step_of(s, i)[0] * half

        def add(j, carry):
            got = blocks(s, OFFSETS[i] + j, 1)
            recvs[s][got] = recvs[s][got] + src_ref[blocks(s, mine + j, 1)]
            return carry

        lax.fori_loop(0, half, add, 0)
        start(s, i + 1)
        if i == 4:
            keep(s, 0)

    def put(s, owner, core, h, value):
        bufs[s][blocks(s, block_index(owner, h, plan[s][2][core]), 1)] = value

    rows_of, ff_rows, col = plan[3][0], plan[0][0], plan[0][1]

    two = 2 * ff_rows

    def turn_outer(t, slot):
        turned[slot * two : (slot + 1) * two, :] = act[:, pl.ds(pl.multiple_of(t * two, 128), two)].T

    def outer_rows(t, slot):
        part = mat(turned[slot * two : (slot + 1) * two, :], db[...]).astype(BF16)
        for e in range(2):
            for s in range(3):
                for h in range(2):
                    at = (2 * s + h) * col
                    put(s, 2 * t + e, e, h, part[e * ff_rows : (e + 1) * ff_rows, at : at + col])

    def outer_four(i, carry):
        turn_outer(2 * i + 1, 1)
        outer_rows(2 * i, 0)
        turn_outer(lax.rem(2 * i + 2, SPAN // 2), 0)
        outer_rows(2 * i + 1, 1)
        return carry

    def by_owner(s, h, product):
        tall = 8 * rows_of

        def some(part, carry):
            block = product(turned[pl.ds(pl.multiple_of(part * tall, tall), tall), :]).astype(BF16)
            for o in range(8):
                put(s, part * 8 + o, o % 2, h, block[o * rows_of : (o + 1) * rows_of])
            return carry

        lax.fori_loop(0, 2, some, 0)


    def outer_slabs():
        turn_outer(0, 0)
        lax.fori_loop(0, SPAN // 4, outer_four, 0)
        for s in range(3):
            start(s, 0)
        load("qkv", qkv_hbm, act.at[:, pl.ds(0, 3 * width)], load_sem.at[8])
        dact_of(0, sa)

    def dact_of(j, into):
        into[...] = times_trans(db[...], wout[span_of(j), :])

    def bend(j, dact):
        sums = jnp.zeros((1, wide), F32)
        for r in range(total // ROW_CHUNK):
            rows = slice(r * ROW_CHUNK, (r + 1) * ROW_CHUNK)
            value = (dact[rows, :] * slope[rows, span_of(j)].astype(F32)).astype(BF16)
            dpre[rows, span_of(j)] = value
            sums += down(value.astype(F32))
        vec[8:9, span_of(j)] = sums

    def backward(i):
        if i == 0:
            for p in range(pairs // 2):
                for e in range(2):
                    prob_copy(dpre, p, pairs // 2, e).wait()
        dact_of(2 * i + 1, sb)
        bend(2 * i, sa)
        if 2 * i + 2 < steps:
            dact_of(2 * i + 2, sa)
        bend(2 * i + 1, sb)
        if i == steps // 2 - 1:
            for j, w in enumerate((wq, wk, wv)):
                load(j, w, wout.at[pl.ds(j * width, width)], load_sem.at[1 + j])
            turned[...] = n1[...].T

    def inner_slab(s):
        c = plan[s][1]
        for h in range(2):
            at = ((s - 3) * 2 + h) * c
            by_owner(s, h, lambda left: mat(left, dpre[:, at : at + c]))
        start(s, 0)

    def dn1_part(c):
        cols = slice(c * 256, (c + 1) * 256)
        acc[:, cols] += times_trans(dpre[...], wi[cols, :])

    def norm_one_back():
        for p in range(pairs // 2):
            for e in range(2):
                prob_back(wi, p, 0, e).start()
                prob_back(dpre, p, pairs // 2, e).start()

        def step(r, sums):
            rows = chunk(r)
            dn1, hat = acc[rows, :], hat1[rows, :]
            dh1 = norm_back(dn1, hat, r1[rows, 0:1], gain)
            acc[rows, :] = dh1
            low_dh1 = dh1.astype(BF16)
            dattn[rows, :] = low_dh1
            return (sums[0] + down(dn1 * hat), sums[1] + down(dn1), sums[2] + down(low_dh1.astype(F32)))

        a, b, c = lax.fori_loop(0, total // NORM_CHUNK, step, (zero, zero, zero))
        vec[3:4, 0:width] = a
        vec[4:5, 0:width] = b
        vec[2:3, 0:width] = c

    half_width = width // 2

    def out_slab():
        turned[...] = ctx[...].T
        for h in range(2):
            by_owner(6, h, lambda left: mat(left, dattn[:, h * half_width : (h + 1) * half_width]))
        start(6, 0)
        for c in range(width // 256):
            cols = slice(c * 256, (c + 1) * 256)
            dctx[:, cols] = times_trans(dattn[...], wo[cols, :]).astype(BF16)

    def head_back(kept, base, p, e):
        prob_back(kept, p, base, e).wait()
        pair = p + base
        qp, kp, vp, dop = act[:, lanes(0, pair)], act[:, lanes(1, pair)], act[:, lanes(2, pair)], dctx[:, lanes(0, pair)]
        dpe, dse = (sa, slope.at[:, 0:total]) if e == 0 else (sb, slope.at[:, total : 2 * total])
        mine_only = (lambda v: jnp.where(first, v, 0)) if e == 0 else (lambda v: jnp.where(first, 0, v))
        dpe[...] = times_trans(mine_only(dop).astype(BF16), vp)
        here = slice(e * HEAD_DIM, (e + 1) * HEAD_DIM)
        turned_q, turned_k, turned_do = qp.T[here], kp.T[here], dop.T[here]
        delta = jnp.sum(mine_only(dop.astype(F32) * ctx[:, lanes(0, pair)].astype(F32)), axis=1, keepdims=True)
        for r in range(total // ROW_CHUNK):
            rows = slice(r * ROW_CHUNK, (r + 1) * ROW_CHUNK)
            dse[rows, :] = (kept[rows, prob_lanes(p, e)].astype(F32) * (dpe[rows, :] - delta[rows])).astype(BF16)
        there = pl.ds(pl.multiple_of((2 * pair + e) * HEAD_DIM, HEAD_DIM), HEAD_DIM)
        dvt[there, :] = mat(turned_do, kept[0:total, prob_lanes(p, e)]).astype(BF16)
        dqt[there, :] = (times_trans(turned_k, dse[...]) * HEAD_DIM ** (-0.5)).astype(BF16)
        dkt[there, :] = mat(turned_q, dse[...]).astype(BF16)

    def pairs_back(low_pair, high_pair):
        if low_pair == 0:
            loads["qkv"].wait()
        kept, base = (wi, 0) if low_pair < pairs // 2 else (dpre, pairs // 2)

        def pair_back(p, carry):
            head_back(kept, base, p, 0)
            head_back(kept, base, p, 1)
            return carry

        for p in range(low_pair - base, high_pair - base):
            pair_back(p, 0)

    def head_slab(s, right):
        if s == 7:
            turned[...] = x[...].T
        pending[s - 4, 0].wait_send()
        sent.add((s - 4, 0))
        for h in range(2):
            by_owner(s, h, lambda left: times_trans(left, right[h * half_width : (h + 1) * half_width, :]))
        start(s, 0)

    def vectors():
        ones = jnp.ones((8, total), BF16)
        vec[0:1, 0:width] = times_trans(ones, dqt[...])[0:1]
        vec[1:2, 0:width] = times_trans(ones, dvt[...])[0:1]
        for o in range(SPAN):
            tmp[...] = jnp.zeros_like(tmp)
            tmp[0:8, 0:rows_of] = vec[0:8, o * rows_of : (o + 1) * rows_of]
            tmp[8:9, :] = vec[8:9, o * ff_rows : o * ff_rows + 128]
            put(10, o, o % 2, 0, tmp[...].astype(BF16))
            tmp[...] = jnp.zeros_like(tmp)
            tmp[8:9, 0 : ff_rows - 128] = vec[8:9, o * ff_rows + 128 : (o + 1) * ff_rows]
            put(10, o, o % 2, 1, tmp[...].astype(BF16))
        start(10, 0)

    def input_part(c):
        if c == 0:
            for i in range(3):
                loads[i].wait()
        cols = slice(c * 256, (c + 1) * 256)
        dxt = sum(
            mat(wout[i * width + c * 256 : i * width + (c + 1) * 256, :], d[...]) for i, d in enumerate((dqt, dkt, dvt))
        )
        dx = (dxt.T + acc[:, cols]).astype(BF16)
        db[:, cols] = dx
        if c == width // 256 - 1:
            sides.append(side(4, db.at[theirs], dx_hbm.at[y]))
            load("dx", db.at[mine], dx_hbm.at[y], load_sem.at[10])

    pieces = [outer_slabs]
    pieces += [functools.partial(backward, i) for i in range(steps // 2)]
    pieces += [functools.partial(inner_slab, s) for s in (3, 4, 5)]
    pieces += [functools.partial(dn1_part, c) for c in range(width // 256)]
    pieces += [norm_one_back, out_slab]
    pieces += [functools.partial(pairs_back, p, p + 1) for p in range(pairs)]
    pieces += [functools.partial(head_slab, s, r) for s, r in ((7, dqt), (8, dkt), (9, dvt))]
    pieces += [vectors] + [functools.partial(input_part, c) for c in range(width // 256)]
    for event in EVENTS:
        if event < 0:
            pieces.pop(0)()
        else:
            advance(event)
    for wait in (*x_swaps, cot_swap):
        wait.wait_send()
    for wait in (*sides, *kept_copies, loads["out"], loads["dx"]):
        wait.wait()
    for key, copy in pending.items():
        if key not in sent:
            copy.wait_send()


def run_layer(plan, low, args):
    count = len(plan)
    tokens = args[0]
    _, span, width = tokens.shape
    total = 2 * span
    ff = args[7].shape[1]
    hbm = pl.BlockSpec(memory_space=pl.ANY)
    vm = pl.BlockSpec(memory_space=pltpu.VMEM)
    smem = pl.BlockSpec(memory_space=pltpu.SMEM)
    low_shape, tall = pltpu.VMEM((total, width), BF16), pltpu.VMEM((total, ff), BF16)
    turned = pltpu.VMEM((width, total), BF16)
    own = [s for s in range(count) if s not in (7, 8, 9)]
    return pl.pallas_call(
        functools.partial(layer_kernel, plan, low),
        out_shape=[jax.ShapeDtypeStruct((2, r, c), BF16) for r, c, _ in plan]
        + [
            jax.ShapeDtypeStruct((2, span, width), BF16),
            jax.ShapeDtypeStruct((2, span, width), BF16),
            jax.ShapeDtypeStruct((width // HEAD_DIM, total, total), BF16),
            jax.ShapeDtypeStruct((total, 3 * width), BF16),
        ],
        in_specs=[hbm, smem] + [hbm] * 7 + [vm] * 9,
        out_specs=[hbm] * (count + 4),
        scratch_shapes=[pltpu.VMEM((32 * plan[s][0], plan[s][1]), BF16) for s in own]
        + [pltpu.VMEM((32 * r, c), BF16) for r, c, _ in plan]
        + [low_shape] * 5
        + [tall] * 3
        + [
            pltpu.VMEM((width, ff), BF16),
            pltpu.VMEM((ff, width), BF16),
            pltpu.VMEM((width, width), BF16),
            pltpu.VMEM((total, width), F32),
            pltpu.VMEM((total, width), F32),
            pltpu.VMEM((total, 128), F32),
            pltpu.VMEM((total, total), F32),
            pltpu.VMEM((total, total), F32),
            turned, turned, turned, turned,
            pltpu.VMEM((16, 128), F32),
            pltpu.VMEM((16, ff), F32),
            pltpu.SemaphoreType.DMA((11,)),
            pltpu.SemaphoreType.DMA((2, width // HEAD_DIM)),
            pltpu.SemaphoreType.DMA((count, 6)),
            pltpu.SemaphoreType.DMA((count, 6)),
            pltpu.SemaphoreType.DMA((2, 5)),
            pltpu.SemaphoreType.DMA((count, 2)),
        ],
        compiler_params=pltpu.CompilerParams(
            collective_id=0, has_side_effects=True, vmem_limit_bytes=VMEM_LIMIT
        ),
        name="layer",
    )(*args)


def finish_kernel(rows, ff_rows, *refs):
    inputs, refs = refs[:13], refs[13:]
    (out_ref, dx_ref, wq, bq, wk, wv, bv, wo, bo, gain, shift, wi, bi, wout, bout, fgain, fshift), refs = refs[:17], refs[17:]
    held, (dx_full, square, wide_full, tall_full, in_sem, out_sem) = refs[:13], refs[13:]
    gets = [pltpu.make_async_copy(src, dst, in_sem.at[i]) for i, (src, dst) in enumerate(zip(inputs, held))]
    order = (1, 0, 2, 3, 4, 5, 6, 7, 8, 9, 10, 11, 12)
    for i in order:
        gets[i].start()
    puts = []

    def put(src, dst):
        copy = pltpu.make_async_copy(src, dst, out_sem.at[len(puts)])
        copy.start()
        puts.append(copy)

    gets[1].wait()
    for n in range(2):
        dx_full[n] = held[1][n].astype(F32)
        put(dx_full.at[n], dx_ref.at[n])
    gets[0].wait()
    put(held[0], out_ref)
    res = held[2:]
    col = res[0].shape[2]
    for s in range(3):
        gets[2 + s].wait()
        for h in range(2):
            at = (2 * s + h) * col
            tall_full[:, at : at + col] = res[s][h].astype(F32)
    put(tall_full, wout)
    wide = res[3].shape[2]
    for s in range(3):
        gets[5 + s].wait()
        for h in range(2):
            at = (2 * s + h) * wide
            wide_full[:, at : at + wide] = res[3 + s][h].astype(F32)
    put(wide_full, wi)
    wide = res[6].shape[2]
    for n, ref in enumerate((wo, wq, wk, wv)):
        gets[8 + n].wait()
        for h in range(2):
            square[n, :, h * wide : (h + 1) * wide] = res[6 + n][h].astype(F32)
        put(square.at[n], ref)
    gets[12].wait()
    vec = res[10][0].astype(F32)
    rest = res[10][1].astype(F32)
    for i, ref in enumerate((bq, bv, bo, gain, shift, bout, fgain, fshift)):
        ref[...] = vec[i, 0:rows]
    bi[0:128] = vec[8, :]
    bi[128:ff_rows] = rest[8, 0 : ff_rows - 128]
    for copy in puts:
        copy.wait()


def finish(out, dx, res, width, ff):
    rows, ff_rows = width // SPAN, ff // SPAN
    square, line = (rows, width), (rows,)
    shapes = (
        square, line, square, square, line, square, line, line, line,
        (rows, ff), (ff_rows,), (ff_rows, width), line, line, line,
    )
    vm = pl.BlockSpec(memory_space=pltpu.VMEM)
    hbm = pl.BlockSpec(memory_space=pl.ANY)
    inputs = (out, dx, *res)
    return pl.pallas_call(
        functools.partial(finish_kernel, rows, ff_rows),
        out_shape=[jax.ShapeDtypeStruct(dx.shape, BF16), jax.ShapeDtypeStruct(dx.shape, F32)]
        + [jax.ShapeDtypeStruct(s, F32) for s in shapes],
        in_specs=[hbm] * len(inputs),
        out_specs=[hbm] * 2 + [hbm if len(s) == 2 else vm for s in shapes],
        scratch_shapes=[pltpu.VMEM(a.shape, a.dtype) for a in inputs]
        + [
            pltpu.VMEM(dx.shape, F32),
            pltpu.VMEM((4, rows, width), F32),
            pltpu.VMEM((rows, ff), F32),
            pltpu.VMEM((ff_rows, width), F32),
            pltpu.SemaphoreType.DMA((len(inputs),)),
            pltpu.SemaphoreType.DMA((9,)),
        ],
        name="finish",
    )(*inputs)


def per_device(
    dp_size,
    tokens,
    lengths,
    query_weight,
    query_bias,
    key_weight,
    value_weight,
    value_bias,
    out_weight,
    out_bias,
    norm_gain,
    norm_shift,
    inner_weight,
    inner_bias,
    outer_weight,
    outer_bias,
    final_gain,
    final_shift,
    cotangent,
):
    width, ff = inner_weight.shape
    plan = slab_plan(width, ff)
    low = dp_size // SPAN
    *res, dx, out, _, _ = run_layer(
        plan, low,
        (
            tokens, lengths, cotangent, query_weight, key_weight, value_weight, out_weight, inner_weight, outer_weight,
            query_bias, value_bias, out_bias, norm_gain, norm_shift, inner_bias, outer_bias, final_gain, final_shift,
        ),
    )
    layer_out, input_grad, *grads = finish(out, dx, res, width, ff)
    if low > 1:
        groups = [[t * low + i for i in range(low)] for t in range(SPAN)]
        grads = [
            lax.psum_scatter(g, "dp", scatter_dimension=0, axis_index_groups=groups, tiled=True)
            for g in grads
        ]
    return (layer_out, input_grad, *grads)


def solution(mesh):
    rows3 = P("dp", "blk", None)
    grad2, grad1 = P("dp", None), P("dp")
    return jax.shard_map(
        functools.partial(per_device, mesh.shape["dp"]),
        mesh=mesh,
        in_specs=(rows3, P("dp")) + (P(),) * 15 + (rows3,),
        out_specs=(
            rows3, rows3, grad2, grad1, grad2, grad2, grad1, grad2, grad1,
            grad1, grad1, grad2, grad1, grad2, grad1, grad1, grad1,
        ),
        check_vma=False,
    )
```

```python
import functools

import jax
import jax.numpy as jnp
from jax import lax
from jax.experimental import pallas as pl
from jax.experimental.pallas import tpu as pltpu
from jax.sharding import PartitionSpec as P

HEADS = 12
HEAD_DIM = 64
HEAD_PAIR = 2 * HEAD_DIM
ROW_CHUNK = 64
NORM_CHUNK = 512
EPS = 1e-12
HALF_ROOT = 0.7071067811865476
INV_ROOT_TAU = 0.3989422804014327
MESH = pl.DeviceIdType.MESH
BF16 = jnp.bfloat16
F32 = jnp.float32

ORDERS = {
    "A": ("c", "x", "y", "zl", "zh"),
    "B": ("c", "y", "zl", "x", "zh"),
    "C": ("c", "zl", "x", "y", "zh"),
    "E": ("c", "x", "zl", "y", "zh"),
    "F": ("c", "zl", "y", "x", "zh"),
    "G": ("c", "y", "x", "zl", "zh"),
    "H": ("c", "x", "zl", "zh", "y"),
    "L": ("c", "zl", "x", "zh", "y"),
}
SLAB_ORDERS = ("CA", "GH", "LG", "BF", "AE", "CG", "AC", "EL", "BC", "AE", "EA")
EVENTS = (
    -1, -1, -1, 0, -1, 1, 2, -1, -1, -1, 0, 3, -1, 4, 5, -1, -1, -1, -1, 1,
    2, -1, -1, 6, -1, 0, -1, 4, -1, -1, 3, 1, -1, 0, -1, 2, -1, 5, 7, 8,
    6, 4, -1, 9, 3, -1, 1, 10, -1, 0, 5, -1, 2, 4, 6, 1, 0, 7, 8, 5,
    9, 6, 4, 3, 7, 10, 2, 1, 5, 8, 10, 9, 6, 4, 3, 8, 7, 9, 2, 8,
    5, 10, 6, 3, 7, 8, 9, 10, 7, 9, 10,
)
BIT_OF = {"c": 1, "x": 2, "zl": 4, "zh": 8}
SPAN = 16
OFFSETS = (0, 16, 24, 28, 30, 31)
VMEM_LIMIT = 67_043_328


def contract_rows(left_mat, right_mat):
    return lax.dot_general(
        left_mat, right_mat, (((0,), (0,)), ((), ())), preferred_element_type=F32
    )


def times_trans(left_mat, right_mat):
    return lax.dot_general(
        left_mat, right_mat, (((1,), (1,)), ((), ())), preferred_element_type=F32
    )


def mat(left_mat, right_mat):
    return jnp.dot(left_mat, right_mat, preferred_element_type=F32)


def norm_rows(hidden, gain_vec, shift_vec):
    row_mean = jnp.mean(hidden, axis=-1, keepdims=True)
    centred = hidden - row_mean
    reciprocal = lax.rsqrt(jnp.mean(centred * centred, axis=-1, keepdims=True) + EPS)
    normed = centred * reciprocal
    return (normed * gain_vec + shift_vec, normed, reciprocal)


def norm_back(grad_in, normed, reciprocal, gain_vec):
    scaled = grad_in * gain_vec
    return reciprocal * (
        scaled
        - jnp.mean(scaled, axis=-1, keepdims=True)
        - normed * jnp.mean(scaled * normed, axis=-1, keepdims=True)
    )


def row_vec(ref):
    return ref[...].astype(F32).reshape(1, -1)


def block_index(owner, half, order):
    place = 0
    for dim in order:
        bit = half if dim == "y" else (owner // BIT_OF[dim]) % 2
        place = place * 2 + bit
    return place


def slab_plan(width, ff):
    rows, ff_rows = width // SPAN, ff // SPAN
    sizes = [(ff_rows, width // 6)] * 3 + [(rows, ff // 6)] * 3 + [(rows, width // 2)] * 4 + [(16, 128)]
    return tuple((r, c, (ORDERS[o[0]], ORDERS[o[1]])) for (r, c), o in zip(sizes, SLAB_ORDERS))


def layer_kernel(plan, low, *refs):
    count = len(plan)
    (tokens, lengths, cot_in, wq, wk, wv, wo_in, wi_in, wout_in, bq, bv, bo, gain_in, shift_in, bi, bout_in, fgain_in, fshift_in) = refs[:18]
    res, refs = refs[18 : 18 + count], refs[18 + count :]
    dx_hbm, out_hbm, prob_hbm, qkv_hbm = refs[:4]
    refs = refs[4:]
    bufs, recvs, refs = refs[: count - 3], refs[count - 3 : 2 * count - 3], refs[2 * count - 3 :]
    (x, cot, ctx, db, n1, act, dpre, slope, wi, wout, wo, hat1, acc, r1, sa, sb) = refs[:16]
    (turned, dqt, dkt, dvt, tmp, vec, load_sem, prob_sem, send_sem, recv_sem, side_sem, keep_sem) = refs[16:]
    dattn, dctx = n1, db
    total, width = x.shape
    span = total // 2
    ff = act.shape[1]
    pairs = width // HEAD_PAIR
    wide = sa.shape[1]
    bufs = list(bufs[:7]) + [bufs[s].at[:, 0 : width // 2] for s in (3, 4, 5)] + [bufs[7]]

    dp = lax.axis_index("dp")
    y = lax.axis_index("blk")
    top = dp // low
    bits = {dim: (top // b) % 2 for dim, b in BIT_OF.items()}
    bits["y"] = y
    partner = {dim: (dp + (1 - 2 * bits[dim]) * (b * low), y) for dim, b in BIT_OF.items()}
    partner["y"] = (dp, 1 - y)

    loads = {}

    def load(name, src, dst, sem):
        loads[name] = pltpu.make_async_copy(src, dst, sem)
        loads[name].start()

    mine, theirs = pl.ds(0, span), pl.ds(span, span)
    load("x", tokens.at[y], x.at[mine], load_sem.at[0])
    for i, w in enumerate((wq, wk, wv)):
        load(i, w, wout.at[pl.ds(i * width, width)], load_sem.at[1 + i])
    load("wo", wo_in, wo, load_sem.at[4])
    load("cot", cot_in.at[y], cot.at[mine], load_sem.at[5])
    load("wi", wi_in, wi, load_sem.at[6])

    barrier = pltpu.get_barrier_semaphore()
    for where in partner.values():
        pl.semaphore_signal(barrier, inc=1, device_id=where, device_id_type=MESH)
    pl.semaphore_wait(barrier, len(partner))

    def remote(src, dst, send, recv, where):
        copy = pltpu.make_async_remote_copy(
            src_ref=src, dst_ref=dst, send_sem=send, recv_sem=recv, device_id=where, device_id_type=MESH
        )
        copy.start()
        return copy

    def side(i, src, dst):
        return remote(src, dst, side_sem.at[0, i], side_sem.at[1, i], partner["y"])

    part = span // 2
    x_swaps = [
        side(i, tokens.at[1 - y, pl.ds(i * part, part)], x.at[pl.ds(span + i * part, part)]) for i in range(2)
    ]
    cot_swap = side(2, cot_in.at[1 - y], cot.at[theirs])

    def down(v):
        return jnp.sum(v, axis=0, keepdims=True)

    loads["x"].wait()
    for half in range(3):
        rows = slice(0, span) if half == 0 else slice(span + (half - 1) * part, span + half * part)
        if half > 0:
            x_swaps[half - 1].wait_recv()
        for i, b_ref in enumerate((bq, None, bv)):
            if half == 0:
                loads[i].wait()
            bias = None if b_ref is None else row_vec(b_ref)
            for c in range(width // 256):
                cols = slice(c * 256, (c + 1) * 256)
                got = mat(x[rows, :], wout[i * width : (i + 1) * width, cols])
                if bias is not None:
                    got = got + bias[:, cols]
                got = got.astype(BF16)
                if i == 0:
                    got = got * jnp.bfloat16(HEAD_DIM ** (-0.5))
                act[rows, i * width + c * 256 : i * width + (c + 1) * 256] = got
    load("wout", wout_in, wout, load_sem.at[7])
    load("qkv", act.at[:, pl.ds(0, 3 * width)], qkv_hbm, load_sem.at[8])

    length = lengths[y]
    at = lax.broadcasted_iota(jnp.int32, (1, total), 1)
    place = jnp.where(at < span, at + y * span, at - span + (1 - y) * span)
    mask = jnp.where(place < length, 0.0, -1e30).astype(F32)
    first = lax.broadcasted_iota(jnp.int32, (1, HEAD_PAIR), 1) < HEAD_DIM

    def lanes(i, p):
        return pl.ds(pl.multiple_of(i * width + p * HEAD_PAIR, HEAD_PAIR), HEAD_PAIR)

    def prob_lanes(p, e):
        return pl.ds(pl.multiple_of((2 * p + e) * total, 128), total)

    def prob_copy(kept, p, base, e):
        return pltpu.make_async_copy(
            kept.at[0:total, prob_lanes(p, e)], prob_hbm.at[2 * (p + base) + e], prob_sem.at[0, 2 * (p + base) + e]
        )

    def prob_back(kept, p, base, e):
        return pltpu.make_async_copy(
            prob_hbm.at[2 * (p + base) + e], kept.at[0:total, prob_lanes(p, e)], prob_sem.at[1, 2 * (p + base) + e]
        )

    def scores(p, e, into):
        qp, kp = act[:, lanes(0, p)], act[:, lanes(1, p)]
        keep = jnp.where(first, qp, 0) if e == 0 else jnp.where(first, 0, qp)
        into[...] = times_trans(keep.astype(BF16), kp)

    def soften(kept, p, base, e, s):
        for r in range(total // ROW_CHUNK):
            rows = slice(r * ROW_CHUNK, (r + 1) * ROW_CHUNK)
            raw = s[rows, :] + mask
            expo = jnp.exp(raw - jnp.max(raw, axis=1, keepdims=True))
            scale = 1.0 / jnp.sum(expo, axis=1, keepdims=True)
            kept[rows, prob_lanes(p, e)] = (expo * scale).astype(BF16)
        prob_copy(kept, p, base, e).start()

    scores(0, 0, sa)
    for p in range(pairs):
        kept, base = (slope, 0) if p < pairs // 2 else (dpre, pairs // 2)
        vp = act[:, lanes(2, p)]
        scores(p, 1, sb)
        soften(kept, p - base, base, 0, sa)
        if p + 1 < pairs:
            scores(p + 1, 0, sa)
        even = mat(kept[0:total, prob_lanes(p - base, 0)], vp)
        soften(kept, p - base, base, 1, sb)
        odd = mat(kept[0:total, prob_lanes(p - base, 1)], vp)
        ctx[:, lanes(0, p)] = jnp.where(first, even, odd).astype(BF16)

    loads["wo"].wait()
    acc[...] = mat(ctx[...], wo[...])
    bo, gain, shift, bout = row_vec(bo), row_vec(gain_in), row_vec(shift_in), row_vec(bout_in)
    fgain, fshift = row_vec(fgain_in), row_vec(fshift_in)
    vec[9:10, :] = row_vec(bi)

    def chunk(r):
        return pl.ds(pl.multiple_of(r * NORM_CHUNK, NORM_CHUNK), NORM_CHUNK)

    def norm_one(r, carry):
        rows = chunk(r)
        normed, hat, recip = norm_rows(x[rows, :].astype(F32) + acc[rows, :] + bo, gain, shift)
        hat1[rows, :] = hat
        r1[rows, :] = jnp.broadcast_to(recip, (NORM_CHUNK, 128))
        n1[rows, :] = normed.astype(BF16)
        acc[rows, :] = normed + bout
        return carry

    lax.fori_loop(0, total // NORM_CHUNK, norm_one, 0)

    for p in range(pairs // 2):
        for e in range(2):
            prob_copy(slope, p, 0, e).wait()
    loads["qkv"].wait()
    loads["wi"].wait()
    loads["wout"].wait()

    def span_of(j):
        return pl.ds(pl.multiple_of(j * wide, wide), wide)

    def pre_of(j, into):
        into[...] = mat(n1[...], wi[:, span_of(j)])

    def activate(j, pre):
        bias = vec[9:10, span_of(j)]
        for r in range(total // ROW_CHUNK):
            rows = slice(r * ROW_CHUNK, (r + 1) * ROW_CHUNK)
            u = pre[rows, :] + bias
            half = 0.5 * (1.0 + lax.erf(u * HALF_ROOT))
            act[rows, span_of(j)] = (u * half).astype(BF16)
            slope[rows, span_of(j)] = (half + u * jnp.exp(-0.5 * u * u) * INV_ROOT_TAU).astype(BF16)

    def second(j):
        acc[...] += mat(act[:, span_of(j)], wout[span_of(j), :])

    steps = ff // wide
    pre_of(0, sa)

    for i in range(steps // 2):
        pre_of(2 * i + 1, sb)
        activate(2 * i, sa)
        if i > 0:
            second(2 * i - 1)
        if i + 1 < steps // 2:
            pre_of(2 * i + 2, sa)
        activate(2 * i + 1, sb)
        second(2 * i)
    second(steps - 1)

    loads["cot"].wait()
    cot_swap.wait_recv()
    zero = jnp.zeros((1, width), F32)

    def norm_two(r, sums):
        rows = chunk(r)
        out, hat2, recip2 = norm_rows(acc[rows, :], fgain, fshift)
        g = cot[rows, :].astype(F32)
        cot[rows, :] = out.astype(BF16)
        dh2 = norm_back(g, hat2, recip2, fgain)
        acc[rows, :] = dh2
        low_dh2 = dh2.astype(BF16)
        db[rows, :] = low_dh2
        return (sums[0] + down(g * hat2), sums[1] + down(g), sums[2] + down(low_dh2.astype(F32)))

    fgain_sum, fshift_sum, bout_sum = lax.fori_loop(0, total // NORM_CHUNK, norm_two, (zero, zero, zero))
    vec[5:6, 0:width] = bout_sum
    vec[6:7, 0:width] = fgain_sum
    vec[7:8, 0:width] = fshift_sum
    load("out", cot.at[mine], out_hbm.at[y], load_sem.at[9])

    pending = {}
    stage_of = {}
    sent = set()

    def blocks(s, base, n):
        size = plan[s][0]
        return pl.ds(pl.multiple_of(base * size, 16), n * size)

    def step_of(s, i):
        even, odd = (plan[s][2][c][i] for c in range(2))
        if even == odd:
            return bits[even], partner[even]
        own = bits["c"]
        return (
            bits[even] + own * (bits[odd] - bits[even]),
            tuple(a + own * (b - a) for a, b in zip(partner[even], partner[odd])),
        )

    def start(s, i):
        if i == 5:
            src, dst, where = recvs[s].at[blocks(s, 30, 1)], recvs[s].at[blocks(s, 31, 1)], partner["y"]
        else:
            half = 16 >> i
            bit, where = step_of(s, i)
            src_ref, base = (bufs[s], 0) if i == 0 else (recvs[s], OFFSETS[i - 1])
            src = src_ref.at[blocks(s, base + (1 - bit) * half, half)]
            dst = recvs[s].at[blocks(s, OFFSETS[i], half)]
        pending[s, i] = remote(src, dst, send_sem.at[s, i], recv_sem.at[s, i], where)
        stage_of[s] = i

    kept_copies = []

    def keep(s, which):
        to = y + which * (1 - 2 * y)
        copy = pltpu.make_async_copy(recvs[s].at[blocks(s, 30 + which, 1)], res[s].at[to], keep_sem.at[s, which])
        copy.start()
        kept_copies.append(copy)

    def advance(s):
        i = stage_of[s]
        pending[s, i].wait_recv()
        if i == 5:
            keep(s, 1)
            stage_of[s] = 6
            return
        half = 16 >> i
        src_ref, base = (bufs[s], 0) if i == 0 else (recvs[s], OFFSETS[i - 1])
        mine = base + step_of(s, i)[0] * half

        def add(j, carry):
            got = blocks(s, OFFSETS[i] + j, 1)
            recvs[s][got] = recvs[s][got] + src_ref[blocks(s, mine + j, 1)]
            return carry

        lax.fori_loop(0, half, add, 0)
        start(s, i + 1)
        if i == 4:
            keep(s, 0)

    def put(s, owner, core, h, value):
        bufs[s][blocks(s, block_index(owner, h, plan[s][2][core]), 1)] = value

    rows_of, ff_rows, col = plan[3][0], plan[0][0], plan[0][1]

    two = 2 * ff_rows

    def turn_outer(t, slot):
        turned[slot * two : (slot + 1) * two, :] = act[:, pl.ds(pl.multiple_of(t * two, 128), two)].T

    def outer_rows(t, slot):
        part = mat(turned[slot * two : (slot + 1) * two, :], db[...]).astype(BF16)
        for e in range(2):
            for s in range(3):
                for h in range(2):
                    at = (2 * s + h) * col
                    put(s, 2 * t + e, e, h, part[e * ff_rows : (e + 1) * ff_rows, at : at + col])

    def outer_four(i, carry):
        turn_outer(2 * i + 1, 1)
        outer_rows(2 * i, 0)
        turn_outer(lax.rem(2 * i + 2, SPAN // 2), 0)
        outer_rows(2 * i + 1, 1)
        return carry

    def by_owner(s, h, product):
        tall = 8 * rows_of

        def some(part, carry):
            block = product(turned[pl.ds(pl.multiple_of(part * tall, tall), tall), :]).astype(BF16)
            for o in range(8):
                put(s, part * 8 + o, o % 2, h, block[o * rows_of : (o + 1) * rows_of])
            return carry

        lax.fori_loop(0, 2, some, 0)

    sides = []

    def outer_slabs():
        turn_outer(0, 0)
        lax.fori_loop(0, SPAN // 4, outer_four, 0)
        for s in range(3):
            start(s, 0)
        sides.append(side(3, cot.at[theirs], out_hbm.at[y]))
        load("qkv", qkv_hbm, act.at[:, pl.ds(0, 3 * width)], load_sem.at[8])
        dact_of(0, sa)

    def dact_of(j, into):
        into[...] = times_trans(db[...], wout[span_of(j), :])

    def bend(j, dact):
        sums = jnp.zeros((1, wide), F32)
        for r in range(total // ROW_CHUNK):
            rows = slice(r * ROW_CHUNK, (r + 1) * ROW_CHUNK)
            value = (dact[rows, :] * slope[rows, span_of(j)].astype(F32)).astype(BF16)
            dpre[rows, span_of(j)] = value
            sums += down(value.astype(F32))
        vec[8:9, span_of(j)] = sums

    def backward(i):
        if i == 0:
            for p in range(pairs // 2):
                for e in range(2):
                    prob_copy(dpre, p, pairs // 2, e).wait()
        dact_of(2 * i + 1, sb)
        bend(2 * i, sa)
        if 2 * i + 2 < steps:
            dact_of(2 * i + 2, sa)
        bend(2 * i + 1, sb)
        if i == steps // 2 - 1:
            for j, w in enumerate((wq, wk, wv)):
                load(j, w, wout.at[pl.ds(j * width, width)], load_sem.at[1 + j])
            turned[...] = n1[...].T

    def inner_slab(s):
        c = plan[s][1]
        for h in range(2):
            at = ((s - 3) * 2 + h) * c
            by_owner(s, h, lambda left: mat(left, dpre[:, at : at + c]))
        start(s, 0)

    def dn1_part(c):
        cols = slice(c * 256, (c + 1) * 256)
        acc[:, cols] += times_trans(dpre[...], wi[cols, :])

    def norm_one_back():
        for p in range(pairs // 2):
            for e in range(2):
                prob_back(wi, p, 0, e).start()
                prob_back(dpre, p, pairs // 2, e).start()

        def step(r, sums):
            rows = chunk(r)
            dn1, hat = acc[rows, :], hat1[rows, :]
            dh1 = norm_back(dn1, hat, r1[rows, 0:1], gain)
            acc[rows, :] = dh1
            low_dh1 = dh1.astype(BF16)
            dattn[rows, :] = low_dh1
            return (sums[0] + down(dn1 * hat), sums[1] + down(dn1), sums[2] + down(low_dh1.astype(F32)))

        a, b, c = lax.fori_loop(0, total // NORM_CHUNK, step, (zero, zero, zero))
        vec[3:4, 0:width] = a
        vec[4:5, 0:width] = b
        vec[2:3, 0:width] = c

    half_width = width // 2

    def out_slab():
        turned[...] = ctx[...].T
        for h in range(2):
            by_owner(6, h, lambda left: mat(left, dattn[:, h * half_width : (h + 1) * half_width]))
        start(6, 0)
        for c in range(width // 256):
            cols = slice(c * 256, (c + 1) * 256)
            dctx[:, cols] = times_trans(dattn[...], wo[cols, :]).astype(BF16)

    def head_back(kept, base, p, e):
        prob_back(kept, p, base, e).wait()
        pair = p + base
        qp, kp, vp, dop = act[:, lanes(0, pair)], act[:, lanes(1, pair)], act[:, lanes(2, pair)], dctx[:, lanes(0, pair)]
        dpe, dse = (sa, slope.at[:, 0:total]) if e == 0 else (sb, slope.at[:, total : 2 * total])
        mine_only = (lambda v: jnp.where(first, v, 0)) if e == 0 else (lambda v: jnp.where(first, 0, v))
        dpe[...] = times_trans(mine_only(dop).astype(BF16), vp)
        here = slice(e * HEAD_DIM, (e + 1) * HEAD_DIM)
        turned_q, turned_k, turned_do = qp.T[here], kp.T[here], dop.T[here]
        delta = jnp.sum(mine_only(dop.astype(F32) * ctx[:, lanes(0, pair)].astype(F32)), axis=1, keepdims=True)
        for r in range(total // ROW_CHUNK):
            rows = slice(r * ROW_CHUNK, (r + 1) * ROW_CHUNK)
            dse[rows, :] = (kept[rows, prob_lanes(p, e)].astype(F32) * (dpe[rows, :] - delta[rows])).astype(BF16)
        there = pl.ds(pl.multiple_of((2 * pair + e) * HEAD_DIM, HEAD_DIM), HEAD_DIM)
        dvt[there, :] = mat(turned_do, kept[0:total, prob_lanes(p, e)]).astype(BF16)
        dqt[there, :] = (times_trans(turned_k, dse[...]) * HEAD_DIM ** (-0.5)).astype(BF16)
        dkt[there, :] = mat(turned_q, dse[...]).astype(BF16)

    def pairs_back(low_pair, high_pair):
        if low_pair == 0:
            loads["qkv"].wait()
        kept, base = (wi, 0) if low_pair < pairs // 2 else (dpre, pairs // 2)

        def pair_back(p, carry):
            head_back(kept, base, p, 0)
            head_back(kept, base, p, 1)
            return carry

        for p in range(low_pair - base, high_pair - base):
            pair_back(p, 0)

    def head_slab(s, right):
        if s == 7:
            turned[...] = x[...].T
        pending[s - 4, 0].wait_send()
        sent.add((s - 4, 0))
        for h in range(2):
            by_owner(s, h, lambda left: times_trans(left, right[h * half_width : (h + 1) * half_width, :]))
        start(s, 0)

    def vectors():
        ones = jnp.ones((8, total), BF16)
        vec[0:1, 0:width] = times_trans(ones, dqt[...])[0:1]
        vec[1:2, 0:width] = times_trans(ones, dvt[...])[0:1]
        for o in range(SPAN):
            tmp[...] = jnp.zeros_like(tmp)
            tmp[0:8, 0:rows_of] = vec[0:8, o * rows_of : (o + 1) * rows_of]
            tmp[8:9, :] = vec[8:9, o * ff_rows : o * ff_rows + 128]
            put(10, o, o % 2, 0, tmp[...].astype(BF16))
            tmp[...] = jnp.zeros_like(tmp)
            tmp[8:9, 0 : ff_rows - 128] = vec[8:9, o * ff_rows + 128 : (o + 1) * ff_rows]
            put(10, o, o % 2, 1, tmp[...].astype(BF16))
        start(10, 0)

    def input_part(c):
        if c == 0:
            for i in range(3):
                loads[i].wait()
        cols = slice(c * 256, (c + 1) * 256)
        dxt = sum(
            mat(wout[i * width + c * 256 : i * width + (c + 1) * 256, :], d[...]) for i, d in enumerate((dqt, dkt, dvt))
        )
        dx = (dxt.T + acc[:, cols]).astype(BF16)
        db[:, cols] = dx
        if c == width // 256 - 1:
            sides.append(side(4, db.at[theirs], dx_hbm.at[y]))
            load("dx", db.at[mine], dx_hbm.at[y], load_sem.at[10])

    pieces = [outer_slabs]
    pieces += [functools.partial(backward, i) for i in range(steps // 2)]
    pieces += [functools.partial(inner_slab, s) for s in (3, 4, 5)]
    pieces += [functools.partial(dn1_part, c) for c in range(width // 256)]
    pieces += [norm_one_back, out_slab]
    pieces += [functools.partial(pairs_back, p, p + 1) for p in range(pairs)]
    pieces += [functools.partial(head_slab, s, r) for s, r in ((7, dqt), (8, dkt), (9, dvt))]
    pieces += [vectors] + [functools.partial(input_part, c) for c in range(width // 256)]
    for event in EVENTS:
        if event < 0:
            pieces.pop(0)()
        else:
            advance(event)
    for wait in (*x_swaps, cot_swap):
        wait.wait_send()
    for wait in (*sides, *kept_copies, loads["out"], loads["dx"]):
        wait.wait()
    for key, copy in pending.items():
        if key not in sent:
            copy.wait_send()


def run_layer(plan, low, args):
    count = len(plan)
    tokens = args[0]
    _, span, width = tokens.shape
    total = 2 * span
    ff = args[7].shape[1]
    hbm = pl.BlockSpec(memory_space=pl.ANY)
    vm = pl.BlockSpec(memory_space=pltpu.VMEM)
    smem = pl.BlockSpec(memory_space=pltpu.SMEM)
    low_shape, tall = pltpu.VMEM((total, width), BF16), pltpu.VMEM((total, ff), BF16)
    turned = pltpu.VMEM((width, total), BF16)
    own = [s for s in range(count) if s not in (7, 8, 9)]
    return pl.pallas_call(
        functools.partial(layer_kernel, plan, low),
        out_shape=[jax.ShapeDtypeStruct((2, r, c), BF16) for r, c, _ in plan]
        + [
            jax.ShapeDtypeStruct((2, span, width), BF16),
            jax.ShapeDtypeStruct((2, span, width), BF16),
            jax.ShapeDtypeStruct((width // HEAD_DIM, total, total), BF16),
            jax.ShapeDtypeStruct((total, 3 * width), BF16),
        ],
        in_specs=[hbm, smem] + [hbm] * 7 + [vm] * 9,
        out_specs=[hbm] * (count + 4),
        scratch_shapes=[pltpu.VMEM((32 * plan[s][0], plan[s][1]), BF16) for s in own]
        + [pltpu.VMEM((32 * r, c), BF16) for r, c, _ in plan]
        + [low_shape] * 5
        + [tall] * 3
        + [
            pltpu.VMEM((width, ff), BF16),
            pltpu.VMEM((ff, width), BF16),
            pltpu.VMEM((width, width), BF16),
            pltpu.VMEM((total, width), F32),
            pltpu.VMEM((total, width), F32),
            pltpu.VMEM((total, 128), F32),
            pltpu.VMEM((total, total), F32),
            pltpu.VMEM((total, total), F32),
            turned, turned, turned, turned,
            pltpu.VMEM((16, 128), F32),
            pltpu.VMEM((16, ff), F32),
            pltpu.SemaphoreType.DMA((11,)),
            pltpu.SemaphoreType.DMA((2, width // HEAD_DIM)),
            pltpu.SemaphoreType.DMA((count, 6)),
            pltpu.SemaphoreType.DMA((count, 6)),
            pltpu.SemaphoreType.DMA((2, 5)),
            pltpu.SemaphoreType.DMA((count, 2)),
        ],
        compiler_params=pltpu.CompilerParams(
            collective_id=0, has_side_effects=True, vmem_limit_bytes=VMEM_LIMIT
        ),
        name="layer",
    )(*args)


def finish_kernel(rows, ff_rows, *refs):
    inputs, refs = refs[:13], refs[13:]
    (out_ref, dx_ref, wq, bq, wk, wv, bv, wo, bo, gain, shift, wi, bi, wout, bout, fgain, fshift), refs = refs[:17], refs[17:]
    held, (dx_full, square, wide_full, tall_full, in_sem, out_sem) = refs[:13], refs[13:]
    gets = [pltpu.make_async_copy(src, dst, in_sem.at[i]) for i, (src, dst) in enumerate(zip(inputs, held))]
    order = (1, 0, 2, 3, 4, 5, 6, 7, 8, 9, 10, 11, 12)
    for i in order:
        gets[i].start()
    puts = []

    def put(src, dst):
        copy = pltpu.make_async_copy(src, dst, out_sem.at[len(puts)])
        copy.start()
        puts.append(copy)

    gets[1].wait()
    for n in range(2):
        dx_full[n] = held[1][n].astype(F32)
        put(dx_full.at[n], dx_ref.at[n])
    gets[0].wait()
    put(held[0], out_ref)
    res = held[2:]
    col = res[0].shape[2]
    for s in range(3):
        gets[2 + s].wait()
        for h in range(2):
            at = (2 * s + h) * col
            tall_full[:, at : at + col] = res[s][h].astype(F32)
    put(tall_full, wout)
    wide = res[3].shape[2]
    for s in range(3):
        gets[5 + s].wait()
        for h in range(2):
            at = (2 * s + h) * wide
            wide_full[:, at : at + wide] = res[3 + s][h].astype(F32)
    put(wide_full, wi)
    wide = res[6].shape[2]
    for n, ref in enumerate((wo, wq, wk, wv)):
        gets[8 + n].wait()
        for h in range(2):
            square[n, :, h * wide : (h + 1) * wide] = res[6 + n][h].astype(F32)
        put(square.at[n], ref)
    gets[12].wait()
    vec = res[10][0].astype(F32)
    rest = res[10][1].astype(F32)
    for i, ref in enumerate((bq, bv, bo, gain, shift, bout, fgain, fshift)):
        ref[...] = vec[i, 0:rows]
    bi[0:128] = vec[8, :]
    bi[128:ff_rows] = rest[8, 0 : ff_rows - 128]
    for copy in puts:
        copy.wait()


def finish(out, dx, res, width, ff):
    rows, ff_rows = width // SPAN, ff // SPAN
    square, line = (rows, width), (rows,)
    shapes = (
        square, line, square, square, line, square, line, line, line,
        (rows, ff), (ff_rows,), (ff_rows, width), line, line, line,
    )
    vm = pl.BlockSpec(memory_space=pltpu.VMEM)
    hbm = pl.BlockSpec(memory_space=pl.ANY)
    inputs = (out, dx, *res)
    return pl.pallas_call(
        functools.partial(finish_kernel, rows, ff_rows),
        out_shape=[jax.ShapeDtypeStruct(dx.shape, BF16), jax.ShapeDtypeStruct(dx.shape, F32)]
        + [jax.ShapeDtypeStruct(s, F32) for s in shapes],
        in_specs=[hbm] * len(inputs),
        out_specs=[hbm] * 2 + [hbm if len(s) == 2 else vm for s in shapes],
        scratch_shapes=[pltpu.VMEM(a.shape, a.dtype) for a in inputs]
        + [
            pltpu.VMEM(dx.shape, F32),
            pltpu.VMEM((4, rows, width), F32),
            pltpu.VMEM((rows, ff), F32),
            pltpu.VMEM((ff_rows, width), F32),
            pltpu.SemaphoreType.DMA((len(inputs),)),
            pltpu.SemaphoreType.DMA((9,)),
        ],
        name="finish",
    )(*inputs)


def per_device(
    dp_size,
    tokens,
    lengths,
    query_weight,
    query_bias,
    key_weight,
    value_weight,
    value_bias,
    out_weight,
    out_bias,
    norm_gain,
    norm_shift,
    inner_weight,
    inner_bias,
    outer_weight,
    outer_bias,
    final_gain,
    final_shift,
    cotangent,
):
    width, ff = inner_weight.shape
    plan = slab_plan(width, ff)
    low = dp_size // SPAN
    *res, dx, out, _, _ = run_layer(
        plan, low,
        (
            tokens, lengths, cotangent, query_weight, key_weight, value_weight, out_weight, inner_weight, outer_weight,
            query_bias, value_bias, out_bias, norm_gain, norm_shift, inner_bias, outer_bias, final_gain, final_shift,
        ),
    )
    layer_out, input_grad, *grads = finish(out, dx, res, width, ff)
    if low > 1:
        groups = [[t * low + i for i in range(low)] for t in range(SPAN)]
        grads = [
            lax.psum_scatter(g, "dp", scatter_dimension=0, axis_index_groups=groups, tiled=True)
            for g in grads
        ]
    return (layer_out, input_grad, *grads)


def solution(mesh):
    rows3 = P("dp", "blk", None)
    grad2, grad1 = P("dp", None), P("dp")
    return jax.shard_map(
        functools.partial(per_device, mesh.shape["dp"]),
        mesh=mesh,
        in_specs=(rows3, P("dp")) + (P(),) * 15 + (rows3,),
        out_specs=(
            rows3, rows3, grad2, grad1, grad2, grad2, grad1, grad2, grad1,
            grad1, grad1, grad2, grad1, grad2, grad1, grad1, grad1,
        ),
        check_vma=False,
    )
```
